32 devices in a mesh: groups: 2 (over x), seq: 16 (over z, y, core).
Axes of the slice: x: 2, y: 2, z: 4, core: 2. Of those that a mesh axis runs over, the one named last changes fastest.
Arguments:
- query_in: bfloat16 [16384, 2048], P(('groups', 'seq')), parts along dimension 0, may hold values from -6 to 6
- key_in: bfloat16 [16384, 2048], P(('groups', 'seq')), parts along dimension 0, may hold values from -6 to 6
- value_in: bfloat16 [16384, 2048], P(('groups', 'seq')), parts along dimension 0, may hold values from -6 to 6
- conv_weight: float32 [4, 6144], replicated, may hold values from -3 to 3
- level_weight: bfloat16 [16, 14, 16384], P(None, None, ('groups', 'seq')), parts along dimension 2, may hold values from 0.099609375 to 1
- out_gain: float32 [2048], replicated, may hold values from 0.1 to 1.9
- doc_starts: int32 [16], P('groups'), parts along dimension 0, may hold values from 0 to 8191, as said below
Outputs:
- mixed: bfloat16 [16384, 2048], P(('groups', 'seq')), parts along dimension 0
The draws below stay inside these ranges and needn't reach their ends.
There are 2 independent parts, one for each index of `groups`. The reference program is written for one: setup_inputs(seed, part) draws one part's arguments, and reference() takes and returns one part's arrays. A program takes and returns all parts, laid end to end along the dimension named above; an argument that names none is the same for every part. Nothing has to cross between parts.
Inputs may be any that keep to these rules, and one draw needn't show every extreme that they name: doc_starts is strictly increasing, its first entry is 0, its last entry is 8191, and no document starts above a quarter of 8192 and at or below three quarters of 8192.
All inputs are finite; a program needn't handle non-finite values.
Results may differ from the reference program's by a relative error of at most 0.0034.
Values may be sent and summed in bfloat16 or wider, within the bound.
No kernel may reach another device: no remote copies, remote signals or barrier semaphores. Data moves between devices by JAX's collectives and lax.ppermute only.
A program may use at most 128 MiB of HBM per device.

```python
import math
import jax
import jax.numpy as jnp
from jax import lax

H = 16
DK = 128
HD = 2048
CONV = 4
TOK_LOG = 9
TOK_DEV = 512
TOKENS = 8192
LEVELS = 14
NDOC = 8
N_SEQ = 16


def draw_doc_starts(key, part):
    half_count = TOKENS // 2
    quarter_count = TOKENS // 4
    shuffled = jax.random.permutation(key, half_count - 2)
    picked = jnp.sort(shuffled[:NDOC - 2]).astype(jnp.int32)
    placed = jnp.where(picked < quarter_count, picked + 1, picked + 1 + half_count).astype(jnp.int32)
    final_start = jnp.full((1,), TOKENS - 1, jnp.int32)
    return jnp.concatenate([jnp.zeros((1,), jnp.int32), placed, final_start])


def levels(stream_key, dims, split, smallest, high):
    level, own = 1.0, jax.random.fold_in(stream_key, 6)
    for axis_at, shards_of in split:
        draws = jnp.exp(jax.random.uniform(jax.random.fold_in(own, axis_at), (shards_of,), jnp.float32, smallest / len(split), high / len(split)))
        level = level * jnp.repeat(draws, dims[axis_at] // shards_of).reshape([-1 if axis == axis_at else 1 for axis in range(len(dims))])
    return level


def bell_draw(own_key, shape, scale, bound, shards=(), kind=jnp.bfloat16):
    array = scale * jax.random.normal(own_key, shape, jnp.float32)
    if shards:
        array = array * levels(own_key, shape, shards, -0.22, 0.18)
    return jnp.clip(array, -bound, bound).astype(kind)


def setup_inputs(seed: int = 0, part: int = 0) -> dict:
    arg_keys = jax.random.split(jax.random.key(seed), 8)
    own_keys = jax.random.split(jax.random.fold_in(arg_keys[7], part), 8)
    return {
        "query_in": bell_draw(own_keys[0], (TOKENS, HD), 1.0, 6.0, ((0, 16),)),
        "key_in": bell_draw(own_keys[1], (TOKENS, HD), 1.0, 6.0, ((0, 16),)),
        "value_in": bell_draw(own_keys[2], (TOKENS, HD), 1.0, 6.0, ((0, 16),)),
        "conv_weight": bell_draw(arg_keys[3], (CONV, 3 * HD), CONV ** -0.5, 3.0, (), jnp.float32),
        "level_weight": jnp.clip(jnp.exp(math.log(1.0) - 2.306499 * jax.random.uniform(own_keys[4], (H, LEVELS, TOKENS), jnp.float32) ** levels(own_keys[4], (H, LEVELS, TOKENS), ((2, 16),), -0.2, 0.2)), 0.099609375, 1.0).astype(jnp.bfloat16),
        "out_gain": jnp.clip(1.0 + 0.18 * jax.random.normal(arg_keys[5], (HD,), jnp.float32), 0.1, 1.9),
        "doc_starts": draw_doc_starts(jax.random.fold_in(jax.random.fold_in(arg_keys[7], part), 71), part),
    }


def start_of(doc_starts, positions):
    is_before = doc_starts[None, :] <= positions[:, None]
    return lax.optimization_barrier(jnp.max(jnp.where(is_before, doc_starts[None, :], 0), axis=1)).astype(jnp.int32)

def bit_width(values, bit_count):
    summed = jnp.zeros(values.shape, jnp.int32)
    for bit_place in range(bit_count):
        summed = summed + (values >= 1 << bit_place).astype(jnp.int32)
    return summed

def convolve(extended, weights, starts_tok, positions):
    conv_width = weights.shape[0]
    row_count = positions.shape[0]
    summed = jnp.zeros((row_count, extended.shape[1]), jnp.float32)
    for offset in range(conv_width):
        shifted = extended[conv_width - 1 - offset:conv_width - 1 - offset + row_count].astype(jnp.float32)
        usable = (positions - offset >= starts_tok)[:, None]
        summed = summed + jnp.where(usable, weights[offset][None, :] * shifted, 0.0)
    return summed

def prepare_heads(query_ext, key_ext, value_ext, conv_weight, starts_tok, positions, head_count):
    width_all = query_ext.shape[1]
    row_count = positions.shape[0]
    queries = jax.nn.silu(convolve(query_ext, conv_weight[:, :width_all], starts_tok, positions))
    queries = queries.astype(jnp.bfloat16).reshape(row_count, head_count, width_all // head_count)
    key_rows = jax.nn.silu(convolve(key_ext, conv_weight[:, width_all:2 * width_all], starts_tok, positions))
    key_rows = key_rows.reshape(row_count, head_count, width_all // head_count)
    key_rows = (key_rows / jnp.sqrt(lax.optimization_barrier(jnp.sum(key_rows * key_rows, axis=2, keepdims=True)) + 1e-06)).astype(jnp.bfloat16)
    value_rows = jax.nn.silu(convolve(value_ext, conv_weight[:, 2 * width_all:], starts_tok, positions))
    value_rows = value_rows.astype(jnp.bfloat16).reshape(row_count, head_count, width_all // head_count)
    return (queries, key_rows, value_rows)

def reference(query_in, key_in, value_in, conv_weight, level_weight, out_gain, doc_starts):
    conv_width = conv_weight.shape[0]
    width_all = H * DK
    dev_bits = N_SEQ.bit_length() - 1

    def padded(inputs):
        return jnp.concatenate([jnp.zeros((conv_width - 1, width_all), inputs.dtype), inputs], axis=0)
    query_pad = padded(query_in)
    key_pad = padded(key_in)
    value_pad = padded(value_in)
    block_ids = jnp.arange(N_SEQ, dtype=jnp.int32)

    def prepare_block(dev_index):
        first_pos = dev_index * TOK_DEV
        positions = first_pos + jnp.arange(TOK_DEV, dtype=jnp.int32)
        starts_tok = start_of(doc_starts, positions)

        def window(source):
            return lax.dynamic_slice_in_dim(source, first_pos, TOK_DEV + conv_width - 1, 0)
        queries, key_rows, value_rows = prepare_heads(window(query_pad), window(key_pad), window(value_pad), conv_weight, starts_tok, positions, H)
        keep_rows = positions >= starts_tok[-1]
        tail_keys = jnp.where(keep_rows[:, None, None], key_rows, jnp.zeros_like(key_rows))
        tail_state = jnp.einsum('shd,she->hde', tail_keys.astype(jnp.float32), value_rows.astype(jnp.float32))
        return (queries, key_rows, value_rows, starts_tok, tail_state)
    queries_all, keys_all, values_all, starts_all, tails = lax.map(prepare_block, block_ids)
    flags = starts_all[:, -1] >= block_ids * TOK_DEV
    level_sums = [tails]
    level_flags = [flags]
    for bit_place in range(dev_bits - 1):
        lower = level_sums[-1][0::2]
        upper = level_sums[-1][1::2]
        upper_has = level_flags[-1][1::2]
        level_sums.append(jnp.where(upper_has[:, None, None, None], upper, lower + upper))
        level_flags.append(level_flags[-1][0::2] | upper_has)
    local_ids = jnp.arange(TOK_DEV, dtype=jnp.int32)
    level_map = bit_width(local_ids[:, None] ^ local_ids[None, :], TOK_LOG)
    local_scale = jnp.exp2(-0.5 * level_map.astype(jnp.float32))

    def output_block(packed):
        dev_index, queries, key_rows, value_rows, starts_tok = packed
        first_pos = dev_index * TOK_DEV
        weights_all = lax.dynamic_slice_in_dim(level_weight, first_pos, TOK_DEV, 2).astype(jnp.float32)
        per_row = jnp.transpose(weights_all, (0, 2, 1))
        picked = jnp.take_along_axis(per_row, jnp.broadcast_to(level_map[None], (H, TOK_DEV, TOK_DEV)), axis=2)
        pair_weight = picked * local_scale[None]
        valid = (local_ids[None, :] <= local_ids[:, None]) & (first_pos + local_ids[None, :] >= starts_tok[:, None])
        scores = jnp.einsum('ihd,jhd->hij', queries.astype(jnp.float32), key_rows.astype(jnp.float32))
        weighted = jnp.where(valid[None], scores * pair_weight, 0.0).astype(jnp.bfloat16)
        near_sum = jnp.einsum('hij,jhd->ihd', weighted.astype(jnp.float32), value_rows.astype(jnp.float32))
        far_sum = jnp.zeros_like(near_sum)
        for bit_place in range(dev_bits):
            is_upper = dev_index >> bit_place & 1 == 1
            sibling = jnp.maximum((dev_index >> bit_place) - 1, 0)
            state = level_sums[bit_place][sibling].astype(jnp.bfloat16)
            level_id = TOK_LOG + 1 + bit_place
            level_mask = is_upper & (starts_tok < (dev_index >> bit_place << bit_place) * TOK_DEV)
            coefs_level = jnp.where(level_mask[:, None], weights_all[:, level_id, :].T * jnp.exp2(jnp.float32(-0.5 * level_id)), 0.0)
            images = jnp.einsum('thd,hde->the', queries.astype(jnp.float32), state.astype(jnp.float32))
            far_sum = far_sum + coefs_level[:, :, None] * images
        summed = near_sum + far_sum
        normed = summed / jnp.sqrt(lax.optimization_barrier(jnp.mean(summed * summed, axis=2, keepdims=True)) + 1e-06)
        return (normed * out_gain.reshape(H, DK)).astype(jnp.bfloat16).reshape(TOK_DEV, H * DK)
    outputs = lax.map(output_block, (block_ids, queries_all, keys_all, values_all, starts_all))
    return outputs.reshape(TOKENS, H * DK)
```

```python
import functools

import jax
import jax.numpy as jnp
from jax import lax
from jax.experimental import pallas as pl
from jax.experimental.pallas import tpu as pltpu
from jax.sharding import PartitionSpec as P

LANES = 128
PAD = 8
NT = (((1,), (1,)), ((), ()))
VMEM_LIMIT = 40 * 1024 * 1024


def exchange(block, partner):
    count = lax.axis_size("seq")
    route = [(i, partner(i)) for i in range(count) if partner(i) is not None]
    return lax.ppermute(block, "seq", route)


def swapped(block, bit):
    return exchange(block, lambda i: i ^ (1 << bit))


def sent_up(block, bit):
    return exchange(block, lambda i: None if i >> bit & 1 else i | 1 << bit)


def start_at(docs_ref, doc_count, positions):
    def step(i, start):
        doc = docs_ref[i]
        return jnp.where(positions >= doc, doc, start)

    return lax.fori_loop(0, doc_count, step, jnp.zeros_like(positions))


def silu(values):
    return values * (0.5 + 0.5 * jnp.tanh(0.5 * values))


def fill_window(window_ref, rim, rows):
    rim_rows = rim.shape[0]
    window_ref[0:PAD, :] = jnp.concatenate(
        [jnp.zeros((PAD - rim_rows, rim.shape[1]), jnp.float32), rim.astype(jnp.float32)], axis=0
    )
    window_ref[PAD:, :] = rows.astype(jnp.float32)


def convolved(window_ref, taps, distance, first, count):
    summed = taps[0:1, :] * window_ref[pl.ds(PAD + first, count), :]
    for offset in range(1, taps.shape[0]):
        term = taps[offset : offset + 1, :] * window_ref[pl.ds(PAD + first - offset, count), :]
        summed = summed + jnp.where(distance >= offset, term, 0.0)
    return summed


def logical_place(head, core_bit, y_bit):
    return ((head >> 3) ^ core_bit) * 8 + (((head >> 2) & 1) ^ y_bit) * 4 + (head & 3)


def distance_rows(docs_ref, doc_count, first_pos, row_count):
    positions = first_pos + lax.broadcasted_iota(jnp.int32, (row_count, LANES), 0)
    return positions - start_at(docs_ref, doc_count, positions)


def key_value_kernel(
    docs_ref,
    key_ref,
    value_ref,
    key_rim_ref,
    value_rim_ref,
    key_taps_ref,
    value_taps_ref,
    key_out_ref,
    value_out_ref,
    state_ref,
    window_ref,
    distance_ref,
    *,
    doc_count,
    chunk,
):
    step = pl.program_id(0)
    row_count, width = key_ref.shape
    heads = width // LANES
    index = lax.axis_index("seq")
    first_pos = index * row_count

    @pl.when(step == 0)
    def _():
        distance_ref[...] = distance_rows(docs_ref, doc_count, first_pos, row_count)

    last_pos = first_pos + row_count - 1
    last_start = start_at(docs_ref, doc_count, jnp.full((1, row_count), last_pos, jnp.int32))
    lanes_pos = first_pos + lax.broadcasted_iota(jnp.int32, (1, row_count), 1)
    keep = jnp.where(lanes_pos >= last_start, 1.0, 0.0)
    for which in range(heads):
        cols = slice(which * LANES, (which + 1) * LANES)
        key_window = window_ref.at[2 * which]
        value_window = window_ref.at[2 * which + 1]
        fill_window(key_window, key_rim_ref[:, cols], key_ref[:, cols])
        fill_window(value_window, value_rim_ref[:, cols], value_ref[:, cols])
        key_taps = key_taps_ref[:, cols]
        value_taps = value_taps_ref[:, cols]
        total = jnp.zeros((LANES, LANES), jnp.float32)
        for first in range(0, row_count, chunk):
            distance = distance_ref[pl.ds(first, chunk), :]
            grown = silu(convolved(key_window, key_taps, distance, first, chunk))
            square = jnp.sum(grown * grown, axis=1, keepdims=True)
            keys = (grown * lax.rsqrt(square + 1e-6)).astype(jnp.bfloat16)
            key_out_ref[pl.ds(first, chunk), cols] = keys
            values = silu(convolved(value_window, value_taps, distance, first, chunk))
            turned = values.T
            value_out_ref[cols, pl.ds(first, chunk)] = turned.astype(jnp.bfloat16)
            kept = (turned * keep[:, first : first + chunk]).astype(jnp.bfloat16)
            total = total + jnp.dot(kept, keys, preferred_element_type=jnp.float32)
        head = step * heads + which
        place = logical_place(head, index & 1, (index >> 1) & 1)
        state_ref[place] = total.astype(jnp.bfloat16)


def near_kernel(
    docs_ref,
    query_ref,
    query_rim_ref,
    query_taps_ref,
    level_ref,
    key_ref,
    value_ref,
    query_out_ref,
    near_ref,
    window_ref,
    distance_ref,
    start_ref,
    coarse_ref,
    *pair_refs,
    doc_count,
    chunk,
):
    step = pl.program_id(0)
    row_count = query_ref.shape[0]
    index = lax.axis_index("seq")
    first_pos = index * row_count
    span = 2 * LANES

    @pl.when(step == 0)
    def _():
        distance_ref[...] = distance_rows(docs_ref, doc_count, first_pos, row_count)
        positions = first_pos + lax.broadcasted_iota(jnp.int32, (8, row_count), 1)
        start_ref[...] = start_at(docs_ref, doc_count, positions) - first_pos
        for pair_ref in pair_refs:
            pair_ref[...] = jnp.zeros_like(pair_ref)

    fill_window(window_ref, query_rim_ref[...], query_ref[...])
    taps = query_taps_ref[...]
    for first in range(0, row_count, chunk):
        distance = distance_ref[pl.ds(first, chunk), :]
        grown = silu(convolved(window_ref, taps, distance, first, chunk))
        query_out_ref[pl.ds(first, chunk), :] = grown.astype(jnp.bfloat16)

    weights = level_ref[0].astype(jnp.float32)
    tok_bits = row_count.bit_length() - 1
    scaled = [weights[lv : lv + 1, :] * 2.0 ** (-lv / 2) for lv in range(tok_bits + 1)]
    row = lax.broadcasted_iota(jnp.int32, (8, row_count), 0)
    lane = lax.broadcasted_iota(jnp.int32, (8, row_count), 1)
    low = row ^ (lane & 7)
    fine = jnp.where(
        low == 0,
        scaled[0],
        jnp.where(low == 1, scaled[1], jnp.where(low < 4, scaled[2], scaled[3])),
    )
    fine = jnp.where(row > (lane & 7), 0.0, fine)
    row = lax.broadcasted_iota(jnp.int32, (16, row_count), 0)
    group = (lax.broadcasted_iota(jnp.int32, (16, row_count), 1) >> 3) & 15
    high = row ^ group
    coarse = jnp.where(
        high < 2,
        scaled[4],
        jnp.where(high < 4, scaled[5], jnp.where(high < 8, scaled[6], scaled[7])),
    )
    coarse = jnp.where(row > group, 0.0, coarse)
    for tile in range(row_count // LANES):
        coarse_ref[tile] = coarse[:, tile * LANES : (tile + 1) * LANES]
    lane_group = lax.broadcasted_iota(jnp.int32, (8, LANES), 1) >> 3
    sublane = lax.broadcasted_iota(jnp.int32, (LANES, LANES), 0)

    for part, pair_ref in enumerate(pair_refs):
        rows = (part + 1) * span
        scores = lax.dot_general(
            key_ref[0:rows, :],
            query_out_ref[part * span : rows, :],
            NT,
            preferred_element_type=jnp.float32,
        )
        for side in range(2):
            tile = 2 * part + side
            lanes = slice(tile * LANES, (tile + 1) * LANES)
            starts = start_ref[0:1, lanes]
            fine_tile = fine[:, lanes]
            for other in range(tile + 1):
                if other == tile:
                    weight = jnp.concatenate(
                        [
                            jnp.where(
                                lane_group == a,
                                fine_tile,
                                coarse_ref[tile, pl.ds(a, 8, stride=0), :],
                            )
                            for a in range(LANES // 8)
                        ],
                        axis=0,
                    )
                else:
                    weight = scaled[7 + (tile ^ other).bit_length()][:, lanes]
                piece = scores[
                    other * LANES : (other + 1) * LANES, side * LANES : (side + 1) * LANES
                ]
                valid = sublane >= starts - other * LANES
                pair_ref[
                    other * LANES : (other + 1) * LANES, side * LANES : (side + 1) * LANES
                ] = jnp.where(valid, piece * weight, 0.0).astype(jnp.bfloat16)
        near_ref[:, part * span : rows] = jnp.dot(
            value_ref[:, 0:rows], pair_ref[...], preferred_element_type=jnp.float32
        )


def far_kernel(
    docs_ref,
    query_ref,
    near_ref,
    level_ref,
    first_state_ref,
    own_state_ref,
    other_state_ref,
    gain_ref,
    out_ref,
    start_ref,
    *,
    doc_count,
    dev_bits,
):
    head = pl.program_id(0)
    row_count = query_ref.shape[0]
    index = lax.axis_index("seq")
    first_pos = index * row_count

    @pl.when(head == 0)
    def _():
        positions = first_pos + lax.broadcasted_iota(jnp.int32, (8, row_count), 1)
        start_ref[...] = start_at(docs_ref, doc_count, positions)

    core_bit = index & 1
    y_bit = (index >> 1) & 1
    tok_bits = row_count.bit_length() - 1
    first_place = logical_place(head, 1 - core_bit, y_bit)
    place = logical_place(head, core_bit, y_bit)
    is_own = place < 8
    states = [first_state_ref[first_place]]
    for level in range(dev_bits - 1):
        states.append(
            jnp.where(is_own, own_state_ref[level, place & 7], other_state_ref[level, place & 7])
        )
    images = lax.dot_general(
        jnp.concatenate(states, axis=0), query_ref[...], NT, preferred_element_type=jnp.float32
    )
    weights = level_ref[0].astype(jnp.float32)
    starts = start_ref[0:1, :]
    summed = near_ref[...]
    for bit in range(dev_bits):
        level_id = tok_bits + 1 + bit
        limit = jnp.where((index >> bit) & 1 == 1, (index >> bit << bit) * row_count, 0)
        coef = jnp.where(
            starts < limit, weights[level_id : level_id + 1, :] * 2.0 ** (-level_id / 2), 0.0
        )
        summed = summed + coef * images[bit * LANES : (bit + 1) * LANES, :]
    mean = jnp.mean(summed * summed, axis=0, keepdims=True)
    normed = summed * lax.rsqrt(mean + 1e-6)
    out_ref[...] = (normed.T * gain_ref[0]).astype(jnp.bfloat16)


def local(query_in, key_in, value_in, conv_weight, level_weight, out_gain, doc_starts):
    row_count, width_all = query_in.shape
    head_count, level_count, _ = level_weight.shape
    head_size = width_all // head_count
    conv_width = conv_weight.shape[0]
    doc_count = doc_starts.shape[0]
    dev_index = lax.axis_index("seq")
    dev_count = lax.axis_size("seq")
    dev_bits = dev_count.bit_length() - 1
    rim_rows = conv_width - 1
    params = pltpu.CompilerParams(vmem_limit_bytes=VMEM_LIMIT)
    smem = pl.BlockSpec(memory_space=pltpu.SMEM)
    whole = pl.BlockSpec(memory_space=pltpu.VMEM)

    tails = jnp.concatenate(
        [query_in[row_count - rim_rows :], key_in[row_count - rim_rows :], value_in[row_count - rim_rows :]],
        axis=1,
    )
    rims = exchange(tails, lambda i: i + 1 if i + 1 < dev_count else None)

    heads = 2
    steps = head_count // heads
    wide = heads * head_size
    keys, values_t, state = pl.pallas_call(
        functools.partial(key_value_kernel, doc_count=doc_count, chunk=LANES),
        grid=(steps,),
        in_specs=[
            smem,
            pl.BlockSpec((row_count, wide), lambda i: (0, i)),
            pl.BlockSpec((row_count, wide), lambda i: (0, i)),
            pl.BlockSpec((rim_rows, wide), lambda i: (0, steps + i)),
            pl.BlockSpec((rim_rows, wide), lambda i: (0, 2 * steps + i)),
            pl.BlockSpec((conv_width, wide), lambda i: (0, steps + i)),
            pl.BlockSpec((conv_width, wide), lambda i: (0, 2 * steps + i)),
        ],
        out_specs=[
            pl.BlockSpec((row_count, wide), lambda i: (0, i)),
            pl.BlockSpec((wide, row_count), lambda i: (i, 0)),
            pl.BlockSpec((head_count, head_size, head_size), lambda i: (0, 0, 0)),
        ],
        out_shape=[
            jax.ShapeDtypeStruct((row_count, width_all), jnp.bfloat16),
            jax.ShapeDtypeStruct((width_all, row_count), jnp.bfloat16),
            jax.ShapeDtypeStruct((head_count, head_size, head_size), jnp.bfloat16),
        ],
        scratch_shapes=[
            pltpu.VMEM((2 * heads, row_count + PAD, LANES), jnp.float32),
            pltpu.VMEM((row_count, LANES), jnp.int32),
        ],
        compiler_params=params,
        cost_estimate=pl.CostEstimate(flops=300_000_000, bytes_accessed=8_000_000, transcendentals=2_000_000),
        name="key_value",
    )(doc_starts, key_in, value_in, rims, rims, conv_weight, conv_weight)

    def joined(mine, theirs, bit):
        stride = 1 << bit
        upper_first = ((dev_index >> bit + 1 << bit + 1) + stride) * row_count
        upper_has = jnp.any(
            (doc_starts >= upper_first) & (doc_starts < upper_first + stride * row_count)
        )
        mine = mine.astype(jnp.float32)
        theirs = theirs.astype(jnp.float32)
        is_upper = dev_index >> bit & 1 == 1
        keep_mine = jnp.where(upper_has & ~is_upper, 0.0, 1.0)
        keep_theirs = jnp.where(upper_has & is_upper, 0.0, 1.0)
        return (mine * keep_mine + theirs * keep_theirs).astype(jnp.bfloat16)

    half = head_count // 2
    quarter = head_count // 4
    first_state = swapped(state, 0)
    pair = joined(state[:half], first_state[half:], 0)
    pair_in = swapped(pair[quarter:], 1)
    carried = joined(pair[:quarter], pair_in, 1)
    received = []
    for bit in range(2, dev_bits):
        last = bit == dev_bits - 1
        arrived = sent_up(carried, bit) if last else swapped(carried, bit)
        received.append(arrived)
        if not last:
            carried = joined(carried, arrived, bit)

    grid = (head_count,)
    queries, near = pl.pallas_call(
        functools.partial(near_kernel, doc_count=doc_count, chunk=LANES),
        grid=grid,
        in_specs=[
            smem,
            pl.BlockSpec((row_count, head_size), lambda i: (0, i)),
            pl.BlockSpec((rim_rows, head_size), lambda i: (0, i)),
            pl.BlockSpec((conv_width, head_size), lambda i: (0, i)),
            pl.BlockSpec((1, level_count, row_count), lambda i: (i, 0, 0)),
            pl.BlockSpec((row_count, head_size), lambda i: (0, i)),
            pl.BlockSpec((head_size, row_count), lambda i: (i, 0)),
        ],
        out_specs=[
            pl.BlockSpec((row_count, head_size), lambda i: (0, i)),
            pl.BlockSpec((head_size, row_count), lambda i: (i, 0)),
        ],
        out_shape=[
            jax.ShapeDtypeStruct((row_count, width_all), jnp.bfloat16),
            jax.ShapeDtypeStruct((width_all, row_count), jnp.float32),
        ],
        scratch_shapes=[
            pltpu.VMEM((row_count + PAD, LANES), jnp.float32),
            pltpu.VMEM((row_count, LANES), jnp.int32),
            pltpu.VMEM((8, row_count), jnp.int32),
            pltpu.VMEM((row_count // LANES, 16, LANES), jnp.float32),
        ]
        + [
            pltpu.VMEM(((part + 1) * 2 * LANES, 2 * LANES), jnp.bfloat16)
            for part in range(row_count // (2 * LANES))
        ],
        compiler_params=params,
        cost_estimate=pl.CostEstimate(flops=2_000_000_000, bytes_accessed=14_000_000, transcendentals=1_000_000),
        name="near",
    )(doc_starts, query_in, rims, conv_weight, level_weight, keys, values_t)

    mine = jnp.stack([pair[:quarter]] + received)
    theirs = swapped(mine, 1)
    own = jnp.concatenate(
        [jnp.concatenate([pair_in[None], mine[1:]], axis=0), theirs], axis=1
    )
    other = swapped(own, 0)

    return pl.pallas_call(
        functools.partial(far_kernel, doc_count=doc_count, dev_bits=dev_bits),
        grid=grid,
        in_specs=[
            smem,
            pl.BlockSpec((row_count, head_size), lambda i: (0, i)),
            pl.BlockSpec((head_size, row_count), lambda i: (i, 0)),
            pl.BlockSpec((1, level_count, row_count), lambda i: (i, 0, 0)),
            whole,
            whole,
            whole,
            pl.BlockSpec((1, 1, head_size), lambda i: (i, 0, 0)),
        ],
        out_specs=pl.BlockSpec((row_count, head_size), lambda i: (0, i)),
        out_shape=jax.ShapeDtypeStruct((row_count, width_all), jnp.bfloat16),
        scratch_shapes=[pltpu.VMEM((8, row_count), jnp.int32)],
        compiler_params=params,
        cost_estimate=pl.CostEstimate(flops=1_000_000_000, bytes_accessed=10_000_000, transcendentals=10_000),
        name="far",
    )(
        doc_starts,
        queries,
        near,
        level_weight,
        first_state,
        own,
        other,
        out_gain.reshape(head_count, 1, head_size),
    )


def solution(mesh):
    in_specs = (
        P(("groups", "seq"), None),
        P(("groups", "seq"), None),
        P(("groups", "seq"), None),
        P(),
        P(None, None, ("groups", "seq")),
        P(),
        P("groups"),
    )
    out_specs = P(("groups", "seq"), None)
    return jax.shard_map(local, mesh=mesh, in_specs=in_specs, out_specs=out_specs, check_vma=False)
```

```python
import functools

import jax
import jax.numpy as jnp
from jax import lax
from jax.experimental import pallas as pl
from jax.experimental.pallas import tpu as pltpu
from jax.sharding import PartitionSpec as P

LANES = 128
PAD = 8
NT = (((1,), (1,)), ((), ()))
VMEM_LIMIT = 56 * 1024 * 1024


def exchange(block, partner):
    count = lax.axis_size("seq")
    route = [(i, partner(i)) for i in range(count) if partner(i) is not None]
    return lax.ppermute(block, "seq", route)


def swapped(block, bit):
    return exchange(block, lambda i: i ^ (1 << bit))


def sent_up(block, bit):
    return exchange(block, lambda i: None if i >> bit & 1 else i | 1 << bit)


def start_at(docs_ref, doc_count, positions):
    def step(i, start):
        doc = docs_ref[i]
        return jnp.where(positions >= doc, doc, start)

    return lax.fori_loop(0, doc_count, step, jnp.zeros_like(positions))


def silu(values):
    return values * (0.5 + 0.5 * jnp.tanh(0.5 * values))


def fill_window(window_ref, rim, rows):
    rim_rows = rim.shape[0]
    window_ref[0:PAD, :] = jnp.concatenate(
        [jnp.zeros((PAD - rim_rows, rim.shape[1]), jnp.float32), rim.astype(jnp.float32)], axis=0
    )
    window_ref[PAD:, :] = rows.astype(jnp.float32)


def convolved(window_ref, taps, distance, first, count):
    summed = taps[0:1, :] * window_ref[pl.ds(PAD + first, count), :]
    for offset in range(1, taps.shape[0]):
        term = taps[offset : offset + 1, :] * window_ref[pl.ds(PAD + first - offset, count), :]
        summed = summed + jnp.where(distance >= offset, term, 0.0)
    return summed


def logical_place(head, core_bit, y_bit):
    return ((head >> 3) ^ core_bit) * 8 + (((head >> 2) & 1) ^ y_bit) * 4 + (head & 3)


def distance_rows(docs_ref, doc_count, first_pos, row_count):
    positions = first_pos + lax.broadcasted_iota(jnp.int32, (row_count, LANES), 0)
    return positions - start_at(docs_ref, doc_count, positions)


def rim_kernel(query_ref, key_ref, value_ref, out_ref):
    rim_rows = out_ref.shape[0]
    width = query_ref.shape[1]
    for part, ref in enumerate((query_ref, key_ref, value_ref)):
        rows = ref.shape[0]
        out_ref[:, part * width : (part + 1) * width] = ref[rows - rim_rows : rows, :]


def key_value_kernel(
    docs_ref,
    key_ref,
    value_ref,
    key_rim_ref,
    value_rim_ref,
    key_taps_ref,
    value_taps_ref,
    key_out_ref,
    value_out_ref,
    state_ref,
    window_ref,
    distance_ref,
    *,
    doc_count,
    chunk,
):
    step = pl.program_id(0)
    row_count, width = key_ref.shape
    heads = width // LANES
    index = lax.axis_index("seq")
    first_pos = index * row_count

    @pl.when(step == 0)
    def _():
        distance_ref[...] = distance_rows(docs_ref, doc_count, first_pos, row_count)

    last_pos = first_pos + row_count - 1
    last_start = start_at(docs_ref, doc_count, jnp.full((1, row_count), last_pos, jnp.int32))
    lanes_pos = first_pos + lax.broadcasted_iota(jnp.int32, (1, row_count), 1)
    keep = jnp.where(lanes_pos >= last_start, 1.0, 0.0)
    for which in range(heads):
        cols = slice(which * LANES, (which + 1) * LANES)
        key_window = window_ref.at[2 * which]
        value_window = window_ref.at[2 * which + 1]
        fill_window(key_window, key_rim_ref[:, cols], key_ref[:, cols])
        fill_window(value_window, value_rim_ref[:, cols], value_ref[:, cols])
        key_taps = key_taps_ref[:, cols]
        value_taps = value_taps_ref[:, cols]
        total = jnp.zeros((LANES, LANES), jnp.float32)
        for first in range(0, row_count, chunk):
            distance = distance_ref[pl.ds(first, chunk), :]
            grown = silu(convolved(key_window, key_taps, distance, first, chunk))
            square = jnp.sum(grown * grown, axis=1, keepdims=True)
            keys = (grown * lax.rsqrt(square + 1e-6)).astype(jnp.bfloat16)
            key_out_ref[pl.ds(first, chunk), cols] = keys
            values = silu(convolved(value_window, value_taps, distance, first, chunk))
            turned = values.T
            value_out_ref[cols, pl.ds(first, chunk)] = turned.astype(jnp.bfloat16)
            kept = (turned * keep[:, first : first + chunk]).astype(jnp.bfloat16)
            total = total + jnp.dot(kept, keys, preferred_element_type=jnp.float32)
        head = step * heads + which
        place = logical_place(head, index & 1, (index >> 1) & 1)
        state_ref[place] = total.astype(jnp.bfloat16)


def near_kernel(
    docs_ref,
    query_ref,
    query_rim_ref,
    query_taps_ref,
    level_ref,
    key_ref,
    value_ref,
    *rest,
    doc_count,
    chunk,
    skipped,
):
    query_out_ref, near_ref, window_ref, distance_ref, start_ref, coarse_ref, *pair_refs = rest[
        skipped:
    ]
    step = pl.program_id(0)
    row_count = query_ref.shape[0]
    index = lax.axis_index("seq")
    first_pos = index * row_count
    span = 2 * LANES

    @pl.when(step == 0)
    def _():
        distance_ref[...] = distance_rows(docs_ref, doc_count, first_pos, row_count)
        positions = first_pos + lax.broadcasted_iota(jnp.int32, (8, row_count), 1)
        start_ref[...] = start_at(docs_ref, doc_count, positions) - first_pos
        for pair_ref in pair_refs:
            pair_ref[...] = jnp.zeros_like(pair_ref)

    fill_window(window_ref, query_rim_ref[...], query_ref[...])
    taps = query_taps_ref[...]
    for first in range(0, row_count, chunk):
        distance = distance_ref[pl.ds(first, chunk), :]
        grown = silu(convolved(window_ref, taps, distance, first, chunk))
        query_out_ref[pl.ds(first, chunk), :] = grown.astype(jnp.bfloat16)

    weights = level_ref[0].astype(jnp.float32)
    tok_bits = row_count.bit_length() - 1
    scaled = [weights[lv : lv + 1, :] * 2.0 ** (-lv / 2) for lv in range(tok_bits + 1)]
    row = lax.broadcasted_iota(jnp.int32, (8, row_count), 0)
    lane = lax.broadcasted_iota(jnp.int32, (8, row_count), 1)
    low = row ^ (lane & 7)
    fine = jnp.where(
        low == 0,
        scaled[0],
        jnp.where(low == 1, scaled[1], jnp.where(low < 4, scaled[2], scaled[3])),
    )
    fine = jnp.where(row > (lane & 7), 0.0, fine)
    row = lax.broadcasted_iota(jnp.int32, (16, row_count), 0)
    group = (lax.broadcasted_iota(jnp.int32, (16, row_count), 1) >> 3) & 15
    high = row ^ group
    coarse = jnp.where(
        high < 2,
        scaled[4],
        jnp.where(high < 4, scaled[5], jnp.where(high < 8, scaled[6], scaled[7])),
    )
    coarse = jnp.where(row > group, 0.0, coarse)
    for tile in range(row_count // LANES):
        coarse_ref[tile] = coarse[:, tile * LANES : (tile + 1) * LANES]
    lane_group = lax.broadcasted_iota(jnp.int32, (8, LANES), 1) >> 3
    sublane = lax.broadcasted_iota(jnp.int32, (LANES, LANES), 0)

    for part, pair_ref in enumerate(pair_refs):
        rows = (part + 1) * span
        scores = lax.dot_general(
            key_ref[0:rows, :],
            query_out_ref[part * span : rows, :],
            NT,
            preferred_element_type=jnp.float32,
        )
        for side in range(2):
            tile = 2 * part + side
            lanes = slice(tile * LANES, (tile + 1) * LANES)
            starts = start_ref[0:1, lanes]
            fine_tile = fine[:, lanes]
            for other in range(tile + 1):
                if other == tile:
                    weight = jnp.concatenate(
                        [
                            jnp.where(
                                lane_group == a,
                                fine_tile,
                                coarse_ref[tile, pl.ds(a, 8, stride=0), :],
                            )
                            for a in range(LANES // 8)
                        ],
                        axis=0,
                    )
                else:
                    weight = scaled[7 + (tile ^ other).bit_length()][:, lanes]
                piece = scores[
                    other * LANES : (other + 1) * LANES, side * LANES : (side + 1) * LANES
                ]
                valid = sublane >= starts - other * LANES
                pair_ref[
                    other * LANES : (other + 1) * LANES, side * LANES : (side + 1) * LANES
                ] = jnp.where(valid, piece * weight, 0.0).astype(jnp.bfloat16)
        near_ref[:, part * span : rows] = jnp.dot(
            value_ref[:, 0:rows], pair_ref[...], preferred_element_type=jnp.float32
        )


def far_kernel(
    docs_ref,
    query_ref,
    near_ref,
    level_ref,
    first_state_ref,
    own_state_ref,
    other_state_ref,
    gain_ref,
    out_ref,
    start_ref,
    *,
    doc_count,
    dev_bits,
):
    head = pl.program_id(0)
    row_count = query_ref.shape[0]
    index = lax.axis_index("seq")
    first_pos = index * row_count

    @pl.when(head == 0)
    def _():
        positions = first_pos + lax.broadcasted_iota(jnp.int32, (8, row_count), 1)
        start_ref[...] = start_at(docs_ref, doc_count, positions)

    core_bit = index & 1
    y_bit = (index >> 1) & 1
    tok_bits = row_count.bit_length() - 1
    first_place = logical_place(head, 1 - core_bit, y_bit)
    place = logical_place(head, core_bit, y_bit)
    is_own = place < 8
    states = [first_state_ref[first_place]]
    for level in range(dev_bits - 1):
        states.append(
            jnp.where(is_own, own_state_ref[level, place & 7], other_state_ref[level, place & 7])
        )
    images = lax.dot_general(
        jnp.concatenate(states, axis=0), query_ref[...], NT, preferred_element_type=jnp.float32
    )
    weights = level_ref[0].astype(jnp.float32)
    starts = start_ref[0:1, :]
    summed = near_ref[...]
    for bit in range(dev_bits):
        level_id = tok_bits + 1 + bit
        limit = jnp.where((index >> bit) & 1 == 1, (index >> bit << bit) * row_count, 0)
        coef = jnp.where(
            starts < limit, weights[level_id : level_id + 1, :] * 2.0 ** (-level_id / 2), 0.0
        )
        summed = summed + coef * images[bit * LANES : (bit + 1) * LANES, :]
    mean = jnp.mean(summed * summed, axis=0, keepdims=True)
    normed = summed * lax.rsqrt(mean + 1e-6)
    out_ref[...] = (normed.T * gain_ref[0]).astype(jnp.bfloat16)


def local(query_in, key_in, value_in, conv_weight, level_weight, out_gain, doc_starts):
    row_count, width_all = query_in.shape
    head_count, level_count, _ = level_weight.shape
    head_size = width_all // head_count
    conv_width = conv_weight.shape[0]
    doc_count = doc_starts.shape[0]
    dev_index = lax.axis_index("seq")
    dev_count = lax.axis_size("seq")
    dev_bits = dev_count.bit_length() - 1
    rim_rows = conv_width - 1
    params = pltpu.CompilerParams(vmem_limit_bytes=VMEM_LIMIT)
    smem = pl.BlockSpec(memory_space=pltpu.SMEM)
    whole = pl.BlockSpec(memory_space=pltpu.VMEM)

    edge = 16
    tails = pl.pallas_call(
        rim_kernel,
        grid=(1,),
        in_specs=[pl.BlockSpec((edge, width_all), lambda i: (row_count // edge - 1, 0))] * 3,
        out_specs=pl.BlockSpec((rim_rows, 3 * width_all), lambda i: (0, 0)),
        out_shape=jax.ShapeDtypeStruct((rim_rows, 3 * width_all), query_in.dtype),
        name="rim",
    )(query_in, key_in, value_in)
    rims = exchange(tails, lambda i: i + 1 if i + 1 < dev_count else None)

    heads = 2
    steps = head_count // heads
    wide = heads * head_size
    keys, values_t, state = pl.pallas_call(
        functools.partial(key_value_kernel, doc_count=doc_count, chunk=LANES),
        grid=(steps,),
        in_specs=[
            smem,
            pl.BlockSpec((row_count, wide), lambda i: (0, i)),
            pl.BlockSpec((row_count, wide), lambda i: (0, i)),
            pl.BlockSpec((rim_rows, wide), lambda i: (0, steps + i)),
            pl.BlockSpec((rim_rows, wide), lambda i: (0, 2 * steps + i)),
            pl.BlockSpec((conv_width, wide), lambda i: (0, steps + i)),
            pl.BlockSpec((conv_width, wide), lambda i: (0, 2 * steps + i)),
        ],
        out_specs=[
            pl.BlockSpec((row_count, wide), lambda i: (0, i)),
            pl.BlockSpec((wide, row_count), lambda i: (i, 0)),
            pl.BlockSpec((head_count, head_size, head_size), lambda i: (0, 0, 0)),
        ],
        out_shape=[
            jax.ShapeDtypeStruct((row_count, width_all), jnp.bfloat16),
            jax.ShapeDtypeStruct((width_all, row_count), jnp.bfloat16),
            jax.ShapeDtypeStruct((head_count, head_size, head_size), jnp.bfloat16),
        ],
        scratch_shapes=[
            pltpu.VMEM((2 * heads, row_count + PAD, LANES), jnp.float32),
            pltpu.VMEM((row_count, LANES), jnp.int32),
        ],
        compiler_params=params,
        cost_estimate=pl.CostEstimate(flops=300_000_000, bytes_accessed=8_000_000, transcendentals=2_000_000),
        name="key_value",
    )(doc_starts, key_in, value_in, rims, rims, conv_weight, conv_weight)

    def joined(mine, theirs, bit):
        stride = 1 << bit
        upper_first = ((dev_index >> bit + 1 << bit + 1) + stride) * row_count
        upper_has = jnp.any(
            (doc_starts >= upper_first) & (doc_starts < upper_first + stride * row_count)
        )
        mine = mine.astype(jnp.float32)
        theirs = theirs.astype(jnp.float32)
        is_upper = dev_index >> bit & 1 == 1
        keep_mine = jnp.where(upper_has & ~is_upper, 0.0, 1.0)
        keep_theirs = jnp.where(upper_has & is_upper, 0.0, 1.0)
        return (mine * keep_mine + theirs * keep_theirs).astype(jnp.bfloat16)

    buffers = None
    piece_heads = head_count // 4

    def near_piece(piece, buffers, docs):
        first = piece * piece_heads
        aliased = {} if buffers is None else {7: 0, 8: 1}
        extra_specs = [] if buffers is None else [pl.BlockSpec(memory_space=pl.ANY)] * 2
        kernel = functools.partial(
            near_kernel, doc_count=doc_count, chunk=LANES, skipped=len(extra_specs)
        )
        return pl.pallas_call(
            kernel,
            grid=(piece_heads,),
            in_specs=[
                smem,
                pl.BlockSpec((row_count, head_size), lambda i: (0, first + i)),
                pl.BlockSpec((rim_rows, head_size), lambda i: (0, first + i)),
                pl.BlockSpec((conv_width, head_size), lambda i: (0, first + i)),
                pl.BlockSpec((1, level_count, row_count), lambda i: (first + i, 0, 0)),
                pl.BlockSpec((row_count, head_size), lambda i: (0, first + i)),
                pl.BlockSpec((head_size, row_count), lambda i: (first + i, 0)),
            ]
            + extra_specs,
            out_specs=[
                pl.BlockSpec((row_count, head_size), lambda i: (0, first + i)),
                pl.BlockSpec((head_size, row_count), lambda i: (first + i, 0)),
            ],
            out_shape=[
                jax.ShapeDtypeStruct((row_count, width_all), jnp.bfloat16),
                jax.ShapeDtypeStruct((width_all, row_count), jnp.float32),
            ],
            scratch_shapes=[
                pltpu.VMEM((row_count + PAD, LANES), jnp.float32),
                pltpu.VMEM((row_count, LANES), jnp.int32),
                pltpu.VMEM((8, row_count), jnp.int32),
                pltpu.VMEM((row_count // LANES, 16, LANES), jnp.float32),
            ]
            + [
                pltpu.VMEM(((part + 1) * 2 * LANES, 2 * LANES), jnp.bfloat16)
                for part in range(row_count // (2 * LANES))
            ],
            input_output_aliases=aliased,
            compiler_params=params,
            cost_estimate=pl.CostEstimate(
                flops=500_000_000, bytes_accessed=3_500_000, transcendentals=300_000
            ),
            name="near",
        )(docs, query_in, rims, conv_weight, level_weight, keys, values_t, *(buffers or ()))

    def covered(payload, send, piece, buffers):
        payload, docs = lax.optimization_barrier((payload, doc_starts))
        arrived = send(payload)
        buffers = near_piece(piece, buffers, docs)
        arrived, buffers = lax.optimization_barrier((arrived, buffers))
        return arrived, buffers

    half = head_count // 2
    quarter = head_count // 4
    first_state = swapped(state, 0)
    pair = joined(state[:half], first_state[half:], 0)
    pair_in, buffers = covered(pair[quarter:], lambda x: swapped(x, 1), 0, buffers)
    carried = joined(pair[:quarter], pair_in, 1)
    received = []
    for bit in range(2, dev_bits):
        last = bit == dev_bits - 1
        if last:
            arrived, buffers = covered(carried, lambda x: sent_up(x, bit), 2, buffers)
        elif bit == 2:
            arrived, buffers = covered(carried, lambda x: swapped(x, bit), 1, buffers)
        else:
            arrived = swapped(carried, bit)
        received.append(arrived)
        if not last:
            carried = joined(carried, arrived, bit)

    mine = jnp.stack([pair[:quarter]] + received)
    theirs, buffers = covered(mine, lambda x: swapped(x, 1), 3, buffers)
    queries, near = buffers
    own = jnp.concatenate(
        [jnp.concatenate([pair_in[None], mine[1:]], axis=0), theirs], axis=1
    )
    other = swapped(own, 0)

    return pl.pallas_call(
        functools.partial(far_kernel, doc_count=doc_count, dev_bits=dev_bits),
        grid=(head_count,),
        in_specs=[
            smem,
            pl.BlockSpec((row_count, head_size), lambda i: (0, i)),
            pl.BlockSpec((head_size, row_count), lambda i: (i, 0)),
            pl.BlockSpec((1, level_count, row_count), lambda i: (i, 0, 0)),
            whole,
            whole,
            whole,
            pl.BlockSpec((1, 1, head_size), lambda i: (i, 0, 0)),
        ],
        out_specs=pl.BlockSpec((row_count, head_size), lambda i: (0, i)),
        out_shape=jax.ShapeDtypeStruct((row_count, width_all), jnp.bfloat16),
        scratch_shapes=[pltpu.VMEM((8, row_count), jnp.int32)],
        compiler_params=params,
        cost_estimate=pl.CostEstimate(flops=1_000_000_000, bytes_accessed=10_000_000, transcendentals=10_000),
        name="far",
    )(
        doc_starts,
        queries,
        near,
        level_weight,
        first_state,
        own,
        other,
        out_gain.reshape(head_count, 1, head_size),
    )


def solution(mesh):
    in_specs = (
        P(("groups", "seq"), None),
        P(("groups", "seq"), None),
        P(("groups", "seq"), None),
        P(),
        P(None, None, ("groups", "seq")),
        P(),
        P("groups"),
    )
    out_specs = P(("groups", "seq"), None)
    return jax.shard_map(local, mesh=mesh, in_specs=in_specs, out_specs=out_specs, check_vma=False)
```

```python
import functools

import jax
import jax.numpy as jnp
from jax import lax
from jax.experimental import pallas as pl
from jax.experimental.pallas import tpu as pltpu
from jax.sharding import PartitionSpec as P

LANES = 128
PAD = 8
NT = (((1,), (1,)), ((), ()))


def exchange(block, partner):
    count = lax.axis_size("seq")
    route = [(i, partner(i)) for i in range(count) if partner(i) is not None]
    return lax.ppermute(block, "seq", route)


def swapped(block, bit):
    return exchange(block, lambda i: i ^ (1 << bit))


def sent_up(block, bit):
    return exchange(block, lambda i: None if i >> bit & 1 else i | 1 << bit)


def limited(mebibytes):
    return pltpu.CompilerParams(vmem_limit_bytes=mebibytes * 1024 * 1024)


def start_at(docs_ref, doc_count, positions):
    def step(i, start):
        doc = docs_ref[i]
        return jnp.where(positions >= doc, doc, start)

    return lax.fori_loop(0, doc_count, step, jnp.zeros_like(positions))


def silu(values):
    return values * (0.5 + 0.5 * jnp.tanh(0.5 * values))


def logical_place(head, core_bit, y_bit):
    return ((head >> 3) ^ core_bit) * 8 + (((head >> 2) & 1) ^ y_bit) * 4 + (head & 3)


def row_at(place):
    return ((place & 7) << 4) | ((place >> 3) & 15)


def selection(row_of, place_of):
    shape = (LANES, LANES)
    rows = lax.broadcasted_iota(jnp.int32, shape, row_of)
    places = lax.broadcasted_iota(jnp.int32, shape, place_of)
    return jnp.where(rows == row_at(places), 1.0, 0.0).astype(jnp.bfloat16)


def rim_kernel(query_ref, key_ref, value_ref, out_ref, buffer, sems):
    rim_rows = out_ref.shape[0]
    edge, width = buffer.shape[1:]
    copies = []
    for part, ref in enumerate((query_ref, key_ref, value_ref)):
        rows = ref.shape[0]
        copy = pltpu.make_async_copy(
            ref.at[rows - edge : rows, :], buffer.at[part], sems.at[part]
        )
        copy.start()
        copies.append(copy)
    for part, copy in enumerate(copies):
        copy.wait()
        out_ref[:, part * width : (part + 1) * width] = buffer[part, edge - rim_rows : edge, :]


def tables_kernel(
    docs_ref,
    level_ref,
    gain_ref,
    table_ref,
    start_ref,
    distance_ref,
    gain_out_ref,
    flag_ref,
    *,
    doc_count,
):
    level_count, head_count, row_count = level_ref.shape
    tiles = row_count // LANES
    tok_bits = row_count.bit_length() - 1
    index = lax.axis_index("seq")
    first_pos = index * row_count
    lanes = lax.broadcasted_iota(jnp.int32, (8, row_count), 1)
    positions = first_pos + (lanes & -LANES) + row_at(lanes & (LANES - 1))
    starts = start_at(docs_ref, doc_count, positions)
    start_ref[...] = starts - first_pos
    select = selection(0, 1)
    starts = jnp.concatenate([starts] * (head_count // 8), axis=0)
    for level in range(level_count):
        scale = 2.0 ** (-level / 2)
        for tile in range(tiles):
            cols = slice(tile * LANES, (tile + 1) * LANES)
            weights = jnp.dot(level_ref[level, :, cols], select, preferred_element_type=jnp.float32)
            weights = weights * scale
            if level > tok_bits:
                bit = level - tok_bits - 1
                limit = jnp.where((index >> bit) & 1 == 1, (index >> bit << bit) * row_count, 0)
                weights = jnp.where(starts[:, cols] < limit, weights, 0.0)
            table_ref[level, :, cols] = weights
    places = lax.broadcasted_iota(jnp.int32, (row_count, LANES), 0)
    positions = first_pos + (places & -LANES) + row_at(places & (LANES - 1))
    distance_ref[...] = positions - start_at(docs_ref, doc_count, positions)

    def gain_step(head, carry):
        gain_out_ref[head] = jnp.broadcast_to(gain_ref[head], (LANES, LANES)).T
        return carry

    lax.fori_loop(0, head_count, gain_step, 0)

    for tile in range(tiles):
        tile_first = first_pos + tile * LANES

        def step(i, flag):
            gap = docs_ref[i] - tile_first
            return jnp.where((gap > -8) & (gap < LANES), 1, flag)

        flag_ref[tile] = lax.fori_loop(0, doc_count, step, jnp.int32(0))


def fill_window(window_ref, rim, rows):
    rim_rows = rim.shape[0]
    window_ref[0:PAD, :] = jnp.concatenate(
        [jnp.zeros((PAD - rim_rows, rim.shape[1]), jnp.float32), rim.astype(jnp.float32)], axis=0
    )
    window_ref[PAD:, :] = rows.astype(jnp.float32)


def convolved(window_ref, taps, tile, distance):
    reach = taps.shape[0] - 1
    rows = [
        window_ref[pl.ds(PAD + tile * LANES + i, 8, stride=16), :] for i in range(-reach, 16)
    ]
    summed = taps[0:1, :] * jnp.concatenate(rows[reach:], axis=0)
    for offset in range(1, reach + 1):
        term = taps[offset : offset + 1, :] * jnp.concatenate(
            rows[reach - offset : reach - offset + 16], axis=0
        )
        if distance is not None:
            term = jnp.where(distance >= offset, term, 0.0)
        summed = summed + term
    return summed


def per_tile(flag_ref, tiles, body):
    for tile in range(tiles):
        flagged = flag_ref[tile] == 1

        @pl.when(flagged)
        def _():
            body(tile, True)

        @pl.when(jnp.logical_not(flagged))
        def _():
            body(tile, False)


def columns(first):
    return pl.ds(pl.multiple_of(first, LANES), LANES)


def key_value_kernel(
    docs_ref,
    flag_ref,
    key_ref,
    value_ref,
    rim_ref,
    taps_ref,
    distance_ref,
    key_out_ref,
    value_out_ref,
    state_ref,
    window_ref,
    *,
    doc_count,
    heads,
):
    row_count, width = key_ref.shape
    head_count = width // LANES
    steps = head_count // heads
    tiles = row_count // LANES
    index = lax.axis_index("seq")
    first_pos = index * row_count

    last_pos = jnp.full((1, row_count), first_pos + row_count - 1, jnp.int32)
    last_start = start_at(docs_ref, doc_count, last_pos)
    lanes = lax.broadcasted_iota(jnp.int32, (1, row_count), 1)
    lanes_pos = first_pos + (lanes & -LANES) + row_at(lanes & (LANES - 1))
    keep = jnp.where(lanes_pos >= last_start, 1.0, 0.0).astype(jnp.bfloat16)

    def pair(step, carry):
        for which in range(heads):
            first = (step * heads + which) * LANES
            fill_window(
                window_ref.at[2 * which],
                rim_ref[:, columns(width + first)],
                key_ref[:, columns(first)],
            )
            fill_window(
                window_ref.at[2 * which + 1],
                rim_ref[:, columns(2 * width + first)],
                value_ref[:, columns(first)],
            )

        def body(tile, masked):
            places = slice(tile * LANES, (tile + 1) * LANES)
            distance = distance_ref[places, :] if masked else None
            for which in range(heads):
                head = step * heads + which
                first = head * LANES
                key_taps = taps_ref[:, columns(width + first)]
                value_taps = taps_ref[:, columns(2 * width + first)]
                grown = silu(convolved(window_ref.at[2 * which], key_taps, tile, distance))
                square = jnp.sum(grown * grown, axis=1, keepdims=True)
                keys = (grown * lax.rsqrt(square + 1e-6)).astype(jnp.bfloat16)
                key_out_ref[head, places, :] = keys
                values = silu(convolved(window_ref.at[2 * which + 1], value_taps, tile, distance))
                value_out_ref[head, :, places] = values.T.astype(jnp.bfloat16)

        per_tile(flag_ref, tiles, body)
        for which in range(heads):
            head = step * heads + which
            place = logical_place(head, index & 1, (index >> 1) & 1)
            state_ref[place] = jnp.dot(
                value_out_ref[head] * keep, key_out_ref[head], preferred_element_type=jnp.float32
            ).astype(jnp.bfloat16)
        return carry

    lax.fori_loop(0, steps, pair, 0)


def join_kernel(docs_ref, mine_ref, theirs_ref, *out_refs, doc_count, row_count, bit, parts):
    index = lax.axis_index("seq")
    stride = 1 << bit
    upper_first = (((index >> (bit + 1)) << (bit + 1)) + stride) * row_count

    def step(i, found):
        gap = docs_ref[i] - upper_first
        return jnp.where((gap >= 0) & (gap < stride * row_count), 1, found)

    upper_has = lax.fori_loop(0, doc_count, step, jnp.int32(0))
    is_upper = (index >> bit) & 1
    keep_mine = jnp.where((upper_has == 1) & (is_upper == 0), 0.0, 1.0)
    keep_theirs = jnp.where((upper_has == 1) & (is_upper == 1), 0.0, 1.0)
    skip = theirs_ref.shape[0] // 2 if parts == 2 else 0
    count = out_refs[0].shape[0]
    for part, out_ref in enumerate(out_refs):
        mine = mine_ref[part * count : (part + 1) * count].astype(jnp.float32)
        theirs = theirs_ref[skip + part * count : skip + (part + 1) * count].astype(jnp.float32)
        out_ref[...] = (mine * keep_mine + theirs * keep_theirs).astype(jnp.bfloat16)


def near_kernel(
    flag_ref,
    query_ref,
    rim_ref,
    taps_ref,
    distance_ref,
    table_ref,
    start_ref,
    key_ref,
    value_ref,
    *rest,
    first_head,
    head_count,
    heads,
    skipped,
):
    query_out_ref, near_ref, window_ref, fine_ref, pair_ref = rest[skipped:]
    row_count = query_ref.shape[0]
    tiles = row_count // LANES
    span = 2 * LANES
    sub = lax.broadcasted_iota(jnp.int32, (8, row_count), 0)
    lane = lax.broadcasted_iota(jnp.int32, (8, row_count), 1)
    high = sub ^ (lane & 7)
    sub16 = lax.broadcasted_iota(jnp.int32, (16, row_count), 0)
    low_row = (lax.broadcasted_iota(jnp.int32, (16, row_count), 1) >> 3) & 15
    low = sub16 ^ low_row
    same_group = lax.broadcasted_iota(jnp.int32, (8, LANES), 0) == (
        lax.broadcasted_iota(jnp.int32, (8, LANES), 1) & 7
    )
    key_row = row_at(lax.broadcasted_iota(jnp.int32, (LANES, LANES), 0))

    def group(step, carry):
        for which in range(heads):
            head = first_head + step * heads + which
            fill_window(
                window_ref.at[which],
                rim_ref[:, columns(head * LANES)],
                query_ref[:, columns(head * LANES)],
            )

        def body(tile, masked):
            places = slice(tile * LANES, (tile + 1) * LANES)
            distance = distance_ref[places, :] if masked else None
            for which in range(heads):
                head = first_head + step * heads + which
                taps = taps_ref[:, columns(head * LANES)]
                grown = silu(convolved(window_ref.at[which], taps, tile, distance))
                query_out_ref[head, places, :] = grown.astype(jnp.bfloat16)

        per_tile(flag_ref, tiles, body)

        for which in range(heads):
            head = first_head + step * heads + which
            tok_bits = row_count.bit_length() - 1
            scaled = [table_ref[level, pl.ds(head, 1), :] for level in range(tok_bits + 1)]
            coarse = jnp.where(high < 2, scaled[5], jnp.where(high < 4, scaled[6], scaled[7]))
            coarse = jnp.where(sub > (lane & 7), 0.0, coarse)
            fine = jnp.where(
                low == 0,
                scaled[0],
                jnp.where(
                    low == 1,
                    scaled[1],
                    jnp.where(low < 4, scaled[2], jnp.where(low < 8, scaled[3], scaled[4])),
                ),
            )
            fine = jnp.where(sub16 > low_row, 0.0, fine)
            for tile in range(tiles):
                fine_ref[which, tile] = fine[:, tile * LANES : (tile + 1) * LANES]
            for part in range(row_count // span):
                rows = (part + 1) * span
                scores = lax.dot_general(
                    key_ref[head, 0:rows, :],
                    query_out_ref[head, part * span : rows, :],
                    NT,
                    preferred_element_type=jnp.float32,
                )
                for side in range(2):
                    tile = 2 * part + side
                    cols = slice(tile * LANES, (tile + 1) * LANES)
                    starts = start_ref[0:1, cols]
                    for other in range(tile + 1):
                        if other == tile:
                            weight = jnp.concatenate(
                                [
                                    jnp.where(
                                        same_group,
                                        fine_ref[which, tile, pl.ds(a, 8, stride=0), :],
                                        coarse[:, cols],
                                    )
                                    for a in range(16)
                                ],
                                axis=0,
                            )
                        else:
                            weight = scaled[7 + (tile ^ other).bit_length()][:, cols]
                        piece = scores[
                            other * LANES : (other + 1) * LANES,
                            side * LANES : (side + 1) * LANES,
                        ]
                        valid = key_row >= starts - other * LANES
                        pair_ref[which, other * LANES : (other + 1) * LANES, cols] = jnp.where(
                            valid, piece * weight, 0.0
                        ).astype(jnp.bfloat16)
                    if side == 0:
                        pair_ref[which, (tile + 1) * LANES : rows, cols] = jnp.zeros(
                            (LANES, LANES), jnp.bfloat16
                        )
                near_ref[head, :, part * span : rows] = jnp.dot(
                    value_ref[head, :, 0:rows],
                    pair_ref[which, 0:rows, part * span : rows],
                    preferred_element_type=jnp.float32,
                )
        return carry

    lax.fori_loop(0, head_count // heads, group, 0)


def far_kernel(
    query_ref,
    near_ref,
    table_ref,
    first_state_ref,
    own_state_ref,
    other_state_ref,
    gain_ref,
    out_hbm_ref,
    out_buffer,
    sems,
    *,
    dev_bits,
    heads,
):
    head_count, row_count, _ = query_ref.shape
    tiles = row_count // LANES
    steps = head_count // heads
    wide = heads * LANES
    index = lax.axis_index("seq")
    core_bit = index & 1
    y_bit = (index >> 1) & 1
    tok_bits = row_count.bit_length() - 1
    select = selection(0, 1)

    def copy(step):
        cols = pl.ds(pl.multiple_of(step * wide, wide), wide)
        return pltpu.make_async_copy(
            out_buffer.at[:, cols], out_hbm_ref.at[:, cols], sems.at[step]
        )

    def group(step, carry):
        for which in range(heads):
            head = step * heads + which
            first_place = logical_place(head, 1 - core_bit, y_bit)
            place = logical_place(head, core_bit, y_bit)
            is_own = place < 8
            states = [first_state_ref[first_place]]
            for level in range(dev_bits - 1):
                states.append(
                    jnp.where(
                        is_own, own_state_ref[level, place & 7], other_state_ref[level, place & 7]
                    )
                )
            images = lax.dot_general(
                jnp.concatenate(states, axis=0),
                query_ref[head],
                NT,
                preferred_element_type=jnp.float32,
            )
            summed = near_ref[head]
            for bit in range(dev_bits):
                coef = table_ref[tok_bits + 1 + bit, pl.ds(head, 1), :]
                summed = summed + coef * images[bit * LANES : (bit + 1) * LANES, :]
            mean = jnp.mean(summed * summed, axis=0, keepdims=True)
            normed = summed * lax.rsqrt(mean + 1e-6)
            gain = gain_ref[head]
            for tile in range(tiles):
                cols = slice(tile * LANES, (tile + 1) * LANES)
                done = (normed[:, cols] * gain).astype(jnp.bfloat16)
                turned = lax.dot_general(select, done, NT, preferred_element_type=jnp.float32)
                out_buffer[cols, columns(head * LANES)] = turned.astype(jnp.bfloat16)
        copy(step).start()
        return carry

    lax.fori_loop(0, steps, group, 0)
    for step in range(steps):
        copy(step).wait()


def local(query_in, key_in, value_in, conv_weight, level_weight, out_gain, doc_starts):
    row_count, width_all = query_in.shape
    head_count, level_count, _ = level_weight.shape
    head_size = width_all // head_count
    conv_width = conv_weight.shape[0]
    doc_count = doc_starts.shape[0]
    dev_index = lax.axis_index("seq")
    dev_count = lax.axis_size("seq")
    dev_bits = dev_count.bit_length() - 1
    rim_rows = conv_width - 1
    tiles = row_count // LANES
    smem = pl.BlockSpec(memory_space=pltpu.SMEM)
    vmem = pl.BlockSpec(memory_space=pltpu.VMEM)
    anywhere = pl.BlockSpec(memory_space=pl.ANY)

    tails = pl.pallas_call(
        rim_kernel,
        in_specs=[pl.BlockSpec(memory_space=pltpu.HBM)] * 3,
        out_specs=vmem,
        out_shape=pltpu.VMEM((rim_rows, 3 * width_all), query_in.dtype),
        scratch_shapes=[
            pltpu.VMEM((3, 16, width_all), query_in.dtype),
            pltpu.SemaphoreType.DMA((3,)),
        ],
        compiler_params=limited(1),
        name="rim",
    )(*(pltpu.with_memory_space_constraint(x, pltpu.HBM) for x in (query_in, key_in, value_in)))
    tails, docs = lax.optimization_barrier((tails, doc_starts))
    rims = exchange(tails, lambda i: i + 1 if i + 1 < dev_count else None)
    table, starts, distance, gains, flags = pl.pallas_call(
        functools.partial(tables_kernel, doc_count=doc_count),
        in_specs=[smem, vmem, vmem],
        out_specs=[vmem, vmem, vmem, vmem, smem],
        out_shape=[
            pltpu.VMEM((level_count, head_count, row_count), jnp.float32),
            pltpu.VMEM((8, row_count), jnp.int32),
            pltpu.VMEM((row_count, LANES), jnp.int32),
            pltpu.VMEM((head_count, head_size, LANES), jnp.float32),
            pltpu.SMEM((tiles,), jnp.int32),
        ],
        compiler_params=limited(4),
        name="tables",
    )(docs, jnp.transpose(level_weight, (1, 0, 2)), out_gain.reshape(head_count, 1, head_size))
    rims, table, starts, distance, gains, flags = lax.optimization_barrier(
        (rims, table, starts, distance, gains, flags)
    )

    heads = 2
    steps = head_count // heads
    keys, values_t, state = pl.pallas_call(
        functools.partial(key_value_kernel, doc_count=doc_count, heads=heads),
        in_specs=[smem, smem] + [vmem] * 5,
        out_specs=[vmem] * 3,
        out_shape=[
            pltpu.VMEM((head_count, row_count, head_size), jnp.bfloat16),
            pltpu.VMEM((head_count, head_size, row_count), jnp.bfloat16),
            pltpu.VMEM((head_count, head_size, head_size), jnp.bfloat16),
        ],
        scratch_shapes=[
            pltpu.VMEM((2 * heads, row_count + PAD, LANES), jnp.float32),
        ],
        compiler_params=limited(4),
        name="key_value",
    )(docs, flags, key_in, value_in, rims, conv_weight, distance)

    def joined(mine, theirs, bit, parts=1):
        count = mine.shape[0] // (2 if parts == 2 else 1)
        shape = (count // parts, head_size, head_size)
        return pl.pallas_call(
            functools.partial(
                join_kernel, doc_count=doc_count, row_count=row_count, bit=bit, parts=parts
            ),
            in_specs=[smem, vmem, vmem],
            out_specs=[vmem] * parts,
            out_shape=[pltpu.VMEM(shape, jnp.bfloat16)] * parts,
            compiler_params=limited(1),
            name="join",
        )(doc_starts, mine, theirs)

    buffers = None
    piece_heads = head_count // 4

    def near_piece(piece, buffers, flags):
        extra = [] if buffers is None else list(buffers)
        return pl.pallas_call(
            functools.partial(
                near_kernel,
                first_head=piece * piece_heads,
                head_count=piece_heads,
                heads=heads,
                skipped=len(extra),
            ),
            in_specs=[smem] + [vmem] * (8 + len(extra)),
            out_specs=[vmem] * 2,
            out_shape=[
                pltpu.VMEM((head_count, row_count, head_size), jnp.bfloat16),
                pltpu.VMEM((head_count, head_size, row_count), jnp.float32),
            ],
            scratch_shapes=[
                pltpu.VMEM((heads, row_count + PAD, LANES), jnp.float32),
                pltpu.VMEM((heads, tiles, 16, LANES), jnp.float32),
                pltpu.VMEM((heads, row_count, row_count), jnp.bfloat16),
            ],
            input_output_aliases={9: 0, 10: 1} if extra else {},
            compiler_params=limited(6),
            cost_estimate=pl.CostEstimate(
                flops=500_000_000, bytes_accessed=3_500_000, transcendentals=300_000
            ),
            name="near",
        )(flags, query_in, rims, conv_weight, distance, table, starts, keys, values_t, *extra)

    def covered(payload, send, piece, buffers):
        payload, tied = lax.optimization_barrier((payload, flags))
        arrived = send(payload)
        buffers = near_piece(piece, buffers, tied)
        arrived, buffers = lax.optimization_barrier((arrived, buffers))
        return arrived, buffers

    first_state = swapped(state, 0)
    pair_kept, pair_sent = joined(state, first_state, 0, parts=2)
    pair_in, buffers = covered(pair_sent, lambda x: swapped(x, 1), 0, buffers)
    (carried,) = joined(pair_kept, pair_in, 1)
    received = []
    for bit in range(2, dev_bits):
        last = bit == dev_bits - 1
        if last:
            arrived, buffers = covered(carried, lambda x: sent_up(x, bit), 2, buffers)
        elif bit == 2:
            arrived, buffers = covered(carried, lambda x: swapped(x, bit), 1, buffers)
        else:
            arrived = swapped(carried, bit)
        received.append(arrived)
        if not last:
            (carried,) = joined(carried, arrived, bit)

    mine = jnp.stack([pair_kept] + received)
    theirs, buffers = covered(mine, lambda x: swapped(x, 1), 3, buffers)
    queries, near = buffers
    own = jnp.concatenate(
        [jnp.concatenate([pair_in[None], mine[1:]], axis=0), theirs], axis=1
    )
    other = swapped(own, 0)

    return pl.pallas_call(
        functools.partial(far_kernel, dev_bits=dev_bits, heads=heads),
        in_specs=[vmem] * 7,
        out_specs=anywhere,
        out_shape=jax.ShapeDtypeStruct((row_count, width_all), jnp.bfloat16),
        scratch_shapes=[
            pltpu.VMEM((row_count, width_all), jnp.bfloat16),
            pltpu.SemaphoreType.DMA((steps,)),
        ],
        compiler_params=limited(8),
        name="far",
    )(queries, near, table, first_state, own, other, gains)


def solution(mesh):
    in_specs = (
        P(("groups", "seq"), None),
        P(("groups", "seq"), None),
        P(("groups", "seq"), None),
        P(),
        P(None, None, ("groups", "seq")),
        P(),
        P("groups"),
    )
    out_specs = P(("groups", "seq"), None)
    return jax.shard_map(local, mesh=mesh, in_specs=in_specs, out_specs=out_specs, check_vma=False)
```

```python
import functools

import jax
import jax.numpy as jnp
from jax import lax
from jax.experimental import pallas as pl
from jax.experimental.pallas import tpu as pltpu
from jax.sharding import PartitionSpec as P

LANES = 128
PAD = 8
NT = (((1,), (1,)), ((), ()))


def exchange(block, partner):
    count = lax.axis_size("seq")
    route = [(i, partner(i)) for i in range(count) if partner(i) is not None]
    return lax.ppermute(block, "seq", route)


def swapped(block, bit):
    return exchange(block, lambda i: i ^ (1 << bit))


def sent_up(block, bit):
    return exchange(block, lambda i: None if i >> bit & 1 else i | 1 << bit)


def limited(mebibytes):
    return pltpu.CompilerParams(vmem_limit_bytes=mebibytes * 1024 * 1024)


def start_at(docs_ref, doc_count, positions):
    def step(i, start):
        doc = docs_ref[i]
        return jnp.where(positions >= doc, doc, start)

    return lax.fori_loop(0, doc_count, step, jnp.zeros_like(positions))


def silu(values):
    return values * (0.5 + 0.5 * jnp.tanh(0.5 * values))


def logical_place(head, core_bit, y_bit):
    return ((head >> 3) ^ core_bit) * 8 + (((head >> 2) & 1) ^ y_bit) * 4 + (head & 3)


def row_at(place):
    return ((place & 7) << 4) | ((place >> 3) & 15)


def selection(row_of, place_of):
    shape = (LANES, LANES)
    rows = lax.broadcasted_iota(jnp.int32, shape, row_of)
    places = lax.broadcasted_iota(jnp.int32, shape, place_of)
    return jnp.where(rows == row_at(places), 1.0, 0.0).astype(jnp.bfloat16)


def rim_kernel(query_ref, key_ref, value_ref, out_ref, buffer, sems):
    rim_rows = out_ref.shape[0]
    edge, width = buffer.shape[1:]
    copies = []
    for part, ref in enumerate((query_ref, key_ref, value_ref)):
        rows = ref.shape[0]
        copy = pltpu.make_async_copy(
            ref.at[rows - edge : rows, :], buffer.at[part], sems.at[part]
        )
        copy.start()
        copies.append(copy)
    for part, copy in enumerate(copies):
        copy.wait()
        out_ref[:, part * width : (part + 1) * width] = buffer[part, edge - rim_rows : edge, :]


def tables_kernel(docs_ref, level_ref, gain_ref, table_ref, start_ref, gain_out_ref, *, doc_count):
    level_count, head_count, row_count = level_ref.shape
    tok_bits = row_count.bit_length() - 1
    index = lax.axis_index("seq")
    first_pos = index * row_count
    lanes = lax.broadcasted_iota(jnp.int32, (8, row_count), 1)
    positions = first_pos + (lanes & -LANES) + row_at(lanes & (LANES - 1))
    starts = start_at(docs_ref, doc_count, positions)
    start_ref[...] = starts - first_pos
    starts = jnp.concatenate([starts] * (head_count // 8), axis=0)
    select = selection(0, 1)
    levels = level_ref[...].reshape(level_count * head_count, row_count)
    for tile in range(row_count // LANES):
        cols = slice(tile * LANES, (tile + 1) * LANES)
        weights = jnp.dot(levels[:, cols], select, preferred_element_type=jnp.float32)
        for level in range(level_count):
            scaled = weights[level * head_count : (level + 1) * head_count] * 2.0 ** (-level / 2)
            if level > tok_bits:
                bit = level - tok_bits - 1
                limit = jnp.where((index >> bit) & 1 == 1, (index >> bit << bit) * row_count, 0)
                scaled = jnp.where(starts[:, cols] < limit, scaled, 0.0)
            table_ref[level, :, cols] = scaled
    for head in range(head_count):
        gain_out_ref[head] = jnp.broadcast_to(gain_ref[head], (LANES, LANES)).T


def fill_rim(window_ref, rim):
    rim_rows = rim.shape[0]
    window_ref[0:PAD, :] = jnp.concatenate(
        [jnp.zeros((PAD - rim_rows, rim.shape[1]), jnp.float32), rim.astype(jnp.float32)], axis=0
    )


def fill_rows(window_ref, rows, first):
    window_ref[PAD + first : PAD + first + rows.shape[0], :] = rows.astype(jnp.float32)


def convolved(window_ref, taps, tile, distance):
    reach = taps.shape[0] - 1
    rows = [
        window_ref[pl.ds(PAD + tile * LANES + i, 8, stride=16), :] for i in range(-reach, 16)
    ]
    summed = taps[0:1, :] * jnp.concatenate(rows[reach:], axis=0)
    for offset in range(1, reach + 1):
        term = taps[offset : offset + 1, :] * jnp.concatenate(
            rows[reach - offset : reach - offset + 16], axis=0
        )
        if distance is not None:
            term = jnp.where(distance >= offset, term, 0.0)
        summed = summed + term
    return summed


def per_tile(flag_ref, tiles, body):
    for tile in tiles:
        flagged = flag_ref[tile] == 1

        @pl.when(flagged)
        def _():
            body(tile, True)

        @pl.when(jnp.logical_not(flagged))
        def _():
            body(tile, False)


def columns(first):
    return pl.ds(pl.multiple_of(first, LANES), LANES)


def key_value_tile(
    rim_ref, taps_ref, distance_ref, key_out_ref, value_out_ref, window_ref, head, slot, tile, masked
):
    width = taps_ref.shape[1] // 3
    places = slice(tile * LANES, (tile + 1) * LANES)
    distance = distance_ref[places, :] if masked else None
    first = head * LANES
    key_taps = taps_ref[:, columns(width + first)]
    value_taps = taps_ref[:, columns(2 * width + first)]
    grown = silu(convolved(window_ref.at[slot], key_taps, tile, distance))
    square = jnp.sum(grown * grown, axis=1, keepdims=True)
    key_out_ref[head, places, :] = (grown * lax.rsqrt(square + 1e-6)).astype(jnp.bfloat16)
    values = silu(convolved(window_ref.at[slot + 1], value_taps, tile, distance))
    value_out_ref[head, :, places] = values.T.astype(jnp.bfloat16)


def kept_lanes(docs_ref, doc_count, first_pos, row_count, tiles):
    last_pos = jnp.full((1, len(tiles) * LANES), first_pos + row_count - 1, jnp.int32)
    last_start = start_at(docs_ref, doc_count, last_pos)
    lanes = tiles[0] * LANES + lax.broadcasted_iota(jnp.int32, last_pos.shape, 1)
    lanes_pos = first_pos + (lanes & -LANES) + row_at(lanes & (LANES - 1))
    return jnp.where(lanes_pos >= last_start, 1.0, 0.0).astype(jnp.bfloat16)


def later_rows_kernel(
    docs_ref,
    key_ref,
    value_ref,
    taps_ref,
    key_out_ref,
    value_out_ref,
    state_ref,
    distance_ref,
    flag_ref,
    window_ref,
    *,
    doc_count,
    heads,
):
    row_count, width = key_ref.shape
    head_count = width // LANES
    tiles = list(range(1, row_count // LANES))
    first_pos = lax.axis_index("seq") * row_count
    keep = kept_lanes(docs_ref, doc_count, first_pos, row_count, tiles)
    places = lax.broadcasted_iota(jnp.int32, (row_count, LANES), 0)
    positions = first_pos + (places & -LANES) + row_at(places & (LANES - 1))
    distance_ref[...] = positions - start_at(docs_ref, doc_count, positions)
    for tile in range(row_count // LANES):
        tile_first = first_pos + tile * LANES

        def step(i, flag):
            gap = docs_ref[i] - tile_first
            return jnp.where((gap > -8) & (gap < LANES), 1, flag)

        flag_ref[tile] = lax.fori_loop(0, doc_count, step, jnp.int32(0))
    ahead = LANES - 16

    def group(step, carry):
        for which in range(heads):
            cols = columns((step * heads + which) * LANES)
            fill_rows(window_ref.at[2 * which], key_ref[ahead:, cols], ahead)
            fill_rows(window_ref.at[2 * which + 1], value_ref[ahead:, cols], ahead)

        def body(tile, masked):
            for which in range(heads):
                key_value_tile(
                    None,
                    taps_ref,
                    distance_ref,
                    key_out_ref,
                    value_out_ref,
                    window_ref,
                    step * heads + which,
                    2 * which,
                    tile,
                    masked,
                )

        per_tile(flag_ref, tiles, body)
        for which in range(heads):
            head = step * heads + which
            state_ref[head] = jnp.dot(
                value_out_ref[head, :, LANES:] * keep,
                key_out_ref[head, LANES:, :],
                preferred_element_type=jnp.float32,
            )
        return carry

    lax.fori_loop(0, head_count // heads, group, 0)


def first_rows_kernel(
    docs_ref,
    flag_ref,
    key_ref,
    value_ref,
    taps_ref,
    rim_ref,
    distance_ref,
    later_state_ref,
    key_in_ref,
    value_in_ref,
    key_out_ref,
    value_out_ref,
    state_ref,
    window_ref,
    *,
    doc_count,
    row_count,
    heads,
):
    width = key_ref.shape[1]
    head_count = width // LANES
    index = lax.axis_index("seq")
    keep = kept_lanes(docs_ref, doc_count, index * row_count, row_count, [0])

    def group(step, carry):
        for which in range(heads):
            first = (step * heads + which) * LANES
            fill_rim(window_ref.at[2 * which], rim_ref[:, columns(width + first)])
            fill_rim(window_ref.at[2 * which + 1], rim_ref[:, columns(2 * width + first)])
            fill_rows(window_ref.at[2 * which], key_ref[0:LANES, columns(first)], 0)
            fill_rows(window_ref.at[2 * which + 1], value_ref[0:LANES, columns(first)], 0)

        def body(tile, masked):
            for which in range(heads):
                key_value_tile(
                    rim_ref,
                    taps_ref,
                    distance_ref,
                    key_out_ref,
                    value_out_ref,
                    window_ref,
                    step * heads + which,
                    2 * which,
                    tile,
                    masked,
                )

        per_tile(flag_ref, [0], body)
        for which in range(heads):
            head = step * heads + which
            total = later_state_ref[head] + jnp.dot(
                value_out_ref[head, :, 0:LANES] * keep,
                key_out_ref[head, 0:LANES, :],
                preferred_element_type=jnp.float32,
            )
            place = logical_place(head, index & 1, (index >> 1) & 1)
            state_ref[place] = total.astype(jnp.bfloat16)
        return carry

    lax.fori_loop(0, head_count // heads, group, 0)


def join_kernel(docs_ref, mine_ref, theirs_ref, *out_refs, doc_count, row_count, bit, parts):
    index = lax.axis_index("seq")
    stride = 1 << bit
    upper_first = (((index >> (bit + 1)) << (bit + 1)) + stride) * row_count

    def step(i, found):
        gap = docs_ref[i] - upper_first
        return jnp.where((gap >= 0) & (gap < stride * row_count), 1, found)

    upper_has = lax.fori_loop(0, doc_count, step, jnp.int32(0))
    is_upper = (index >> bit) & 1
    keep_mine = jnp.where((upper_has == 1) & (is_upper == 0), 0.0, 1.0)
    keep_theirs = jnp.where((upper_has == 1) & (is_upper == 1), 0.0, 1.0)
    skip = theirs_ref.shape[0] // 2 if parts == 2 else 0
    count = out_refs[0].shape[0]
    for part, out_ref in enumerate(out_refs):
        mine = mine_ref[part * count : (part + 1) * count].astype(jnp.float32)
        theirs = theirs_ref[skip + part * count : skip + (part + 1) * count].astype(jnp.float32)
        out_ref[...] = (mine * keep_mine + theirs * keep_theirs).astype(jnp.bfloat16)


def near_kernel(
    flag_ref,
    query_ref,
    rim_ref,
    taps_ref,
    distance_ref,
    table_ref,
    start_ref,
    key_ref,
    value_ref,
    *rest,
    first_head,
    head_count,
    heads,
    skipped,
):
    query_out_ref, near_ref, window_ref, fine_ref, pair_ref = rest[skipped:]
    row_count = query_ref.shape[0]
    tiles = row_count // LANES
    span = 2 * LANES
    sub = lax.broadcasted_iota(jnp.int32, (8, row_count), 0)
    lane = lax.broadcasted_iota(jnp.int32, (8, row_count), 1)
    high = sub ^ (lane & 7)
    sub16 = lax.broadcasted_iota(jnp.int32, (16, row_count), 0)
    low_row = (lax.broadcasted_iota(jnp.int32, (16, row_count), 1) >> 3) & 15
    low = sub16 ^ low_row
    same_group = lax.broadcasted_iota(jnp.int32, (8, LANES), 0) == (
        lax.broadcasted_iota(jnp.int32, (8, LANES), 1) & 7
    )
    key_row = row_at(lax.broadcasted_iota(jnp.int32, (LANES, LANES), 0))

    def group(step, carry):
        for which in range(heads):
            head = first_head + step * heads + which
            fill_rim(window_ref.at[which], rim_ref[:, columns(head * LANES)])
            fill_rows(window_ref.at[which], query_ref[:, columns(head * LANES)], 0)

        def body(tile, masked):
            places = slice(tile * LANES, (tile + 1) * LANES)
            distance = distance_ref[places, :] if masked else None
            for which in range(heads):
                head = first_head + step * heads + which
                taps = taps_ref[:, columns(head * LANES)]
                grown = silu(convolved(window_ref.at[which], taps, tile, distance))
                query_out_ref[head, places, :] = grown.astype(jnp.bfloat16)

        per_tile(flag_ref, range(tiles), body)

        for which in range(heads):
            head = first_head + step * heads + which
            tok_bits = row_count.bit_length() - 1
            scaled = [table_ref[level, pl.ds(head, 1), :] for level in range(tok_bits + 1)]
            coarse = jnp.where(high < 2, scaled[5], jnp.where(high < 4, scaled[6], scaled[7]))
            coarse = jnp.where(sub > (lane & 7), 0.0, coarse)
            fine = jnp.where(
                low == 0,
                scaled[0],
                jnp.where(
                    low == 1,
                    scaled[1],
                    jnp.where(low < 4, scaled[2], jnp.where(low < 8, scaled[3], scaled[4])),
                ),
            )
            fine = jnp.where(sub16 > low_row, 0.0, fine)
            for tile in range(tiles):
                fine_ref[which, tile] = fine[:, tile * LANES : (tile + 1) * LANES]
            for part in range(row_count // span):
                rows = (part + 1) * span
                scores = lax.dot_general(
                    key_ref[head, 0:rows, :],
                    query_out_ref[head, part * span : rows, :],
                    NT,
                    preferred_element_type=jnp.float32,
                )
                for side in range(2):
                    tile = 2 * part + side
                    cols = slice(tile * LANES, (tile + 1) * LANES)
                    starts = start_ref[0:1, cols]
                    for other in range(tile + 1):
                        if other == tile:
                            weight = jnp.concatenate(
                                [
                                    jnp.where(
                                        same_group,
                                        fine_ref[which, tile, pl.ds(a, 8, stride=0), :],
                                        coarse[:, cols],
                                    )
                                    for a in range(16)
                                ],
                                axis=0,
                            )
                        else:
                            weight = scaled[7 + (tile ^ other).bit_length()][:, cols]
                        piece = scores[
                            other * LANES : (other + 1) * LANES,
                            side * LANES : (side + 1) * LANES,
                        ]
                        valid = key_row >= starts - other * LANES
                        pair_ref[which, other * LANES : (other + 1) * LANES, cols] = jnp.where(
                            valid, piece * weight, 0.0
                        ).astype(jnp.bfloat16)
                    if side == 0:
                        pair_ref[which, (tile + 1) * LANES : rows, cols] = jnp.zeros(
                            (LANES, LANES), jnp.bfloat16
                        )
                near_ref[head, :, part * span : rows] = jnp.dot(
                    value_ref[head, :, 0:rows],
                    pair_ref[which, 0:rows, part * span : rows],
                    preferred_element_type=jnp.float32,
                )
        return carry

    lax.fori_loop(0, head_count // heads, group, 0)


def far_kernel(
    query_ref,
    near_ref,
    table_ref,
    gain_ref,
    first_state_ref,
    lower_ref,
    *rest,
    groups,
    dev_bits,
    heads,
    skipped,
):
    last_refs = rest[: len(groups)]
    out_hbm_ref, out_buffer, sems = rest[len(groups) + skipped :]
    head_count, row_count, _ = query_ref.shape
    tiles = row_count // LANES
    quarter = head_count // 4
    index = lax.axis_index("seq")
    core_bit = index & 1
    y_bit = (index >> 1) & 1
    tok_bits = row_count.bit_length() - 1
    select = selection(0, 1)
    copies = []
    for group, (last_ref, (other_half, other_quarter)) in enumerate(zip(last_refs, groups)):
        first_head = (core_bit ^ other_half) * 2 * quarter + (y_bit ^ other_quarter) * quarter

        def body(step, carry):
            for which in range(heads):
                local_head = step * heads + which
                head = first_head + local_head
                first_place = logical_place(head, 1 - core_bit, y_bit)
                place = logical_place(head, core_bit, y_bit) & 7
                states = [first_state_ref[first_place]]
                for level in range(dev_bits - 2):
                    states.append(lower_ref[level, place])
                states.append(last_ref[local_head])
                images = lax.dot_general(
                    jnp.concatenate(states, axis=0),
                    query_ref[head],
                    NT,
                    preferred_element_type=jnp.float32,
                )
                summed = near_ref[head]
                for bit in range(dev_bits):
                    coef = table_ref[tok_bits + 1 + bit, pl.ds(head, 1), :]
                    summed = summed + coef * images[bit * LANES : (bit + 1) * LANES, :]
                mean = jnp.mean(summed * summed, axis=0, keepdims=True)
                normed = summed * lax.rsqrt(mean + 1e-6)
                gain = gain_ref[head]
                for tile in range(tiles):
                    cols = slice(tile * LANES, (tile + 1) * LANES)
                    done = (normed[:, cols] * gain).astype(jnp.bfloat16)
                    turned = lax.dot_general(select, done, NT, preferred_element_type=jnp.float32)
                    out_buffer[group, cols, columns(local_head * LANES)] = turned.astype(
                        jnp.bfloat16
                    )
            return carry

        lax.fori_loop(0, quarter // heads, body, 0)
        wide = quarter * LANES
        cols = pl.ds(pl.multiple_of(first_head * LANES, wide), wide)
        copy = pltpu.make_async_copy(out_buffer.at[group], out_hbm_ref.at[:, cols], sems.at[group])
        copy.start()
        copies.append(copy)
    for copy in copies:
        copy.wait()


def local(query_in, key_in, value_in, conv_weight, level_weight, out_gain, doc_starts):
    row_count, width_all = query_in.shape
    head_count, level_count, _ = level_weight.shape
    head_size = width_all // head_count
    conv_width = conv_weight.shape[0]
    doc_count = doc_starts.shape[0]
    dev_index = lax.axis_index("seq")
    dev_count = lax.axis_size("seq")
    dev_bits = dev_count.bit_length() - 1
    rim_rows = conv_width - 1
    tiles = row_count // LANES
    smem = pl.BlockSpec(memory_space=pltpu.SMEM)
    vmem = pl.BlockSpec(memory_space=pltpu.VMEM)
    anywhere = pl.BlockSpec(memory_space=pl.ANY)

    tails = pl.pallas_call(
        rim_kernel,
        in_specs=[pl.BlockSpec(memory_space=pltpu.HBM)] * 3,
        out_specs=vmem,
        out_shape=pltpu.VMEM((rim_rows, 3 * width_all), query_in.dtype),
        scratch_shapes=[
            pltpu.VMEM((3, 16, width_all), query_in.dtype),
            pltpu.SemaphoreType.DMA((3,)),
        ],
        compiler_params=limited(1),
        name="rim",
    )(*(pltpu.with_memory_space_constraint(x, pltpu.HBM) for x in (query_in, key_in, value_in)))
    tails, docs = lax.optimization_barrier((tails, doc_starts))
    rims = exchange(tails, lambda i: i + 1 if i + 1 < dev_count else None)
    heads = 2
    keys, values_t, later_state, distance, flags = pl.pallas_call(
        functools.partial(later_rows_kernel, doc_count=doc_count, heads=heads),
        in_specs=[smem] + [vmem] * 3,
        out_specs=[vmem] * 4 + [smem],
        out_shape=[
            pltpu.VMEM((head_count, row_count, head_size), jnp.bfloat16),
            pltpu.VMEM((head_count, head_size, row_count), jnp.bfloat16),
            pltpu.VMEM((head_count, head_size, head_size), jnp.float32),
            pltpu.VMEM((row_count, LANES), jnp.int32),
            pltpu.SMEM((tiles,), jnp.int32),
        ],
        scratch_shapes=[pltpu.VMEM((2 * heads, row_count + PAD, LANES), jnp.float32)],
        compiler_params=limited(3),
        cost_estimate=pl.CostEstimate(
            flops=500_000_000, bytes_accessed=4_000_000, transcendentals=1_500_000
        ),
        name="later_rows",
    )(docs, key_in, value_in, conv_weight)
    rims, keys, values_t, later_state, flags = lax.optimization_barrier(
        (rims, keys, values_t, later_state, flags)
    )
    keys, values_t, state = pl.pallas_call(
        functools.partial(
            first_rows_kernel, doc_count=doc_count, row_count=row_count, heads=heads
        ),
        in_specs=[smem, smem] + [vmem] * 8,
        out_specs=[vmem] * 3,
        out_shape=[
            pltpu.VMEM((head_count, row_count, head_size), jnp.bfloat16),
            pltpu.VMEM((head_count, head_size, row_count), jnp.bfloat16),
            pltpu.VMEM((head_count, head_size, head_size), jnp.bfloat16),
        ],
        scratch_shapes=[pltpu.VMEM((2 * heads, LANES + PAD, LANES), jnp.float32)],
        input_output_aliases={8: 0, 9: 1},
        compiler_params=limited(2),
        name="first_rows",
    )(docs, flags, key_in, value_in, conv_weight, rims, distance, later_state, keys, values_t)

    def joined(mine, theirs, bit, parts=1):
        count = mine.shape[0] // (2 if parts == 2 else 1)
        shape = (count // parts, head_size, head_size)
        return pl.pallas_call(
            functools.partial(
                join_kernel, doc_count=doc_count, row_count=row_count, bit=bit, parts=parts
            ),
            in_specs=[smem, vmem, vmem],
            out_specs=[vmem] * parts,
            out_shape=[pltpu.VMEM(shape, jnp.bfloat16)] * parts,
            compiler_params=limited(1),
            name="join",
        )(doc_starts, mine, theirs)

    def near_piece(first_head, piece_heads, buffers, flags):
        extra = [] if buffers is None else list(buffers)
        return pl.pallas_call(
            functools.partial(
                near_kernel,
                first_head=first_head,
                head_count=piece_heads,
                heads=heads,
                skipped=len(extra),
            ),
            in_specs=[smem] + [vmem] * (8 + len(extra)),
            out_specs=[vmem] * 2,
            out_shape=[
                pltpu.VMEM((head_count, row_count, head_size), jnp.bfloat16),
                pltpu.VMEM((head_count, head_size, row_count), jnp.float32),
            ],
            scratch_shapes=[
                pltpu.VMEM((heads, row_count + PAD, LANES), jnp.float32),
                pltpu.VMEM((heads, tiles, 16, LANES), jnp.float32),
                pltpu.VMEM((heads, row_count, row_count), jnp.bfloat16),
            ],
            input_output_aliases={9: 0, 10: 1} if extra else {},
            compiler_params=limited(6),
            cost_estimate=pl.CostEstimate(
                flops=1_000_000, bytes_accessed=10_000, transcendentals=0
            ),
            name="near",
        )(flags, query_in, rims, conv_weight, distance, table, starts, keys, values_t, *extra)

    def far_piece(groups, lower, last_states, out):
        extra = [] if out is None else [out]
        return pl.pallas_call(
            functools.partial(
                far_kernel, groups=groups, dev_bits=dev_bits, heads=heads, skipped=len(extra)
            ),
            in_specs=[vmem] * (6 + len(groups)) + [anywhere] * len(extra),
            out_specs=anywhere,
            out_shape=jax.ShapeDtypeStruct((row_count, width_all), jnp.bfloat16),
            scratch_shapes=[
                pltpu.VMEM((len(groups), row_count, quarter * head_size), jnp.bfloat16),
                pltpu.SemaphoreType.DMA((len(groups),)),
            ],
            input_output_aliases={6 + len(groups): 0} if extra else {},
            compiler_params=limited(4),
            cost_estimate=pl.CostEstimate(
                flops=1_000_000, bytes_accessed=10_000, transcendentals=0
            ),
            name="far",
        )(queries, near, table, gains, first_state, lower, *last_states, *extra)

    quarter = head_count // 4
    state, docs = lax.optimization_barrier((state, docs))
    first_state = swapped(state, 0)
    table, starts, gains = pl.pallas_call(
        functools.partial(tables_kernel, doc_count=doc_count),
        in_specs=[smem, vmem, vmem],
        out_specs=[vmem] * 3,
        out_shape=[
            pltpu.VMEM((level_count, head_count, row_count), jnp.float32),
            pltpu.VMEM((8, row_count), jnp.int32),
            pltpu.VMEM((head_count, head_size, LANES), jnp.float32),
        ],
        compiler_params=limited(2),
        name="tables",
    )(docs, jnp.transpose(level_weight, (1, 0, 2)), out_gain.reshape(head_count, 1, head_size))
    first_state, table, starts, gains = lax.optimization_barrier(
        (first_state, table, starts, gains)
    )
    pair_kept, pair_sent = joined(state, first_state, 0, parts=2)

    pair_sent, tied = lax.optimization_barrier((pair_sent, flags))
    pair_in = swapped(pair_sent, 1)
    buffers = near_piece(0, quarter, None, tied)
    pair_in, buffers = lax.optimization_barrier((pair_in, buffers))
    (carried,) = joined(pair_kept, pair_in, 1)

    received = []
    for bit in range(2, dev_bits - 1):
        if bit == 2:
            carried, tied = lax.optimization_barrier((carried, flags))
        arrived = swapped(carried, bit)
        if bit == 2:
            buffers = near_piece(quarter, quarter, buffers, tied)
            arrived, buffers = lax.optimization_barrier((arrived, buffers))
        received.append(arrived)
        (carried,) = joined(carried, arrived, bit)

    mine = jnp.stack([pair_kept] + received)
    carried, mine, tied = lax.optimization_barrier((carried, mine, flags))
    last_own = sent_up(carried, dev_bits - 1)
    theirs = swapped(mine, 1)
    buffers = near_piece(2 * quarter, 2 * quarter, buffers, tied)
    last_own, theirs, buffers = lax.optimization_barrier((last_own, theirs, buffers))
    queries, near = buffers
    own = jnp.concatenate([jnp.stack([pair_in] + received), theirs], axis=1)
    own, last_own = lax.optimization_barrier((own, last_own))

    last_next = swapped(last_own, 1)
    other = swapped(own, 0)
    last_other = swapped(last_own, 0)
    out = far_piece(((0, 0),), own, (last_own,), None)
    other, last_other, out = lax.optimization_barrier((other, last_other, out))
    out = far_piece(((1, 0),), other, (last_other,), out)
    last_next, out = lax.optimization_barrier((last_next, out))
    last_far = swapped(last_next, 0)
    out = far_piece(((0, 1),), own, (last_next,), out)
    last_far, out = lax.optimization_barrier((last_far, out))
    return far_piece(((1, 1),), other, (last_far,), out)


def solution(mesh):
    in_specs = (
        P(("groups", "seq"), None),
        P(("groups", "seq"), None),
        P(("groups", "seq"), None),
        P(),
        P(None, None, ("groups", "seq")),
        P(),
        P("groups"),
    )
    out_specs = P(("groups", "seq"), None)
    return jax.shard_map(local, mesh=mesh, in_specs=in_specs, out_specs=out_specs, check_vma=False)
```

```python
import functools

import jax
import jax.numpy as jnp
from jax import lax
from jax.experimental import pallas as pl
from jax.experimental.pallas import tpu as pltpu
from jax.sharding import PartitionSpec as P

LANES = 128
GROUP = 16
PITCH = 24
NT = (((1,), (1,)), ((), ()))


def exchange(block, partner):
    count = lax.axis_size("seq")
    route = [(i, partner(i)) for i in range(count) if partner(i) is not None]
    return lax.ppermute(block, "seq", route)


def swapped(block, bit):
    return exchange(block, lambda i: i ^ (1 << bit))


def sent_up(block, bit):
    return exchange(block, lambda i: None if i >> bit & 1 else i | 1 << bit)


def limited(mebibytes):
    return pltpu.CompilerParams(vmem_limit_bytes=mebibytes * 1024 * 1024)


def start_at(docs_ref, doc_count, positions):
    def step(i, start):
        doc = docs_ref[i]
        return jnp.where(positions >= doc, doc, start)

    return lax.fori_loop(0, doc_count, step, jnp.zeros_like(positions))


def silu(values):
    return values * (0.5 + 0.5 * jnp.tanh(0.5 * values))


def logical_place(head, core_bit, y_bit):
    return ((head >> 3) ^ core_bit) * 8 + (((head >> 2) & 1) ^ y_bit) * 4 + (head & 3)


def row_at(place):
    return ((place & 7) << 4) | ((place >> 3) & 15)


def selection(size):
    rows = lax.broadcasted_iota(jnp.int32, (size, size), 0)
    places = lax.broadcasted_iota(jnp.int32, (size, size), 1)
    chosen = rows == (places & -LANES) + row_at(places & (LANES - 1))
    return jnp.where(chosen, 1.0, 0.0).astype(jnp.bfloat16)


def rim_kernel(query_ref, key_ref, value_ref, out_ref, buffer, sems):
    rim_rows = out_ref.shape[0]
    edge, width = buffer.shape[1:]
    copies = []
    for part, ref in enumerate((query_ref, key_ref, value_ref)):
        rows = ref.shape[0]
        copy = pltpu.make_async_copy(
            ref.at[rows - edge : rows, :], buffer.at[part], sems.at[part]
        )
        copy.start()
        copies.append(copy)
    for part, copy in enumerate(copies):
        copy.wait()
        out_ref[:, part * width : (part + 1) * width] = buffer[part, edge - rim_rows : edge, :]


def tables_kernel(docs_ref, level_ref, gain_ref, table_ref, start_ref, gain_out_ref, *, doc_count):
    level_count, head_count, row_count = level_ref.shape
    tok_bits = row_count.bit_length() - 1
    index = lax.axis_index("seq")
    first_pos = index * row_count
    lanes = lax.broadcasted_iota(jnp.int32, (8, row_count), 1)
    positions = first_pos + (lanes & -LANES) + row_at(lanes & (LANES - 1))
    starts = start_at(docs_ref, doc_count, positions)
    start_ref[...] = starts - first_pos
    starts = jnp.concatenate([starts] * (head_count // 8), axis=0)
    select = selection(LANES)
    levels = level_ref[...].reshape(level_count * head_count, row_count)
    for tile in range(row_count // LANES):
        cols = slice(tile * LANES, (tile + 1) * LANES)
        weights = jnp.dot(levels[:, cols], select, preferred_element_type=jnp.float32)
        for level in range(level_count):
            scaled = weights[level * head_count : (level + 1) * head_count] * 2.0 ** (-level / 2)
            if level > tok_bits:
                bit = level - tok_bits - 1
                limit = jnp.where((index >> bit) & 1 == 1, (index >> bit << bit) * row_count, 0)
                scaled = jnp.where(starts[:, cols] < limit, scaled, 0.0)
            table_ref[level, :, cols] = scaled
    for head in range(head_count):
        gain_out_ref[head] = jnp.broadcast_to(gain_ref[head], (LANES, LANES)).T


def window_rows(row_count):
    return (row_count // GROUP + 1) * PITCH


def fill_rim(window_ref, rim):
    rim_rows = rim.shape[0]
    window_ref[GROUP - 8 : GROUP, :] = jnp.concatenate(
        [jnp.zeros((8 - rim_rows, rim.shape[1]), jnp.float32), rim.astype(jnp.float32)], axis=0
    )


def fill_rows(window_ref, rows, first):
    rows = rows.astype(jnp.float32)
    for start in range(0, rows.shape[0], GROUP):
        place = ((first + start) // GROUP + 1) * PITCH
        window_ref[place : place + GROUP, :] = rows[start : start + GROUP, :]


def convolved(window_ref, taps, inside_ref, tile):
    reach = taps.shape[0] - 1
    base = (tile * (LANES // GROUP) + 1) * PITCH
    places = [base - PITCH + GROUP + i for i in range(-reach, 0)]
    places += [base + i for i in range(GROUP)]
    rows = [window_ref[pl.ds(place, 8, stride=PITCH), :] for place in places]
    summed = None
    for offset in range(reach, -1, -1):
        term = taps[offset : offset + 1, :] * jnp.concatenate(
            rows[reach - offset : reach - offset + 16], axis=0
        )
        summed = term if summed is None else term + summed
        if offset:
            first = (reach - offset) * 8
            summed = summed * inside_ref[tile, first : first + LANES, :]
    return summed


def inside_masks(docs_ref, doc_count, first_pos, inside_ref):
    tiles, places, _ = inside_ref.shape
    ahead = (places - LANES) // 8
    place = lax.broadcasted_iota(jnp.int32, (places, LANES), 0)
    rows = ((place & 7) << 4) + (place >> 3) - ahead
    for tile in range(tiles):
        positions = rows + (first_pos + tile * LANES)

        def step(i, inside):
            return jnp.where(positions == docs_ref[i], 0.0, inside)

        inside_ref[tile] = lax.fori_loop(
            0, doc_count, step, jnp.ones((places, LANES), jnp.float32), unroll=8
        )


def columns(first):
    return pl.ds(pl.multiple_of(first, LANES), LANES)


def key_value_tile(
    taps_ref, inside_ref, key_out_ref, value_out_ref, window_ref, head, slot, tile
):
    width = taps_ref.shape[1] // 3
    places = slice(tile * LANES, (tile + 1) * LANES)
    first = head * LANES
    key_taps = taps_ref[:, columns(width + first)]
    value_taps = taps_ref[:, columns(2 * width + first)]
    grown = silu(convolved(window_ref.at[slot], key_taps, inside_ref, tile))
    square = jnp.sum(grown * grown, axis=1, keepdims=True)
    key_out_ref[head, places, :] = (grown * lax.rsqrt(square + 1e-6)).astype(jnp.bfloat16)
    values = silu(convolved(window_ref.at[slot + 1], value_taps, inside_ref, tile))
    value_out_ref[head, :, places] = values.T.astype(jnp.bfloat16)


def kept_lanes(docs_ref, doc_count, first_pos, row_count, tiles):
    last_pos = jnp.full((1, len(tiles) * LANES), first_pos + row_count - 1, jnp.int32)
    last_start = start_at(docs_ref, doc_count, last_pos)
    lanes = tiles[0] * LANES + lax.broadcasted_iota(jnp.int32, last_pos.shape, 1)
    lanes_pos = first_pos + (lanes & -LANES) + row_at(lanes & (LANES - 1))
    return jnp.where(lanes_pos >= last_start, 1.0, 0.0).astype(jnp.bfloat16)


def later_rows_kernel(
    docs_ref,
    key_ref,
    value_ref,
    taps_ref,
    key_out_ref,
    value_out_ref,
    state_ref,
    inside_ref,
    window_ref,
    *,
    doc_count,
    heads,
):
    row_count, width = key_ref.shape
    head_count = width // LANES
    tiles = list(range(1, row_count // LANES))
    first_pos = lax.axis_index("seq") * row_count
    keep = kept_lanes(docs_ref, doc_count, first_pos, row_count, tiles)
    inside_masks(docs_ref, doc_count, first_pos, inside_ref)
    ahead = LANES - 16

    def add_state(head):
        state_ref[head] = jnp.dot(
            value_out_ref[head, :, LANES:] * keep,
            key_out_ref[head, LANES:, :],
            preferred_element_type=jnp.float32,
        )

    def group(step):
        for which in range(heads):
            cols = columns((step * heads + which) * LANES)
            fill_rows(window_ref.at[2 * which], key_ref[ahead:, cols], ahead)
            fill_rows(window_ref.at[2 * which + 1], value_ref[ahead:, cols], ahead)
        for tile in tiles:
            for which in range(heads):
                key_value_tile(
                    taps_ref,
                    inside_ref,
                    key_out_ref,
                    value_out_ref,
                    window_ref,
                    step * heads + which,
                    2 * which,
                    tile,
                )

    group(0)

    def body(step, carry):
        for which in range(heads):
            add_state((step - 1) * heads + which)
        group(step)
        return carry

    steps = head_count // heads
    lax.fori_loop(1, steps, body, 0)
    for which in range(heads):
        add_state((steps - 1) * heads + which)


def first_rows_kernel(
    docs_ref,
    key_ref,
    value_ref,
    taps_ref,
    rim_ref,
    inside_ref,
    later_state_ref,
    key_in_ref,
    value_in_ref,
    key_out_ref,
    value_out_ref,
    state_ref,
    window_ref,
    *,
    doc_count,
    row_count,
    heads,
):
    width = key_ref.shape[1]
    head_count = width // LANES
    index = lax.axis_index("seq")
    keep = kept_lanes(docs_ref, doc_count, index * row_count, row_count, [0])

    def add_state(head):
        total = later_state_ref[head] + jnp.dot(
            value_out_ref[head, :, 0:LANES] * keep,
            key_out_ref[head, 0:LANES, :],
            preferred_element_type=jnp.float32,
        )
        place = logical_place(head, index & 1, (index >> 1) & 1)
        state_ref[place] = total.astype(jnp.bfloat16)

    def group(step):
        for which in range(heads):
            first = (step * heads + which) * LANES
            fill_rim(window_ref.at[2 * which], rim_ref[:, columns(width + first)])
            fill_rim(window_ref.at[2 * which + 1], rim_ref[:, columns(2 * width + first)])
            fill_rows(window_ref.at[2 * which], key_ref[0:LANES, columns(first)], 0)
            fill_rows(window_ref.at[2 * which + 1], value_ref[0:LANES, columns(first)], 0)
        for which in range(heads):
            key_value_tile(
                taps_ref,
                inside_ref,
                key_out_ref,
                value_out_ref,
                window_ref,
                step * heads + which,
                2 * which,
                0,
            )

    group(0)

    def body(step, carry):
        for which in range(heads):
            add_state((step - 1) * heads + which)
        group(step)
        return carry

    steps = head_count // heads
    lax.fori_loop(1, steps, body, 0)
    for which in range(heads):
        add_state((steps - 1) * heads + which)


def join_kernel(docs_ref, mine_ref, theirs_ref, *out_refs, doc_count, row_count, bit, parts):
    index = lax.axis_index("seq")
    stride = 1 << bit
    upper_first = (((index >> (bit + 1)) << (bit + 1)) + stride) * row_count

    def step(i, found):
        gap = docs_ref[i] - upper_first
        return jnp.where((gap >= 0) & (gap < stride * row_count), 1, found)

    upper_has = lax.fori_loop(0, doc_count, step, jnp.int32(0))
    is_upper = (index >> bit) & 1
    keep_mine = jnp.where((upper_has == 1) & (is_upper == 0), 0.0, 1.0)
    keep_theirs = jnp.where((upper_has == 1) & (is_upper == 1), 0.0, 1.0)
    skip = theirs_ref.shape[0] // 2 if parts == 2 else 0
    count = out_refs[0].shape[0]
    for part, out_ref in enumerate(out_refs):
        mine = mine_ref[part * count : (part + 1) * count].astype(jnp.float32)
        theirs = theirs_ref[skip + part * count : skip + (part + 1) * count].astype(jnp.float32)
        out_ref[...] = (mine * keep_mine + theirs * keep_theirs).astype(jnp.bfloat16)


def near_kernel(
    docs_ref,
    query_ref,
    rim_ref,
    taps_ref,
    inside_ref,
    table_ref,
    start_ref,
    key_ref,
    value_ref,
    *rest,
    first_head,
    head_count,
    heads,
    skipped,
):
    query_out_ref, near_ref, window_ref, fine_ref, pair_ref = rest[skipped:]
    row_count = query_ref.shape[0]
    tiles = row_count // LANES
    span = 2 * LANES
    sub = lax.broadcasted_iota(jnp.int32, (8, row_count), 0)
    lane = lax.broadcasted_iota(jnp.int32, (8, row_count), 1)
    high = sub ^ (lane & 7)
    sub16 = lax.broadcasted_iota(jnp.int32, (16, row_count), 0)
    low_row = (lax.broadcasted_iota(jnp.int32, (16, row_count), 1) >> 3) & 15
    low = sub16 ^ low_row
    same_group = lax.broadcasted_iota(jnp.int32, (8, LANES), 0) == (
        lax.broadcasted_iota(jnp.int32, (8, LANES), 1) & 7
    )
    key_row = row_at(lax.broadcasted_iota(jnp.int32, (LANES, LANES), 0))

    def group(step, carry):
        for which in range(heads):
            head = first_head + step * heads + which
            fill_rim(window_ref.at[which], rim_ref[:, columns(head * LANES)])
            fill_rows(window_ref.at[which], query_ref[:, columns(head * LANES)], 0)

        for which in range(heads):
            head = first_head + step * heads + which
            taps = taps_ref[:, columns(head * LANES)]
            for tile in range(tiles):
                grown = silu(convolved(window_ref.at[which], taps, inside_ref, tile))
                query_out_ref[head, tile * LANES : (tile + 1) * LANES, :] = grown.astype(
                    jnp.bfloat16
                )

        for which in range(heads):
            head = first_head + step * heads + which
            tok_bits = row_count.bit_length() - 1
            scaled = [table_ref[level, pl.ds(head, 1), :] for level in range(tok_bits + 1)]
            coarse = jnp.where(high < 2, scaled[5], jnp.where(high < 4, scaled[6], scaled[7]))
            coarse = jnp.where(sub > (lane & 7), 0.0, coarse)
            fine = jnp.where(
                low == 0,
                scaled[0],
                jnp.where(
                    low == 1,
                    scaled[1],
                    jnp.where(low < 4, scaled[2], jnp.where(low < 8, scaled[3], scaled[4])),
                ),
            )
            fine = jnp.where(sub16 > low_row, 0.0, fine)
            for tile in range(tiles):
                fine_ref[which, tile] = fine[:, tile * LANES : (tile + 1) * LANES]
            for part in range(row_count // span):
                rows = (part + 1) * span
                scores = lax.dot_general(
                    key_ref[head, 0:rows, :],
                    query_out_ref[head, part * span : rows, :],
                    NT,
                    preferred_element_type=jnp.float32,
                )
                for side in range(2):
                    tile = 2 * part + side
                    cols = slice(tile * LANES, (tile + 1) * LANES)
                    starts = start_ref[0:1, cols]
                    for other in range(tile + 1):
                        if other == tile:
                            weight = jnp.concatenate(
                                [
                                    jnp.where(
                                        same_group,
                                        fine_ref[which, tile, pl.ds(a, 8, stride=0), :],
                                        coarse[:, cols],
                                    )
                                    for a in range(16)
                                ],
                                axis=0,
                            )
                        else:
                            weight = scaled[7 + (tile ^ other).bit_length()][:, cols]
                        piece = scores[
                            other * LANES : (other + 1) * LANES,
                            side * LANES : (side + 1) * LANES,
                        ]
                        valid = key_row >= starts - other * LANES
                        pair_ref[which, other * LANES : (other + 1) * LANES, cols] = jnp.where(
                            valid, piece * weight, 0.0
                        ).astype(jnp.bfloat16)
                    if side == 0:
                        pair_ref[which, (tile + 1) * LANES : rows, cols] = jnp.zeros(
                            (LANES, LANES), jnp.bfloat16
                        )
                near_ref[head, :, part * span : rows] = jnp.dot(
                    value_ref[head, :, 0:rows],
                    pair_ref[which, 0:rows, part * span : rows],
                    preferred_element_type=jnp.float32,
                )
        return carry

    lax.fori_loop(0, head_count // heads, group, 0)


def far_kernel(
    query_ref,
    near_ref,
    table_ref,
    gain_ref,
    first_state_ref,
    lower_ref,
    last_ref,
    *rest,
    group,
    previous,
    writes_own,
    dev_bits,
):
    head_count, row_count, _ = query_ref.shape
    quarter = head_count // 4
    wide = quarter * LANES
    span = 2 * LANES
    index = lax.axis_index("seq")
    core_bit = index & 1
    y_bit = (index >> 1) & 1
    tok_bits = row_count.bit_length() - 1

    def first_head_of(group):
        other_half, other_quarter = group
        return (core_bit ^ other_half) * 2 * quarter + (y_bit ^ other_quarter) * quarter

    def copy_out(result_ref, group, sem):
        cols = pl.ds(pl.multiple_of(first_head_of(group) * LANES, wide), wide)
        return pltpu.make_async_copy(result_ref, out_hbm_ref.at[:, cols], sem)

    rest = list(rest)
    previous_ref = rest.pop(0) if previous else None
    sems = rest.pop() if previous or writes_own else None
    result_ref = rest.pop()
    out_hbm_ref = rest.pop() if previous or writes_own else None
    copies = [copy_out(previous_ref, previous, sems.at[0])] if previous else []
    for copy in copies:
        copy.start()

    first_head = first_head_of(group)
    select = selection(span)
    finished = []
    for local_head in range(quarter):
        head = first_head + local_head
        first_place = logical_place(head, 1 - core_bit, y_bit)
        place = logical_place(head, core_bit, y_bit) & 7
        states = [first_state_ref[first_place]]
        for level in range(dev_bits - 2):
            states.append(lower_ref[level, place])
        states.append(last_ref[local_head])
        images = lax.dot_general(
            jnp.concatenate(states, axis=0),
            query_ref[head],
            NT,
            preferred_element_type=jnp.float32,
        )
        summed = near_ref[head]
        for bit in range(dev_bits):
            coef = table_ref[tok_bits + 1 + bit, pl.ds(head, 1), :]
            summed = summed + coef * images[bit * LANES : (bit + 1) * LANES, :]
        mean = jnp.mean(summed * summed, axis=0, keepdims=True)
        normed = summed * lax.rsqrt(mean + 1e-6)
        gain = jnp.concatenate([gain_ref[head]] * (row_count // LANES), axis=1)
        finished.append((normed * gain).astype(jnp.bfloat16))
        if local_head % 2 == 1:
            both = jnp.concatenate(finished[-2:], axis=0)
            cols = slice((local_head - 1) * LANES, (local_head + 1) * LANES)
            for first in range(0, row_count, span):
                turned = lax.dot_general(
                    select, both[:, first : first + span], NT, preferred_element_type=jnp.float32
                )
                result_ref[first : first + span, cols] = turned.astype(jnp.bfloat16)
    if writes_own:
        copies.append(copy_out(result_ref, group, sems.at[1]))
        copies[-1].start()
    for copy in copies:
        copy.wait()


def far_skip(*refs, **settings):
    far_kernel(*refs[:8], *refs[9:], **settings)


def local(query_in, key_in, value_in, conv_weight, level_weight, out_gain, doc_starts):
    row_count, width_all = query_in.shape
    head_count, level_count, _ = level_weight.shape
    head_size = width_all // head_count
    conv_width = conv_weight.shape[0]
    doc_count = doc_starts.shape[0]
    dev_index = lax.axis_index("seq")
    dev_count = lax.axis_size("seq")
    dev_bits = dev_count.bit_length() - 1
    rim_rows = conv_width - 1
    tiles = row_count // LANES
    smem = pl.BlockSpec(memory_space=pltpu.SMEM)
    vmem = pl.BlockSpec(memory_space=pltpu.VMEM)
    anywhere = pl.BlockSpec(memory_space=pl.ANY)

    tails = pl.pallas_call(
        rim_kernel,
        in_specs=[pl.BlockSpec(memory_space=pltpu.HBM)] * 3,
        out_specs=vmem,
        out_shape=pltpu.VMEM((rim_rows, 3 * width_all), query_in.dtype),
        scratch_shapes=[
            pltpu.VMEM((3, 16, width_all), query_in.dtype),
            pltpu.SemaphoreType.DMA((3,)),
        ],
        compiler_params=limited(1),
        name="rim",
    )(*(pltpu.with_memory_space_constraint(x, pltpu.HBM) for x in (query_in, key_in, value_in)))
    tails, docs = lax.optimization_barrier((tails, doc_starts))
    rims = exchange(tails, lambda i: i + 1 if i + 1 < dev_count else None)
    heads = 4
    keys, values_t, later_state, inside = pl.pallas_call(
        functools.partial(later_rows_kernel, doc_count=doc_count, heads=heads),
        in_specs=[smem] + [vmem] * 3,
        out_specs=[vmem] * 4,
        out_shape=[
            pltpu.VMEM((head_count, row_count, head_size), jnp.bfloat16),
            pltpu.VMEM((head_count, head_size, row_count), jnp.bfloat16),
            pltpu.VMEM((head_count, head_size, head_size), jnp.float32),
            pltpu.VMEM((tiles, LANES + 8 * (rim_rows - 1), LANES), jnp.float32),
        ],
        scratch_shapes=[pltpu.VMEM((2 * heads, window_rows(row_count), LANES), jnp.float32)],
        compiler_params=limited(6),
        cost_estimate=pl.CostEstimate(
            flops=500_000_000, bytes_accessed=4_000_000, transcendentals=1_500_000
        ),
        name="later_rows",
    )(docs, key_in, value_in, conv_weight)
    rims, keys, values_t, later_state = lax.optimization_barrier(
        (rims, keys, values_t, later_state)
    )
    keys, values_t, state = pl.pallas_call(
        functools.partial(
            first_rows_kernel, doc_count=doc_count, row_count=row_count, heads=heads
        ),
        in_specs=[smem] + [vmem] * 8,
        out_specs=[vmem] * 3,
        out_shape=[
            pltpu.VMEM((head_count, row_count, head_size), jnp.bfloat16),
            pltpu.VMEM((head_count, head_size, row_count), jnp.bfloat16),
            pltpu.VMEM((head_count, head_size, head_size), jnp.bfloat16),
        ],
        scratch_shapes=[pltpu.VMEM((2 * heads, window_rows(LANES), LANES), jnp.float32)],
        input_output_aliases={7: 0, 8: 1},
        compiler_params=limited(4),
        name="first_rows",
    )(docs, key_in, value_in, conv_weight, rims, inside, later_state, keys, values_t)

    def joined(mine, theirs, bit, parts=1):
        count = mine.shape[0] // (2 if parts == 2 else 1)
        shape = (count // parts, head_size, head_size)
        return pl.pallas_call(
            functools.partial(
                join_kernel, doc_count=doc_count, row_count=row_count, bit=bit, parts=parts
            ),
            in_specs=[smem, vmem, vmem],
            out_specs=[vmem] * parts,
            out_shape=[pltpu.VMEM(shape, jnp.bfloat16)] * parts,
            compiler_params=limited(1),
            name="join",
        )(doc_starts, mine, theirs)

    def near_piece(first_head, piece_heads, buffers, docs):
        extra = [] if buffers is None else list(buffers)
        return pl.pallas_call(
            functools.partial(
                near_kernel,
                first_head=first_head,
                head_count=piece_heads,
                heads=heads,
                skipped=len(extra),
            ),
            in_specs=[smem] + [vmem] * (8 + len(extra)),
            out_specs=[vmem] * 2,
            out_shape=[
                pltpu.VMEM((head_count, row_count, head_size), jnp.bfloat16),
                pltpu.VMEM((head_count, head_size, row_count), jnp.float32),
            ],
            scratch_shapes=[
                pltpu.VMEM((heads, window_rows(row_count), LANES), jnp.float32),
                pltpu.VMEM((heads, tiles, 16, LANES), jnp.float32),
                pltpu.VMEM((heads, row_count, row_count), jnp.bfloat16),
            ],
            input_output_aliases={9: 0, 10: 1} if extra else {},
            compiler_params=limited(6),
            cost_estimate=pl.CostEstimate(
                flops=5_000_000_000, bytes_accessed=35_000_000, transcendentals=300_000
            ),
            name="near",
        )(docs, query_in, rims, conv_weight, inside, table, starts, keys, values_t, *extra)

    def far_piece(group, lower, last_state, previous=None, before=None, out=None, writes_own=False):
        writes = previous or writes_own
        extra = ([before] if previous else []) + ([] if out is None else [out])
        out_type = jax.ShapeDtypeStruct((row_count, width_all), jnp.bfloat16)
        result_type = pltpu.VMEM((row_count, width_all // 4), jnp.bfloat16)
        return pl.pallas_call(
            functools.partial(
                far_skip if out is not None else far_kernel,
                group=group,
                previous=previous,
                writes_own=writes_own,
                dev_bits=dev_bits,
            ),
            in_specs=[vmem] * (8 if previous else 7) + ([] if out is None else [anywhere]),
            out_specs=([anywhere] if writes else []) + ([] if writes_own else [vmem]),
            out_shape=([out_type] if writes else []) + ([] if writes_own else [result_type]),
            scratch_shapes=([result_type] if writes_own else [])
            + ([pltpu.SemaphoreType.DMA((2,))] if writes else []),
            input_output_aliases={} if out is None else {8: 0},
            compiler_params=limited(4),
            cost_estimate=pl.CostEstimate(
                flops=1_000_000, bytes_accessed=10_000, transcendentals=0
            ),
            name="far",
        )(queries, near, table, gains, first_state, lower, last_state, *extra)

    quarter = head_count // 4
    state, docs = lax.optimization_barrier((state, docs))
    first_state = swapped(state, 0)
    table, starts, gains = pl.pallas_call(
        functools.partial(tables_kernel, doc_count=doc_count),
        in_specs=[smem, vmem, vmem],
        out_specs=[vmem] * 3,
        out_shape=[
            pltpu.VMEM((level_count, head_count, row_count), jnp.float32),
            pltpu.VMEM((8, row_count), jnp.int32),
            pltpu.VMEM((head_count, head_size, LANES), jnp.float32),
        ],
        compiler_params=limited(2),
        name="tables",
    )(docs, jnp.transpose(level_weight, (1, 0, 2)), out_gain.reshape(head_count, 1, head_size))
    first_state, table, starts, gains = lax.optimization_barrier(
        (first_state, table, starts, gains)
    )
    pair_kept, pair_sent = joined(state, first_state, 0, parts=2)

    pair_sent, tied = lax.optimization_barrier((pair_sent, docs))
    pair_in = swapped(pair_sent, 1)
    buffers = near_piece(0, quarter, None, tied)
    pair_in, buffers = lax.optimization_barrier((pair_in, buffers))
    (carried,) = joined(pair_kept, pair_in, 1)

    received = []
    for bit in range(2, dev_bits - 1):
        if bit == 2:
            carried, tied = lax.optimization_barrier((carried, docs))
        arrived = swapped(carried, bit)
        if bit == 2:
            buffers = near_piece(quarter, quarter, buffers, tied)
            arrived, buffers = lax.optimization_barrier((arrived, buffers))
        received.append(arrived)
        (carried,) = joined(carried, arrived, bit)

    mine = jnp.stack([pair_kept] + received)
    carried, mine, tied = lax.optimization_barrier((carried, mine, docs))
    last_own = sent_up(carried, dev_bits - 1)
    theirs = swapped(mine, 1)
    buffers = near_piece(2 * quarter, 2 * quarter, buffers, tied)
    last_own, theirs, buffers = lax.optimization_barrier((last_own, theirs, buffers))
    queries, near = buffers
    own = jnp.concatenate([jnp.stack([pair_in] + received), theirs], axis=1)
    own, last_own = lax.optimization_barrier((own, last_own))

    last_next = swapped(last_own, 1)
    other = swapped(own, 0)
    last_other = swapped(last_own, 0)
    (done,) = far_piece((0, 0), own, last_own)
    other, last_other, done = lax.optimization_barrier((other, last_other, done))
    (out,) = far_piece((1, 0), other, last_other, (0, 0), done, writes_own=True)
    last_next, out = lax.optimization_barrier((last_next, out))
    last_far = swapped(last_next, 0)
    (done,) = far_piece((0, 1), own, last_next)
    last_far, out, done = lax.optimization_barrier((last_far, out, done))
    (out,) = far_piece((1, 1), other, last_far, (0, 1), done, out, writes_own=True)
    return out


def solution(mesh):
    in_specs = (
        P(("groups", "seq"), None),
        P(("groups", "seq"), None),
        P(("groups", "seq"), None),
        P(),
        P(None, None, ("groups", "seq")),
        P(),
        P("groups"),
    )
    out_specs = P(("groups", "seq"), None)
    return jax.shard_map(local, mesh=mesh, in_specs=in_specs, out_specs=out_specs, check_vma=False)
```

```python
import functools

import jax
import jax.numpy as jnp
from jax import lax
from jax.experimental import pallas as pl
from jax.experimental.pallas import tpu as pltpu
from jax.sharding import PartitionSpec as P

LANES = 128
GROUP = 16
PITCH = 24
NT = (((1,), (1,)), ((), ()))


def exchange(block, partner):
    count = lax.axis_size("seq")
    route = [(i, partner(i)) for i in range(count) if partner(i) is not None]
    return lax.ppermute(block, "seq", route)


def swapped(block, bit):
    return exchange(block, lambda i: i ^ (1 << bit))


def limited(mebibytes):
    return pltpu.CompilerParams(vmem_limit_bytes=mebibytes * 1024 * 1024)


def start_at(docs_ref, doc_count, positions):
    def step(i, start):
        doc = docs_ref[i]
        return jnp.where(positions >= doc, doc, start)

    return lax.fori_loop(0, doc_count, step, jnp.zeros_like(positions))


def silu_of_twice(half):
    return half + half * jnp.tanh(half)


def logical_place(head, core_bit, y_bit):
    return ((head >> 3) ^ core_bit) * 8 + (((head >> 2) & 1) ^ y_bit) * 4 + (head & 3)


def row_at(place):
    return ((place & 7) << 4) | ((place >> 3) & 15)


def selection(size):
    rows = lax.broadcasted_iota(jnp.int32, (size, size), 0)
    places = lax.broadcasted_iota(jnp.int32, (size, size), 1)
    chosen = rows == (places & -LANES) + row_at(places & (LANES - 1))
    return jnp.where(chosen, 1.0, 0.0).astype(jnp.bfloat16)


def rim_kernel(query_ref, key_ref, value_ref, out_ref, buffer, sems):
    rim_rows = out_ref.shape[0]
    edge, width = buffer.shape[1:]
    copies = []
    for part, ref in enumerate((query_ref, key_ref, value_ref)):
        rows = ref.shape[0]
        copy = pltpu.make_async_copy(
            ref.at[rows - edge : rows, :], buffer.at[part], sems.at[part]
        )
        copy.start()
        copies.append(copy)
    for part, copy in enumerate(copies):
        copy.wait()
        out_ref[:, part * width : (part + 1) * width] = buffer[part, edge - rim_rows : edge, :]


def tables_kernel(
    docs_ref, level_ref, gain_ref, table_ref, start_ref, gain_out_ref, factor_ref, *, doc_count
):
    join_factors(docs_ref, doc_count, level_ref.shape[2], factor_ref)
    level_count, head_count, row_count = level_ref.shape
    tok_bits = row_count.bit_length() - 1
    index = lax.axis_index("seq")
    first_pos = index * row_count
    lanes = lax.broadcasted_iota(jnp.int32, (8, row_count), 1)
    positions = first_pos + (lanes & -LANES) + row_at(lanes & (LANES - 1))
    starts = start_at(docs_ref, doc_count, positions)
    start_ref[...] = starts - first_pos
    starts = jnp.concatenate([starts] * (head_count // 8), axis=0)
    select = selection(LANES)
    levels = level_ref[...].reshape(level_count * head_count, row_count)
    for tile in range(row_count // LANES):
        cols = slice(tile * LANES, (tile + 1) * LANES)
        weights = jnp.dot(levels[:, cols], select, preferred_element_type=jnp.float32)
        for level in range(level_count):
            scaled = weights[level * head_count : (level + 1) * head_count] * 2.0 ** (-level / 2)
            if level > tok_bits:
                bit = level - tok_bits - 1
                limit = jnp.where((index >> bit) & 1 == 1, (index >> bit << bit) * row_count, 0)
                scaled = jnp.where(starts[:, cols] < limit, scaled, 0.0)
            table_ref[level, :, cols] = scaled
    for head in range(head_count):
        gain_out_ref[head] = jnp.broadcast_to(gain_ref[head], (LANES, LANES)).T


def window_rows(row_count):
    return (row_count // GROUP + 1) * PITCH


def fill_rim(window_ref, rim):
    rim_rows = rim.shape[0]
    window_ref[GROUP - 8 : GROUP, :] = jnp.concatenate(
        [jnp.zeros((8 - rim_rows, rim.shape[1]), jnp.float32), rim.astype(jnp.float32)], axis=0
    )


def fill_rows(window_ref, rows, first):
    rows = rows.astype(jnp.float32)
    for start in range(0, rows.shape[0], GROUP):
        place = ((first + start) // GROUP + 1) * PITCH
        window_ref[place : place + GROUP, :] = rows[start : start + GROUP, :]


def convolved(window_ref, taps, inside_ref, tile):
    reach = taps.shape[0] - 1
    base = (tile * (LANES // GROUP) + 1) * PITCH
    places = [base - PITCH + GROUP + i for i in range(-reach, 0)]
    places += [base + i for i in range(GROUP)]
    rows = [window_ref[pl.ds(place, 8, stride=PITCH), :] for place in places]
    summed = None
    for offset in range(reach, -1, -1):
        term = taps[offset : offset + 1, :] * jnp.concatenate(
            rows[reach - offset : reach - offset + 16], axis=0
        )
        summed = term if summed is None else term + summed
        if offset:
            first = (reach - offset) * 8
            summed = summed * inside_ref[tile, first : first + LANES, :]
    return summed


def inside_masks(docs_ref, doc_count, first_pos, inside_ref):
    tiles, places, _ = inside_ref.shape
    ahead = (places - LANES) // 8
    place = lax.broadcasted_iota(jnp.int32, (places, LANES), 0)
    rows = ((place & 7) << 4) + (place >> 3) - ahead
    for tile in range(tiles):
        positions = rows + (first_pos + tile * LANES)

        def step(i, inside):
            return jnp.where(positions == docs_ref[i], 0.0, inside)

        inside_ref[tile] = lax.fori_loop(
            0, doc_count, step, jnp.ones((places, LANES), jnp.float32), unroll=8
        )


def columns(first):
    return pl.ds(pl.multiple_of(first, LANES), LANES)


def key_value_tile(
    taps_ref, inside_ref, key_out_ref, value_out_ref, window_ref, head, slot, tile
):
    width = taps_ref.shape[1] // 3
    places = slice(tile * LANES, (tile + 1) * LANES)
    first = head * LANES
    key_taps = 0.5 * taps_ref[:, columns(width + first)]
    value_taps = 0.5 * taps_ref[:, columns(2 * width + first)]
    grown = silu_of_twice(convolved(window_ref.at[slot], key_taps, inside_ref, tile))
    square = jnp.sum(grown * grown, axis=1, keepdims=True)
    key_out_ref[head, places, :] = (grown * lax.rsqrt(square + 1e-6)).astype(jnp.bfloat16)
    values = silu_of_twice(convolved(window_ref.at[slot + 1], value_taps, inside_ref, tile))
    value_out_ref[head, :, places] = values.T.astype(jnp.bfloat16)


def kept_lanes(docs_ref, doc_count, first_pos, row_count, tiles):
    last_pos = jnp.full((1, len(tiles) * LANES), first_pos + row_count - 1, jnp.int32)
    last_start = start_at(docs_ref, doc_count, last_pos)
    lanes = tiles[0] * LANES + lax.broadcasted_iota(jnp.int32, last_pos.shape, 1)
    lanes_pos = first_pos + (lanes & -LANES) + row_at(lanes & (LANES - 1))
    return jnp.where(lanes_pos >= last_start, 1.0, 0.0).astype(jnp.bfloat16)


def later_rows_kernel(
    docs_ref,
    key_ref,
    value_ref,
    taps_ref,
    key_out_ref,
    value_out_ref,
    state_ref,
    inside_ref,
    window_ref,
    *,
    doc_count,
    heads,
):
    row_count, width = key_ref.shape
    head_count = width // LANES
    tiles = list(range(1, row_count // LANES))
    first_pos = lax.axis_index("seq") * row_count
    keep = kept_lanes(docs_ref, doc_count, first_pos, row_count, tiles)
    inside_masks(docs_ref, doc_count, first_pos, inside_ref)
    ahead = LANES - 16

    def add_state(head):
        state_ref[head] = jnp.dot(
            value_out_ref[head, :, LANES:] * keep,
            key_out_ref[head, LANES:, :],
            preferred_element_type=jnp.float32,
        )

    def group(step):
        for which in range(heads):
            cols = columns((step * heads + which) * LANES)
            fill_rows(window_ref.at[2 * which], key_ref[ahead:, cols], ahead)
            fill_rows(window_ref.at[2 * which + 1], value_ref[ahead:, cols], ahead)
        for tile in tiles:
            for which in range(heads):
                key_value_tile(
                    taps_ref,
                    inside_ref,
                    key_out_ref,
                    value_out_ref,
                    window_ref,
                    step * heads + which,
                    2 * which,
                    tile,
                )

    group(0)

    def body(step, carry):
        for which in range(heads):
            add_state((step - 1) * heads + which)
        group(step)
        return carry

    steps = head_count // heads
    lax.fori_loop(1, steps, body, 0)
    for which in range(heads):
        add_state((steps - 1) * heads + which)


def first_rows_kernel(
    docs_ref,
    key_ref,
    value_ref,
    taps_ref,
    rim_ref,
    inside_ref,
    later_state_ref,
    key_in_ref,
    value_in_ref,
    key_out_ref,
    value_out_ref,
    state_ref,
    window_ref,
    *,
    doc_count,
    row_count,
    heads,
):
    width = key_ref.shape[1]
    head_count = width // LANES
    index = lax.axis_index("seq")
    keep = kept_lanes(docs_ref, doc_count, index * row_count, row_count, [0])

    def add_state(head):
        total = later_state_ref[head] + jnp.dot(
            value_out_ref[head, :, 0:LANES] * keep,
            key_out_ref[head, 0:LANES, :],
            preferred_element_type=jnp.float32,
        )
        place = logical_place(head, index & 1, (index >> 1) & 1)
        state_ref[place] = total.astype(jnp.bfloat16)

    def group(step):
        for which in range(heads):
            first = (step * heads + which) * LANES
            fill_rim(window_ref.at[2 * which], rim_ref[:, columns(width + first)])
            fill_rim(window_ref.at[2 * which + 1], rim_ref[:, columns(2 * width + first)])
            fill_rows(window_ref.at[2 * which], key_ref[0:LANES, columns(first)], 0)
            fill_rows(window_ref.at[2 * which + 1], value_ref[0:LANES, columns(first)], 0)
        for which in range(heads):
            key_value_tile(
                taps_ref,
                inside_ref,
                key_out_ref,
                value_out_ref,
                window_ref,
                step * heads + which,
                2 * which,
                0,
            )

    group(0)

    def body(step, carry):
        for which in range(heads):
            add_state((step - 1) * heads + which)
        group(step)
        return carry

    steps = head_count // heads
    lax.fori_loop(1, steps, body, 0)
    for which in range(heads):
        add_state((steps - 1) * heads + which)


def join_factors(docs_ref, doc_count, row_count, factor_ref):
    index = lax.axis_index("seq")
    for bit in range(factor_ref.shape[0] // 2):
        stride = 1 << bit
        upper_first = (((index >> (bit + 1)) << (bit + 1)) + stride) * row_count

        def step(i, found):
            gap = docs_ref[i] - upper_first
            return jnp.where((gap >= 0) & (gap < stride * row_count), 1, found)

        upper_has = lax.fori_loop(0, doc_count, step, jnp.int32(0), unroll=8)
        is_upper = (index >> bit) & 1
        keep_mine = jnp.where((upper_has == 1) & (is_upper == 0), 0.0, 1.0)
        keep_theirs = jnp.where((upper_has == 1) & (is_upper == 1), 0.0, 1.0)
        factor_ref[2 * bit : 2 * bit + 1, :] = jnp.full((1, LANES), keep_mine, jnp.float32)
        factor_ref[2 * bit + 1 : 2 * bit + 2, :] = jnp.full((1, LANES), keep_theirs, jnp.float32)


def near_kernel(
    docs_ref,
    query_ref,
    rim_ref,
    taps_ref,
    inside_ref,
    table_ref,
    start_ref,
    key_ref,
    value_ref,
    *rest,
    first_head,
    head_count,
    heads,
    skipped,
):
    query_out_ref, near_ref, window_ref, fine_ref, pair_ref = rest[skipped:]
    row_count = query_ref.shape[0]
    tiles = row_count // LANES
    span = 2 * LANES
    sub = lax.broadcasted_iota(jnp.int32, (8, row_count), 0)
    lane = lax.broadcasted_iota(jnp.int32, (8, row_count), 1)
    high = sub ^ (lane & 7)
    sub16 = lax.broadcasted_iota(jnp.int32, (16, row_count), 0)
    low_row = (lax.broadcasted_iota(jnp.int32, (16, row_count), 1) >> 3) & 15
    low = sub16 ^ low_row
    same_group = lax.broadcasted_iota(jnp.int32, (8, LANES), 0) == (
        lax.broadcasted_iota(jnp.int32, (8, LANES), 1) & 7
    )
    key_row = row_at(lax.broadcasted_iota(jnp.int32, (LANES, LANES), 0))

    def group(step, carry):
        for which in range(heads):
            head = first_head + step * heads + which
            fill_rim(window_ref.at[which], rim_ref[:, columns(head * LANES)])
            fill_rows(window_ref.at[which], query_ref[:, columns(head * LANES)], 0)

        for which in range(heads):
            head = first_head + step * heads + which
            taps = 0.5 * taps_ref[:, columns(head * LANES)]
            for tile in range(tiles):
                grown = silu_of_twice(convolved(window_ref.at[which], taps, inside_ref, tile))
                query_out_ref[head, tile * LANES : (tile + 1) * LANES, :] = grown.astype(
                    jnp.bfloat16
                )

        for which in range(heads):
            head = first_head + step * heads + which
            tok_bits = row_count.bit_length() - 1
            scaled = [table_ref[level, pl.ds(head, 1), :] for level in range(tok_bits + 1)]
            coarse = jnp.where(high < 2, scaled[5], jnp.where(high < 4, scaled[6], scaled[7]))
            coarse = jnp.where(sub > (lane & 7), 0.0, coarse)
            fine = jnp.where(
                low == 0,
                scaled[0],
                jnp.where(
                    low == 1,
                    scaled[1],
                    jnp.where(low < 4, scaled[2], jnp.where(low < 8, scaled[3], scaled[4])),
                ),
            )
            fine = jnp.where(sub16 > low_row, 0.0, fine)
            for tile in range(tiles):
                fine_ref[which, tile] = fine[:, tile * LANES : (tile + 1) * LANES]
            for part in range(row_count // span):
                rows = (part + 1) * span
                scores = lax.dot_general(
                    key_ref[head, 0:rows, :],
                    query_out_ref[head, part * span : rows, :],
                    NT,
                    preferred_element_type=jnp.float32,
                )
                for side in range(2):
                    tile = 2 * part + side
                    cols = slice(tile * LANES, (tile + 1) * LANES)
                    starts = start_ref[0:1, cols]
                    for other in range(tile + 1):
                        if other == tile:
                            weight = jnp.concatenate(
                                [
                                    jnp.where(
                                        same_group,
                                        fine_ref[which, tile, pl.ds(a, 8, stride=0), :],
                                        coarse[:, cols],
                                    )
                                    for a in range(16)
                                ],
                                axis=0,
                            )
                        else:
                            weight = scaled[7 + (tile ^ other).bit_length()][:, cols]
                        piece = scores[
                            other * LANES : (other + 1) * LANES,
                            side * LANES : (side + 1) * LANES,
                        ]
                        valid = key_row >= starts - other * LANES
                        pair_ref[which, other * LANES : (other + 1) * LANES, cols] = jnp.where(
                            valid, piece * weight, 0.0
                        ).astype(jnp.bfloat16)
                    if side == 0:
                        pair_ref[which, (tile + 1) * LANES : rows, cols] = jnp.zeros(
                            (LANES, LANES), jnp.bfloat16
                        )
                near_ref[head, :, part * span : rows] = jnp.dot(
                    value_ref[head, :, 0:rows],
                    pair_ref[which, 0:rows, part * span : rows],
                    preferred_element_type=jnp.float32,
                )
        return carry

    lax.fori_loop(0, head_count // heads, group, 0)


def far_kernel(
    query_ref,
    near_ref,
    table_ref,
    gain_ref,
    first_state_ref,
    lower_ref,
    last_ref,
    *rest,
    group,
    previous,
    writes_own,
    dev_bits,
):
    head_count, row_count, _ = query_ref.shape
    quarter = head_count // 4
    wide = quarter * LANES
    span = 2 * LANES
    index = lax.axis_index("seq")
    core_bit = index & 1
    y_bit = (index >> 1) & 1
    tok_bits = row_count.bit_length() - 1

    def first_head_of(group):
        other_half, other_quarter = group
        return (core_bit ^ other_half) * 2 * quarter + (y_bit ^ other_quarter) * quarter

    def copy_out(result_ref, group, sem):
        cols = pl.ds(pl.multiple_of(first_head_of(group) * LANES, wide), wide)
        return pltpu.make_async_copy(result_ref, out_hbm_ref.at[:, cols], sem)

    rest = list(rest)
    previous_ref = rest.pop(0) if previous else None
    sems = rest.pop() if previous or writes_own else None
    result_ref = rest.pop()
    out_hbm_ref = rest.pop() if previous or writes_own else None
    copies = [copy_out(previous_ref, previous, sems.at[0])] if previous else []
    for copy in copies:
        copy.start()

    first_head = first_head_of(group)
    select = selection(span)
    finished = []
    for local_head in range(quarter):
        head = first_head + local_head
        first_place = logical_place(head, 1 - core_bit, y_bit)
        place = logical_place(head, core_bit, y_bit) & 7
        states = [first_state_ref[first_place]]
        for level in range(dev_bits - 2):
            states.append(lower_ref[level, place])
        states.append(last_ref[local_head])
        images = lax.dot_general(
            jnp.concatenate(states, axis=0),
            query_ref[head],
            NT,
            preferred_element_type=jnp.float32,
        )
        summed = near_ref[head]
        for bit in range(dev_bits):
            coef = table_ref[tok_bits + 1 + bit, pl.ds(head, 1), :]
            summed = summed + coef * images[bit * LANES : (bit + 1) * LANES, :]
        mean = jnp.mean(summed * summed, axis=0, keepdims=True)
        normed = summed * lax.rsqrt(mean + 1e-6)
        gain = jnp.concatenate([gain_ref[head]] * (row_count // LANES), axis=1)
        finished.append((normed * gain).astype(jnp.bfloat16))
        if local_head % 2 == 1:
            both = jnp.concatenate(finished[-2:], axis=0)
            cols = slice((local_head - 1) * LANES, (local_head + 1) * LANES)
            for first in range(0, row_count, span):
                turned = lax.dot_general(
                    select, both[:, first : first + span], NT, preferred_element_type=jnp.float32
                )
                result_ref[first : first + span, cols] = turned.astype(jnp.bfloat16)
    if writes_own:
        copies.append(copy_out(result_ref, group, sems.at[1]))
        copies[-1].start()
    for copy in copies:
        copy.wait()


def far_skip(*refs, **settings):
    far_kernel(*refs[:8], *refs[9:], **settings)


def local(query_in, key_in, value_in, conv_weight, level_weight, out_gain, doc_starts):
    row_count, width_all = query_in.shape
    head_count, level_count, _ = level_weight.shape
    head_size = width_all // head_count
    conv_width = conv_weight.shape[0]
    doc_count = doc_starts.shape[0]
    dev_index = lax.axis_index("seq")
    dev_count = lax.axis_size("seq")
    dev_bits = dev_count.bit_length() - 1
    rim_rows = conv_width - 1
    tiles = row_count // LANES
    smem = pl.BlockSpec(memory_space=pltpu.SMEM)
    vmem = pl.BlockSpec(memory_space=pltpu.VMEM)
    anywhere = pl.BlockSpec(memory_space=pl.ANY)

    tails = pl.pallas_call(
        rim_kernel,
        in_specs=[pl.BlockSpec(memory_space=pltpu.HBM)] * 3,
        out_specs=vmem,
        out_shape=pltpu.VMEM((rim_rows, 3 * width_all), query_in.dtype),
        scratch_shapes=[
            pltpu.VMEM((3, 16, width_all), query_in.dtype),
            pltpu.SemaphoreType.DMA((3,)),
        ],
        compiler_params=limited(1),
        name="rim",
    )(*(pltpu.with_memory_space_constraint(x, pltpu.HBM) for x in (query_in, key_in, value_in)))
    tails, docs = lax.optimization_barrier((tails, doc_starts))
    rims = exchange(tails, lambda i: i + 1 if i + 1 < dev_count else None)
    heads = 4
    keys, values_t, later_state, inside = pl.pallas_call(
        functools.partial(later_rows_kernel, doc_count=doc_count, heads=heads),
        in_specs=[smem] + [vmem] * 3,
        out_specs=[vmem] * 4,
        out_shape=[
            pltpu.VMEM((head_count, row_count, head_size), jnp.bfloat16),
            pltpu.VMEM((head_count, head_size, row_count), jnp.bfloat16),
            pltpu.VMEM((head_count, head_size, head_size), jnp.float32),
            pltpu.VMEM((tiles, LANES + 8 * (rim_rows - 1), LANES), jnp.float32),
        ],
        scratch_shapes=[pltpu.VMEM((2 * heads, window_rows(row_count), LANES), jnp.float32)],
        compiler_params=limited(6),
        cost_estimate=pl.CostEstimate(
            flops=500_000_000, bytes_accessed=4_000_000, transcendentals=1_500_000
        ),
        name="later_rows",
    )(docs, key_in, value_in, conv_weight)
    rims, keys, values_t, later_state = lax.optimization_barrier(
        (rims, keys, values_t, later_state)
    )
    keys, values_t, state = pl.pallas_call(
        functools.partial(
            first_rows_kernel, doc_count=doc_count, row_count=row_count, heads=heads
        ),
        in_specs=[smem] + [vmem] * 8,
        out_specs=[vmem] * 3,
        out_shape=[
            pltpu.VMEM((head_count, row_count, head_size), jnp.bfloat16),
            pltpu.VMEM((head_count, head_size, row_count), jnp.bfloat16),
            pltpu.VMEM((head_count, head_size, head_size), jnp.bfloat16),
        ],
        scratch_shapes=[pltpu.VMEM((2 * heads, window_rows(LANES), LANES), jnp.float32)],
        input_output_aliases={7: 0, 8: 1},
        compiler_params=limited(4),
        name="first_rows",
    )(docs, key_in, value_in, conv_weight, rims, inside, later_state, keys, values_t)

    def joined(mine, theirs, bit):
        mine = mine.astype(jnp.float32) * factors[2 * bit]
        theirs = theirs.astype(jnp.float32) * factors[2 * bit + 1]
        return (mine + theirs).astype(jnp.bfloat16)

    def near_piece(first_head, piece_heads, buffers, docs):
        extra = [] if buffers is None else list(buffers)
        return pl.pallas_call(
            functools.partial(
                near_kernel,
                first_head=first_head,
                head_count=piece_heads,
                heads=heads,
                skipped=len(extra),
            ),
            in_specs=[smem] + [vmem] * (8 + len(extra)),
            out_specs=[vmem] * 2,
            out_shape=[
                pltpu.VMEM((head_count, row_count, head_size), jnp.bfloat16),
                pltpu.VMEM((head_count, head_size, row_count), jnp.float32),
            ],
            scratch_shapes=[
                pltpu.VMEM((heads, window_rows(row_count), LANES), jnp.float32),
                pltpu.VMEM((heads, tiles, 16, LANES), jnp.float32),
                pltpu.VMEM((heads, row_count, row_count), jnp.bfloat16),
            ],
            input_output_aliases={9: 0, 10: 1} if extra else {},
            compiler_params=limited(6),
            cost_estimate=pl.CostEstimate(
                flops=5_000_000_000, bytes_accessed=35_000_000, transcendentals=300_000
            ),
            name="near",
        )(docs, query_in, rims, conv_weight, inside, table, starts, keys, values_t, *extra)

    def far_piece(group, lower, last_state, previous=None, before=None, out=None, writes_own=False):
        writes = previous or writes_own
        extra = ([before] if previous else []) + ([] if out is None else [out])
        out_type = jax.ShapeDtypeStruct((row_count, width_all), jnp.bfloat16)
        result_type = pltpu.VMEM((row_count, width_all // 4), jnp.bfloat16)
        return pl.pallas_call(
            functools.partial(
                far_skip if out is not None else far_kernel,
                group=group,
                previous=previous,
                writes_own=writes_own,
                dev_bits=dev_bits,
            ),
            in_specs=[vmem] * (8 if previous else 7) + ([] if out is None else [anywhere]),
            out_specs=([anywhere] if writes else []) + ([] if writes_own else [vmem]),
            out_shape=([out_type] if writes else []) + ([] if writes_own else [result_type]),
            scratch_shapes=([result_type] if writes_own else [])
            + ([pltpu.SemaphoreType.DMA((2,))] if writes else []),
            input_output_aliases={} if out is None else {8: 0},
            compiler_params=limited(4),
            cost_estimate=pl.CostEstimate(
                flops=1_000_000, bytes_accessed=10_000, transcendentals=0
            ),
            name="far",
        )(queries, near, table, gains, first_state, lower, last_state, *extra)

    quarter = head_count // 4
    state, docs = lax.optimization_barrier((state, docs))
    first_state = swapped(state, 0)
    table, starts, gains, factors = pl.pallas_call(
        functools.partial(tables_kernel, doc_count=doc_count),
        in_specs=[smem, vmem, vmem],
        out_specs=[vmem] * 4,
        out_shape=[
            pltpu.VMEM((level_count, head_count, row_count), jnp.float32),
            pltpu.VMEM((8, row_count), jnp.int32),
            pltpu.VMEM((head_count, head_size, LANES), jnp.float32),
            pltpu.VMEM((2 * (dev_bits - 1), LANES), jnp.float32),
        ],
        compiler_params=limited(2),
        name="tables",
    )(docs, jnp.transpose(level_weight, (1, 0, 2)), out_gain.reshape(head_count, 1, head_size))
    first_state, table, starts, gains, factors = lax.optimization_barrier(
        (first_state, table, starts, gains, factors)
    )
    half = 2 * quarter
    pair_kept = joined(state[:quarter], first_state[half : half + quarter], 0)
    pair_sent = joined(state[quarter:half], first_state[half + quarter :], 0)

    pair_sent, tied = lax.optimization_barrier((pair_sent, docs))
    pair_in = swapped(pair_sent, 1)
    buffers = near_piece(0, quarter, None, tied)
    pair_in, buffers = lax.optimization_barrier((pair_in, buffers))
    carried = joined(pair_kept, pair_in, 1)

    received = []
    for bit in range(2, dev_bits - 1):
        if bit == 2:
            carried, tied = lax.optimization_barrier((carried, docs))
        arrived = swapped(carried, bit)
        if bit == 2:
            buffers = near_piece(quarter, quarter, buffers, tied)
            arrived, buffers = lax.optimization_barrier((arrived, buffers))
        received.append(arrived)
        carried = joined(carried, arrived, bit)

    mine = jnp.stack([pair_kept] + received)
    carried, mine, tied = lax.optimization_barrier((carried, mine, docs))
    last_own = swapped(carried, dev_bits - 1)
    theirs = swapped(mine, 1)
    buffers = near_piece(2 * quarter, 2 * quarter, buffers, tied)
    last_own, theirs, buffers = lax.optimization_barrier((last_own, theirs, buffers))
    queries, near = buffers
    own = jnp.concatenate([jnp.stack([pair_in] + received), theirs], axis=1)
    own, last_own = lax.optimization_barrier((own, last_own))

    last_next = swapped(last_own, 1)
    other = swapped(own, 0)
    last_other = swapped(last_own, 0)
    (done,) = far_piece((0, 0), own, last_own)
    other, last_other, done = lax.optimization_barrier((other, last_other, done))
    (out,) = far_piece((1, 0), other, last_other, (0, 0), done, writes_own=True)
    last_next, out = lax.optimization_barrier((last_next, out))
    last_far = swapped(last_next, 0)
    (done,) = far_piece((0, 1), own, last_next)
    last_far, out, done = lax.optimization_barrier((last_far, out, done))
    (out,) = far_piece((1, 1), other, last_far, (0, 1), done, out, writes_own=True)
    return out


def solution(mesh):
    in_specs = (
        P(("groups", "seq"), None),
        P(("groups", "seq"), None),
        P(("groups", "seq"), None),
        P(),
        P(None, None, ("groups", "seq")),
        P(),
        P("groups"),
    )
    out_specs = P(("groups", "seq"), None)
    return jax.shard_map(local, mesh=mesh, in_specs=in_specs, out_specs=out_specs, check_vma=False)
```

```python
import functools

import jax
import jax.numpy as jnp
from jax import lax
from jax.experimental import pallas as pl
from jax.experimental.pallas import tpu as pltpu
from jax.sharding import PartitionSpec as P

LANES = 128
GROUP = 16
PITCH = 24
NT = (((1,), (1,)), ((), ()))


def exchange(block, partner):
    count = lax.axis_size("seq")
    route = [(i, partner(i)) for i in range(count) if partner(i) is not None]
    return lax.ppermute(block, "seq", route)


def swapped(block, bit):
    return exchange(block, lambda i: i ^ (1 << bit))


def limited(mebibytes):
    return pltpu.CompilerParams(vmem_limit_bytes=mebibytes * 1024 * 1024)


def start_at(docs_ref, doc_count, positions):
    def step(i, start):
        doc = docs_ref[i]
        return jnp.where(positions >= doc, doc, start)

    return lax.fori_loop(0, doc_count, step, jnp.zeros_like(positions))


def silu_of_twice(half):
    return half + half * jnp.tanh(half)


def logical_place(head, core_bit, y_bit):
    return ((head >> 3) ^ core_bit) * 8 + (((head >> 2) & 1) ^ y_bit) * 4 + (head & 3)


def row_at(place):
    return ((place & 7) << 4) | ((place >> 3) & 15)


def selection(size):
    rows = lax.broadcasted_iota(jnp.int32, (size, size), 0)
    places = lax.broadcasted_iota(jnp.int32, (size, size), 1)
    chosen = rows == (places & -LANES) + row_at(places & (LANES - 1))
    return jnp.where(chosen, 1.0, 0.0).astype(jnp.bfloat16)


def rim_kernel(query_ref, key_ref, value_ref, out_ref, buffer, sems):
    rim_rows = out_ref.shape[0]
    edge, width = buffer.shape[1:]
    copies = []
    for part, ref in enumerate((query_ref, key_ref, value_ref)):
        rows = ref.shape[0]
        copy = pltpu.make_async_copy(
            ref.at[rows - edge : rows, :], buffer.at[part], sems.at[part]
        )
        copy.start()
        copies.append(copy)
    for part, copy in enumerate(copies):
        copy.wait()
        out_ref[:, part * width : (part + 1) * width] = buffer[part, edge - rim_rows : edge, :]


def tables_kernel(
    docs_ref, level_ref, gain_ref, table_ref, start_ref, gain_out_ref, factor_ref, *, doc_count
):
    join_factors(docs_ref, doc_count, level_ref.shape[2], factor_ref)
    level_count, head_count, row_count = level_ref.shape
    tok_bits = row_count.bit_length() - 1
    index = lax.axis_index("seq")
    first_pos = index * row_count
    lanes = lax.broadcasted_iota(jnp.int32, (8, row_count), 1)
    positions = first_pos + (lanes & -LANES) + row_at(lanes & (LANES - 1))
    starts = start_at(docs_ref, doc_count, positions)
    start_ref[...] = starts - first_pos
    starts = jnp.concatenate([starts] * (head_count // 8), axis=0)
    select = selection(LANES)
    levels = level_ref[...].reshape(level_count * head_count, row_count)
    for tile in range(row_count // LANES):
        cols = slice(tile * LANES, (tile + 1) * LANES)
        weights = jnp.dot(levels[:, cols], select, preferred_element_type=jnp.float32)
        for level in range(level_count):
            scaled = weights[level * head_count : (level + 1) * head_count] * 2.0 ** (-level / 2)
            if level > tok_bits:
                bit = level - tok_bits - 1
                limit = jnp.where((index >> bit) & 1 == 1, (index >> bit << bit) * row_count, 0)
                scaled = jnp.where(starts[:, cols] < limit, scaled, 0.0)
            table_ref[level, :, cols] = scaled
    for head in range(head_count):
        gain_out_ref[head] = jnp.broadcast_to(gain_ref[head], (LANES, LANES)).T


def window_rows(row_count):
    return (row_count // GROUP + 1) * PITCH


def fill_rim(window_ref, rim):
    rim_rows = rim.shape[0]
    window_ref[GROUP - 8 : GROUP, :] = jnp.concatenate(
        [jnp.zeros((8 - rim_rows, rim.shape[1]), jnp.float32), rim.astype(jnp.float32)], axis=0
    )


def fill_rows(window_ref, rows, first):
    rows = rows.astype(jnp.float32)
    for start in range(0, rows.shape[0], GROUP):
        place = ((first + start) // GROUP + 1) * PITCH
        window_ref[place : place + GROUP, :] = rows[start : start + GROUP, :]


def convolved(window_ref, taps, inside_ref, tile):
    reach = taps.shape[0] - 1
    base = (tile * (LANES // GROUP) + 1) * PITCH
    places = [base - PITCH + GROUP + i for i in range(-reach, 0)]
    places += [base + i for i in range(GROUP)]
    rows = [window_ref[pl.ds(place, 8, stride=PITCH), :] for place in places]
    summed = None
    for offset in range(reach, -1, -1):
        term = taps[offset : offset + 1, :] * jnp.concatenate(
            rows[reach - offset : reach - offset + 16], axis=0
        )
        summed = term if summed is None else term + summed
        if offset:
            first = (reach - offset) * 8
            summed = summed * inside_ref[tile, first : first + LANES, :]
    return summed


def inside_masks(docs_ref, doc_count, first_pos, inside_ref):
    tiles, places, _ = inside_ref.shape
    ahead = (places - LANES) // 8
    place = lax.broadcasted_iota(jnp.int32, (places, LANES), 0)
    rows = ((place & 7) << 4) + (place >> 3) - ahead
    for tile in range(tiles):
        positions = rows + (first_pos + tile * LANES)

        def step(i, inside):
            return jnp.where(positions == docs_ref[i], 0.0, inside)

        inside_ref[tile] = lax.fori_loop(
            0, doc_count, step, jnp.ones((places, LANES), jnp.float32), unroll=8
        )


def columns(first):
    return pl.ds(pl.multiple_of(first, LANES), LANES)


def key_value_tile(
    taps_ref, inside_ref, key_out_ref, value_out_ref, window_ref, head, slot, tile
):
    width = taps_ref.shape[1] // 3
    places = slice(tile * LANES, (tile + 1) * LANES)
    first = head * LANES
    key_taps = 0.5 * taps_ref[:, columns(width + first)]
    value_taps = 0.5 * taps_ref[:, columns(2 * width + first)]
    grown = silu_of_twice(convolved(window_ref.at[slot], key_taps, inside_ref, tile))
    square = jnp.sum(grown * grown, axis=1, keepdims=True)
    key_out_ref[head, places, :] = (grown * lax.rsqrt(square + 1e-6)).astype(jnp.bfloat16)
    values = silu_of_twice(convolved(window_ref.at[slot + 1], value_taps, inside_ref, tile))
    value_out_ref[head, :, places] = values.T.astype(jnp.bfloat16)


def kept_lanes(docs_ref, doc_count, first_pos, row_count, tiles):
    last_pos = jnp.full((1, len(tiles) * LANES), first_pos + row_count - 1, jnp.int32)
    last_start = start_at(docs_ref, doc_count, last_pos)
    lanes = tiles[0] * LANES + lax.broadcasted_iota(jnp.int32, last_pos.shape, 1)
    lanes_pos = first_pos + (lanes & -LANES) + row_at(lanes & (LANES - 1))
    return jnp.where(lanes_pos >= last_start, 1.0, 0.0).astype(jnp.bfloat16)


def later_rows_kernel(
    docs_ref,
    key_ref,
    value_ref,
    taps_ref,
    key_out_ref,
    value_out_ref,
    state_ref,
    inside_ref,
    window_ref,
    *,
    doc_count,
    heads,
):
    row_count, width = key_ref.shape
    head_count = width // LANES
    tiles = list(range(1, row_count // LANES))
    first_pos = lax.axis_index("seq") * row_count
    keep = kept_lanes(docs_ref, doc_count, first_pos, row_count, tiles)
    inside_masks(docs_ref, doc_count, first_pos, inside_ref)
    ahead = LANES - 16

    def add_state(head):
        state_ref[head] = jnp.dot(
            value_out_ref[head, :, LANES:] * keep,
            key_out_ref[head, LANES:, :],
            preferred_element_type=jnp.float32,
        )

    def group(step):
        for which in range(heads):
            cols = columns((step * heads + which) * LANES)
            fill_rows(window_ref.at[2 * which], key_ref[ahead:, cols], ahead)
            fill_rows(window_ref.at[2 * which + 1], value_ref[ahead:, cols], ahead)
        for tile in tiles:
            for which in range(heads):
                key_value_tile(
                    taps_ref,
                    inside_ref,
                    key_out_ref,
                    value_out_ref,
                    window_ref,
                    step * heads + which,
                    2 * which,
                    tile,
                )

    group(0)

    def body(step, carry):
        for which in range(heads):
            add_state((step - 1) * heads + which)
        group(step)
        return carry

    steps = head_count // heads
    lax.fori_loop(1, steps, body, 0)
    for which in range(heads):
        add_state((steps - 1) * heads + which)


def first_rows_kernel(
    docs_ref,
    key_ref,
    value_ref,
    taps_ref,
    rim_ref,
    inside_ref,
    later_state_ref,
    key_in_ref,
    value_in_ref,
    key_out_ref,
    value_out_ref,
    state_ref,
    window_ref,
    *,
    doc_count,
    row_count,
    heads,
):
    width = key_ref.shape[1]
    head_count = width // LANES
    index = lax.axis_index("seq")
    keep = kept_lanes(docs_ref, doc_count, index * row_count, row_count, [0])

    def add_state(head):
        total = later_state_ref[head] + jnp.dot(
            value_out_ref[head, :, 0:LANES] * keep,
            key_out_ref[head, 0:LANES, :],
            preferred_element_type=jnp.float32,
        )
        place = logical_place(head, index & 1, (index >> 1) & 1)
        state_ref[place] = total.astype(jnp.bfloat16)

    def group(step):
        for which in range(heads):
            first = (step * heads + which) * LANES
            fill_rim(window_ref.at[2 * which], rim_ref[:, columns(width + first)])
            fill_rim(window_ref.at[2 * which + 1], rim_ref[:, columns(2 * width + first)])
            fill_rows(window_ref.at[2 * which], key_ref[0:LANES, columns(first)], 0)
            fill_rows(window_ref.at[2 * which + 1], value_ref[0:LANES, columns(first)], 0)
        for which in range(heads):
            key_value_tile(
                taps_ref,
                inside_ref,
                key_out_ref,
                value_out_ref,
                window_ref,
                step * heads + which,
                2 * which,
                0,
            )

    group(0)

    def body(step, carry):
        for which in range(heads):
            add_state((step - 1) * heads + which)
        group(step)
        return carry

    steps = head_count // heads
    lax.fori_loop(1, steps, body, 0)
    for which in range(heads):
        add_state((steps - 1) * heads + which)


def join_factors(docs_ref, doc_count, row_count, factor_ref):
    index = lax.axis_index("seq")
    for bit in range(factor_ref.shape[0] // 2):
        stride = 1 << bit
        upper_first = (((index >> (bit + 1)) << (bit + 1)) + stride) * row_count

        def step(i, found):
            gap = docs_ref[i] - upper_first
            return jnp.where((gap >= 0) & (gap < stride * row_count), 1, found)

        upper_has = lax.fori_loop(0, doc_count, step, jnp.int32(0), unroll=8)
        is_upper = (index >> bit) & 1
        keep_mine = jnp.where((upper_has == 1) & (is_upper == 0), 0.0, 1.0)
        keep_theirs = jnp.where((upper_has == 1) & (is_upper == 1), 0.0, 1.0)
        factor_ref[2 * bit : 2 * bit + 1, :] = jnp.full((1, LANES), keep_mine, jnp.float32)
        factor_ref[2 * bit + 1 : 2 * bit + 2, :] = jnp.full((1, LANES), keep_theirs, jnp.float32)


def near_kernel(
    docs_ref,
    query_ref,
    rim_ref,
    taps_ref,
    inside_ref,
    table_ref,
    start_ref,
    key_ref,
    value_ref,
    *rest,
    first_head,
    head_count,
    heads,
    skipped,
):
    query_out_ref, near_ref, window_ref, fine_ref, pair_ref = rest[skipped:]
    row_count = query_ref.shape[0]
    tiles = row_count // LANES
    span = 2 * LANES
    sub = lax.broadcasted_iota(jnp.int32, (8, row_count), 0)
    lane = lax.broadcasted_iota(jnp.int32, (8, row_count), 1)
    high = sub ^ (lane & 7)
    sub16 = lax.broadcasted_iota(jnp.int32, (16, row_count), 0)
    low_row = (lax.broadcasted_iota(jnp.int32, (16, row_count), 1) >> 3) & 15
    low = sub16 ^ low_row
    same_group = lax.broadcasted_iota(jnp.int32, (8, LANES), 0) == (
        lax.broadcasted_iota(jnp.int32, (8, LANES), 1) & 7
    )
    key_row = row_at(lax.broadcasted_iota(jnp.int32, (LANES, LANES), 0))

    def group(step, carry):
        for which in range(heads):
            head = first_head + step * heads + which
            fill_rim(window_ref.at[which], rim_ref[:, columns(head * LANES)])
            fill_rows(window_ref.at[which], query_ref[:, columns(head * LANES)], 0)

        for which in range(heads):
            head = first_head + step * heads + which
            taps = 0.5 * taps_ref[:, columns(head * LANES)]
            for tile in range(tiles):
                grown = silu_of_twice(convolved(window_ref.at[which], taps, inside_ref, tile))
                query_out_ref[head, tile * LANES : (tile + 1) * LANES, :] = grown.astype(
                    jnp.bfloat16
                )

        for which in range(heads):
            head = first_head + step * heads + which
            tok_bits = row_count.bit_length() - 1
            scaled = [table_ref[level, pl.ds(head, 1), :] for level in range(tok_bits + 1)]
            coarse = jnp.where(high < 2, scaled[5], jnp.where(high < 4, scaled[6], scaled[7]))
            coarse = jnp.where(sub > (lane & 7), 0.0, coarse)
            fine = jnp.where(
                low == 0,
                scaled[0],
                jnp.where(
                    low == 1,
                    scaled[1],
                    jnp.where(low < 4, scaled[2], jnp.where(low < 8, scaled[3], scaled[4])),
                ),
            )
            fine = jnp.where(sub16 > low_row, 0.0, fine)
            for tile in range(tiles):
                fine_ref[which, tile, 0:16, :] = fine[:, tile * LANES : (tile + 1) * LANES]
            for part in range(row_count // span):
                rows = (part + 1) * span
                scores = lax.dot_general(
                    key_ref[head, 0:rows, :],
                    query_out_ref[head, part * span : rows, :],
                    NT,
                    preferred_element_type=jnp.float32,
                )
                for side in range(2):
                    tile = 2 * part + side
                    cols = slice(tile * LANES, (tile + 1) * LANES)
                    starts = start_ref[0:1, cols]
                    for other in range(tile + 1):
                        if other == tile:
                            weight = jnp.concatenate(
                                [
                                    jnp.where(
                                        same_group,
                                        fine_ref[which, tile, pl.ds(a, 8, stride=0), :],
                                        coarse[:, cols],
                                    )
                                    for a in range(16)
                                ],
                                axis=0,
                            )
                        else:
                            weight = scaled[7 + (tile ^ other).bit_length()][:, cols]
                        piece = scores[
                            other * LANES : (other + 1) * LANES,
                            side * LANES : (side + 1) * LANES,
                        ]
                        valid = key_row >= starts - other * LANES
                        pair_ref[which, other * LANES : (other + 1) * LANES, cols] = jnp.where(
                            valid, piece * weight, 0.0
                        ).astype(jnp.bfloat16)
                    if side == 0:
                        pair_ref[which, (tile + 1) * LANES : rows, cols] = jnp.zeros(
                            (LANES, LANES), jnp.bfloat16
                        )
                near_ref[head, :, part * span : rows] = jnp.dot(
                    value_ref[head, :, 0:rows],
                    pair_ref[which, 0:rows, part * span : rows],
                    preferred_element_type=jnp.float32,
                )
        return carry

    lax.fori_loop(0, head_count // heads, group, 0)


def far_kernel(
    query_ref,
    near_ref,
    table_ref,
    gain_ref,
    first_state_ref,
    lower_ref,
    last_ref,
    *rest,
    group,
    previous,
    writes_own,
    dev_bits,
):
    head_count, row_count, _ = query_ref.shape
    quarter = head_count // 4
    wide = quarter * LANES
    span = 2 * LANES
    index = lax.axis_index("seq")
    core_bit = index & 1
    y_bit = (index >> 1) & 1
    tok_bits = row_count.bit_length() - 1

    def first_head_of(group):
        other_half, other_quarter = group
        return (core_bit ^ other_half) * 2 * quarter + (y_bit ^ other_quarter) * quarter

    def copy_out(result_ref, group, sem):
        cols = pl.ds(pl.multiple_of(first_head_of(group) * LANES, wide), wide)
        return pltpu.make_async_copy(result_ref, out_hbm_ref.at[:, cols], sem)

    rest = list(rest)
    previous_ref = rest.pop(0) if previous else None
    sems = rest.pop() if previous or writes_own else None
    result_ref = rest.pop()
    out_hbm_ref = rest.pop() if previous or writes_own else None
    copies = [copy_out(previous_ref, previous, sems.at[0])] if previous else []
    for copy in copies:
        copy.start()

    first_head = first_head_of(group)
    select = selection(span)
    finished = []
    for local_head in range(quarter):
        head = first_head + local_head
        first_place = logical_place(head, 1 - core_bit, y_bit)
        place = logical_place(head, core_bit, y_bit) & 7
        states = [first_state_ref[first_place]]
        for level in range(dev_bits - 2):
            states.append(lower_ref[level, place])
        states.append(last_ref[local_head])
        images = lax.dot_general(
            jnp.concatenate(states, axis=0),
            query_ref[head],
            NT,
            preferred_element_type=jnp.float32,
        )
        summed = near_ref[head]
        for bit in range(dev_bits):
            coef = table_ref[tok_bits + 1 + bit, pl.ds(head, 1), :]
            summed = summed + coef * images[bit * LANES : (bit + 1) * LANES, :]
        mean = jnp.mean(summed * summed, axis=0, keepdims=True)
        normed = summed * lax.rsqrt(mean + 1e-6)
        gain = jnp.concatenate([gain_ref[head]] * (row_count // LANES), axis=1)
        finished.append((normed * gain).astype(jnp.bfloat16))
        if local_head % 2 == 1:
            both = jnp.concatenate(finished[-2:], axis=0)
            cols = slice((local_head - 1) * LANES, (local_head + 1) * LANES)
            for first in range(0, row_count, span):
                turned = lax.dot_general(
                    select, both[:, first : first + span], NT, preferred_element_type=jnp.float32
                )
                result_ref[first : first + span, cols] = turned.astype(jnp.bfloat16)
    if writes_own:
        copies.append(copy_out(result_ref, group, sems.at[1]))
        copies[-1].start()
    for copy in copies:
        copy.wait()


def far_skip(*refs, **settings):
    far_kernel(*refs[:8], *refs[9:], **settings)


def local(query_in, key_in, value_in, conv_weight, level_weight, out_gain, doc_starts):
    row_count, width_all = query_in.shape
    head_count, level_count, _ = level_weight.shape
    head_size = width_all // head_count
    conv_width = conv_weight.shape[0]
    doc_count = doc_starts.shape[0]
    dev_index = lax.axis_index("seq")
    dev_count = lax.axis_size("seq")
    dev_bits = dev_count.bit_length() - 1
    rim_rows = conv_width - 1
    tiles = row_count // LANES
    smem = pl.BlockSpec(memory_space=pltpu.SMEM)
    vmem = pl.BlockSpec(memory_space=pltpu.VMEM)
    anywhere = pl.BlockSpec(memory_space=pl.ANY)

    tails = pl.pallas_call(
        rim_kernel,
        in_specs=[pl.BlockSpec(memory_space=pltpu.HBM)] * 3,
        out_specs=vmem,
        out_shape=pltpu.VMEM((rim_rows, 3 * width_all), query_in.dtype),
        scratch_shapes=[
            pltpu.VMEM((3, 16, width_all), query_in.dtype),
            pltpu.SemaphoreType.DMA((3,)),
        ],
        compiler_params=limited(1),
        name="rim",
    )(*(pltpu.with_memory_space_constraint(x, pltpu.HBM) for x in (query_in, key_in, value_in)))
    tails, docs = lax.optimization_barrier((tails, doc_starts))
    rims = exchange(tails, lambda i: i + 1 if i + 1 < dev_count else None)
    heads = 4
    keys, values_t, later_state, inside = pl.pallas_call(
        functools.partial(later_rows_kernel, doc_count=doc_count, heads=2 * heads),
        in_specs=[smem] + [vmem] * 3,
        out_specs=[vmem] * 4,
        out_shape=[
            pltpu.VMEM((head_count, row_count, head_size), jnp.bfloat16),
            pltpu.VMEM((head_count, head_size, row_count), jnp.bfloat16),
            pltpu.VMEM((head_count, head_size, head_size), jnp.float32),
            pltpu.VMEM((tiles, LANES + 8 * (rim_rows - 1), LANES), jnp.float32),
        ],
        scratch_shapes=[pltpu.VMEM((4 * heads, window_rows(row_count), LANES), jnp.float32)],
        compiler_params=limited(14),
        cost_estimate=pl.CostEstimate(
            flops=500_000_000, bytes_accessed=4_000_000, transcendentals=1_500_000
        ),
        name="later_rows",
    )(docs, key_in, value_in, conv_weight)
    rims, keys, values_t, later_state = lax.optimization_barrier(
        (rims, keys, values_t, later_state)
    )
    keys, values_t, state = pl.pallas_call(
        functools.partial(
            first_rows_kernel, doc_count=doc_count, row_count=row_count, heads=2 * heads
        ),
        in_specs=[smem] + [vmem] * 8,
        out_specs=[vmem] * 3,
        out_shape=[
            pltpu.VMEM((head_count, row_count, head_size), jnp.bfloat16),
            pltpu.VMEM((head_count, head_size, row_count), jnp.bfloat16),
            pltpu.VMEM((head_count, head_size, head_size), jnp.bfloat16),
        ],
        scratch_shapes=[pltpu.VMEM((4 * heads, window_rows(LANES), LANES), jnp.float32)],
        input_output_aliases={7: 0, 8: 1},
        compiler_params=limited(6),
        name="first_rows",
    )(docs, key_in, value_in, conv_weight, rims, inside, later_state, keys, values_t)

    def joined(mine, theirs, bit):
        mine = mine.astype(jnp.float32) * factors[2 * bit]
        theirs = theirs.astype(jnp.float32) * factors[2 * bit + 1]
        return (mine + theirs).astype(jnp.bfloat16)

    def near_piece(first_head, piece_heads, buffers, docs):
        heads = piece_heads
        extra = [] if buffers is None else list(buffers)
        return pl.pallas_call(
            functools.partial(
                near_kernel,
                first_head=first_head,
                head_count=piece_heads,
                heads=heads,
                skipped=len(extra),
            ),
            in_specs=[smem] + [vmem] * (8 + len(extra)),
            out_specs=[vmem] * 2,
            out_shape=[
                pltpu.VMEM((head_count, row_count, head_size), jnp.bfloat16),
                pltpu.VMEM((head_count, head_size, row_count), jnp.float32),
            ],
            scratch_shapes=[
                pltpu.VMEM((heads, window_rows(row_count), LANES), jnp.float32),
                pltpu.VMEM((heads, tiles, 24, LANES), jnp.float32),
                pltpu.VMEM((heads, row_count, row_count), jnp.bfloat16),
            ],
            input_output_aliases={9: 0, 10: 1} if extra else {},
            compiler_params=limited(10),
            cost_estimate=pl.CostEstimate(
                flops=5_000_000_000, bytes_accessed=35_000_000, transcendentals=300_000
            ),
            name="near",
        )(docs, query_in, rims, conv_weight, inside, table, starts, keys, values_t, *extra)

    def far_piece(group, lower, last_state, previous=None, before=None, out=None, writes_own=False):
        writes = previous or writes_own
        extra = ([before] if previous else []) + ([] if out is None else [out])
        out_type = jax.ShapeDtypeStruct((row_count, width_all), jnp.bfloat16)
        result_type = pltpu.VMEM((row_count, width_all // 4), jnp.bfloat16)
        return pl.pallas_call(
            functools.partial(
                far_skip if out is not None else far_kernel,
                group=group,
                previous=previous,
                writes_own=writes_own,
                dev_bits=dev_bits,
            ),
            in_specs=[vmem] * (8 if previous else 7) + ([] if out is None else [anywhere]),
            out_specs=([anywhere] if writes else []) + ([] if writes_own else [vmem]),
            out_shape=([out_type] if writes else []) + ([] if writes_own else [result_type]),
            scratch_shapes=([result_type] if writes_own else [])
            + ([pltpu.SemaphoreType.DMA((2,))] if writes else []),
            input_output_aliases={} if out is None else {8: 0},
            compiler_params=limited(4),
            cost_estimate=pl.CostEstimate(
                flops=5_000_000_000, bytes_accessed=35_000_000, transcendentals=0
            ),
            name="far",
        )(queries, near, table, gains, first_state, lower, last_state, *extra)

    quarter = head_count // 4
    state, docs = lax.optimization_barrier((state, docs))
    first_state = swapped(state, 0)
    table, starts, gains, factors = pl.pallas_call(
        functools.partial(tables_kernel, doc_count=doc_count),
        in_specs=[smem, vmem, vmem],
        out_specs=[vmem] * 4,
        out_shape=[
            pltpu.VMEM((level_count, head_count, row_count), jnp.float32),
            pltpu.VMEM((8, row_count), jnp.int32),
            pltpu.VMEM((head_count, head_size, LANES), jnp.float32),
            pltpu.VMEM((2 * (dev_bits - 1), LANES), jnp.float32),
        ],
        compiler_params=limited(2),
        name="tables",
    )(docs, jnp.transpose(level_weight, (1, 0, 2)), out_gain.reshape(head_count, 1, head_size))
    first_state, table, starts, gains, factors = lax.optimization_barrier(
        (first_state, table, starts, gains, factors)
    )
    half = 2 * quarter
    pair_kept = joined(state[:quarter], first_state[half : half + quarter], 0)
    pair_sent = joined(state[quarter:half], first_state[half + quarter :], 0)

    pair_sent, tied = lax.optimization_barrier((pair_sent, docs))
    pair_in = swapped(pair_sent, 1)
    buffers = near_piece(0, quarter, None, tied)
    pair_in, buffers = lax.optimization_barrier((pair_in, buffers))
    carried = joined(pair_kept, pair_in, 1)

    received = []
    for bit in range(2, dev_bits - 1):
        if bit == 2:
            carried, tied = lax.optimization_barrier((carried, docs))
        arrived = swapped(carried, bit)
        if bit == 2:
            buffers = near_piece(quarter, quarter, buffers, tied)
            arrived, buffers = lax.optimization_barrier((arrived, buffers))
        received.append(arrived)
        carried = joined(carried, arrived, bit)

    mine = jnp.stack([pair_kept] + received)
    carried, mine, tied = lax.optimization_barrier((carried, mine, docs))
    last_own = swapped(carried, dev_bits - 1)
    theirs = swapped(mine, 1)
    buffers = near_piece(2 * quarter, 2 * quarter, buffers, tied)
    last_own, theirs, buffers = lax.optimization_barrier((last_own, theirs, buffers))
    queries, near = buffers
    own = jnp.concatenate([jnp.stack([pair_in] + received), theirs], axis=1)
    own, last_own = lax.optimization_barrier((own, last_own))

    last_next = swapped(last_own, 1)
    other = swapped(own, 0)
    last_other = swapped(last_own, 0)
    (done,) = far_piece((0, 0), own, last_own)
    other, last_other, done = lax.optimization_barrier((other, last_other, done))
    (out,) = far_piece((1, 0), other, last_other, (0, 0), done, writes_own=True)
    last_next, out = lax.optimization_barrier((last_next, out))
    last_far = swapped(last_next, 0)
    (done,) = far_piece((0, 1), own, last_next)
    last_far, out, done = lax.optimization_barrier((last_far, out, done))
    (out,) = far_piece((1, 1), other, last_far, (0, 1), done, out, writes_own=True)
    return out


def solution(mesh):
    in_specs = (
        P(("groups", "seq"), None),
        P(("groups", "seq"), None),
        P(("groups", "seq"), None),
        P(),
        P(None, None, ("groups", "seq")),
        P(),
        P("groups"),
    )
    out_specs = P(("groups", "seq"), None)
    return jax.shard_map(local, mesh=mesh, in_specs=in_specs, out_specs=out_specs, check_vma=False)
```

```python
import functools

import jax
import jax.numpy as jnp
from jax import lax
from jax.experimental import pallas as pl
from jax.experimental.pallas import tpu as pltpu
from jax.sharding import PartitionSpec as P

LANES = 128
GROUP = 16
PITCH = 24
NT = (((1,), (1,)), ((), ()))


def exchange(block, partner):
    count = lax.axis_size("seq")
    route = [(i, partner(i)) for i in range(count) if partner(i) is not None]
    return lax.ppermute(block, "seq", route)


def swapped(block, bit):
    return exchange(block, lambda i: i ^ (1 << bit))


def limited(mebibytes):
    return pltpu.CompilerParams(vmem_limit_bytes=mebibytes * 1024 * 1024)


def start_at(docs_ref, doc_count, positions):
    def step(i, start):
        doc = docs_ref[i]
        return jnp.where(positions >= doc, doc, start)

    return lax.fori_loop(0, doc_count, step, jnp.zeros_like(positions))


def silu_of_twice(half):
    return half + half * jnp.tanh(half)


def logical_place(head, core_bit, y_bit):
    return ((head >> 3) ^ core_bit) * 8 + (((head >> 2) & 1) ^ y_bit) * 4 + (head & 3)


def row_at(place):
    return ((place & 7) << 4) | ((place >> 3) & 15)


def selection(size):
    rows = lax.broadcasted_iota(jnp.int32, (size, size), 0)
    places = lax.broadcasted_iota(jnp.int32, (size, size), 1)
    chosen = rows == (places & -LANES) + row_at(places & (LANES - 1))
    return jnp.where(chosen, 1.0, 0.0).astype(jnp.bfloat16)


def rim_kernel(query_ref, key_ref, value_ref, out_ref, buffer, sems):
    rim_rows = out_ref.shape[0]
    edge, width = buffer.shape[1:]
    copies = []
    for part, ref in enumerate((query_ref, key_ref, value_ref)):
        rows = ref.shape[0]
        copy = pltpu.make_async_copy(
            ref.at[rows - edge : rows, :], buffer.at[part], sems.at[part]
        )
        copy.start()
        copies.append(copy)
    for part, copy in enumerate(copies):
        copy.wait()
        out_ref[:, part * width : (part + 1) * width] = buffer[part, edge - rim_rows : edge, :]


def tables_kernel(
    docs_ref, level_ref, gain_ref, table_ref, start_ref, gain_out_ref, factor_ref, *, doc_count
):
    join_factors(docs_ref, doc_count, level_ref.shape[2], factor_ref)
    level_count, head_count, row_count = level_ref.shape
    tok_bits = row_count.bit_length() - 1
    index = lax.axis_index("seq")
    first_pos = index * row_count
    lanes = lax.broadcasted_iota(jnp.int32, (8, row_count), 1)
    positions = first_pos + (lanes & -LANES) + row_at(lanes & (LANES - 1))
    starts = start_at(docs_ref, doc_count, positions)
    start_ref[...] = starts - first_pos
    starts = jnp.concatenate([starts] * (head_count // 8), axis=0)
    select = selection(LANES)
    levels = level_ref[...].reshape(level_count * head_count, row_count)
    for tile in range(row_count // LANES):
        cols = slice(tile * LANES, (tile + 1) * LANES)
        weights = jnp.dot(levels[:, cols], select, preferred_element_type=jnp.float32)
        for level in range(level_count):
            scaled = weights[level * head_count : (level + 1) * head_count] * 2.0 ** (-level / 2)
            if level > tok_bits:
                bit = level - tok_bits - 1
                limit = jnp.where((index >> bit) & 1 == 1, (index >> bit << bit) * row_count, 0)
                scaled = jnp.where(starts[:, cols] < limit, scaled, 0.0)
            table_ref[level, :, cols] = scaled
    for head in range(head_count):
        gain_out_ref[head] = jnp.broadcast_to(gain_ref[head], (LANES, LANES)).T


def window_rows(row_count):
    return (row_count // GROUP + 1) * PITCH


def fill_rim(window_ref, rim):
    rim_rows = rim.shape[0]
    window_ref[GROUP - 8 : GROUP, :] = jnp.concatenate(
        [jnp.zeros((8 - rim_rows, rim.shape[1]), jnp.float32), rim.astype(jnp.float32)], axis=0
    )


def fill_rows(window_ref, rows, first):
    rows = rows.astype(jnp.float32)
    for start in range(0, rows.shape[0], GROUP):
        place = ((first + start) // GROUP + 1) * PITCH
        window_ref[place : place + GROUP, :] = rows[start : start + GROUP, :]


def convolved(window_ref, taps, inside_ref, tile):
    reach = taps.shape[0] - 1
    base = (tile * (LANES // GROUP) + 1) * PITCH
    places = [base - PITCH + GROUP + i for i in range(-reach, 0)]
    places += [base + i for i in range(GROUP)]
    rows = [window_ref[pl.ds(place, 8, stride=PITCH), :] for place in places]
    summed = None
    for offset in range(reach, -1, -1):
        term = taps[offset : offset + 1, :] * jnp.concatenate(
            rows[reach - offset : reach - offset + 16], axis=0
        )
        summed = term if summed is None else term + summed
        if offset:
            first = (reach - offset) * 8
            summed = summed * inside_ref[tile, first : first + LANES, :]
    return summed


def inside_masks(docs_ref, doc_count, first_pos, inside_ref):
    tiles, places, _ = inside_ref.shape
    ahead = (places - LANES) // 8
    place = lax.broadcasted_iota(jnp.int32, (places, LANES), 0)
    rows = ((place & 7) << 4) + (place >> 3) - ahead
    for tile in range(tiles):
        positions = rows + (first_pos + tile * LANES)

        def step(i, inside):
            return jnp.where(positions == docs_ref[i], 0.0, inside)

        inside_ref[tile] = lax.fori_loop(
            0, doc_count, step, jnp.ones((places, LANES), jnp.float32), unroll=8
        )


def columns(first):
    return pl.ds(pl.multiple_of(first, LANES), LANES)


def key_value_tile(
    taps_ref, inside_ref, key_out_ref, value_out_ref, window_ref, head, slot, tile
):
    width = taps_ref.shape[1] // 3
    places = slice(tile * LANES, (tile + 1) * LANES)
    first = head * LANES
    key_taps = 0.5 * taps_ref[:, columns(width + first)]
    value_taps = 0.5 * taps_ref[:, columns(2 * width + first)]
    grown = silu_of_twice(convolved(window_ref.at[slot], key_taps, inside_ref, tile))
    square = jnp.sum(grown * grown, axis=1, keepdims=True)
    key_out_ref[head, places, :] = (grown * lax.rsqrt(square + 1e-6)).astype(jnp.bfloat16)
    values = silu_of_twice(convolved(window_ref.at[slot + 1], value_taps, inside_ref, tile))
    value_out_ref[head, :, places] = values.T.astype(jnp.bfloat16)


def kept_lanes(docs_ref, doc_count, first_pos, row_count, tiles):
    last_pos = jnp.full((1, len(tiles) * LANES), first_pos + row_count - 1, jnp.int32)
    last_start = start_at(docs_ref, doc_count, last_pos)
    lanes = tiles[0] * LANES + lax.broadcasted_iota(jnp.int32, last_pos.shape, 1)
    lanes_pos = first_pos + (lanes & -LANES) + row_at(lanes & (LANES - 1))
    return jnp.where(lanes_pos >= last_start, 1.0, 0.0).astype(jnp.bfloat16)


def later_rows_kernel(
    docs_ref,
    key_ref,
    value_ref,
    taps_ref,
    key_out_ref,
    value_out_ref,
    state_ref,
    inside_ref,
    window_ref,
    *,
    doc_count,
    heads,
):
    row_count, width = key_ref.shape
    head_count = width // LANES
    tiles = list(range(1, row_count // LANES))
    first_pos = lax.axis_index("seq") * row_count
    keep = kept_lanes(docs_ref, doc_count, first_pos, row_count, tiles)
    inside_masks(docs_ref, doc_count, first_pos, inside_ref)
    ahead = LANES - 16

    def add_state(head):
        state_ref[head] = jnp.dot(
            value_out_ref[head, :, LANES:] * keep,
            key_out_ref[head, LANES:, :],
            preferred_element_type=jnp.float32,
        )

    def group(step):
        for which in range(heads):
            cols = columns((step * heads + which) * LANES)
            fill_rows(window_ref.at[2 * which], key_ref[ahead:, cols], ahead)
            fill_rows(window_ref.at[2 * which + 1], value_ref[ahead:, cols], ahead)
        for tile in tiles:
            for which in range(heads):
                key_value_tile(
                    taps_ref,
                    inside_ref,
                    key_out_ref,
                    value_out_ref,
                    window_ref,
                    step * heads + which,
                    2 * which,
                    tile,
                )

    group(0)

    def body(step, carry):
        for which in range(heads):
            add_state((step - 1) * heads + which)
        group(step)
        return carry

    steps = head_count // heads
    lax.fori_loop(1, steps, body, 0)
    for which in range(heads):
        add_state((steps - 1) * heads + which)


def first_rows_kernel(
    docs_ref,
    key_ref,
    value_ref,
    taps_ref,
    rim_ref,
    inside_ref,
    later_state_ref,
    key_in_ref,
    value_in_ref,
    key_out_ref,
    value_out_ref,
    state_ref,
    window_ref,
    *,
    doc_count,
    row_count,
    heads,
):
    width = key_ref.shape[1]
    head_count = width // LANES
    index = lax.axis_index("seq")
    keep = kept_lanes(docs_ref, doc_count, index * row_count, row_count, [0])

    def add_state(head):
        total = later_state_ref[head] + jnp.dot(
            value_out_ref[head, :, 0:LANES] * keep,
            key_out_ref[head, 0:LANES, :],
            preferred_element_type=jnp.float32,
        )
        place = logical_place(head, index & 1, (index >> 1) & 1)
        state_ref[place] = total.astype(jnp.bfloat16)

    def group(step):
        for which in range(heads):
            first = (step * heads + which) * LANES
            fill_rim(window_ref.at[2 * which], rim_ref[:, columns(width + first)])
            fill_rim(window_ref.at[2 * which + 1], rim_ref[:, columns(2 * width + first)])
            fill_rows(window_ref.at[2 * which], key_ref[0:LANES, columns(first)], 0)
            fill_rows(window_ref.at[2 * which + 1], value_ref[0:LANES, columns(first)], 0)
        for which in range(heads):
            key_value_tile(
                taps_ref,
                inside_ref,
                key_out_ref,
                value_out_ref,
                window_ref,
                step * heads + which,
                2 * which,
                0,
            )

    group(0)

    def body(step, carry):
        for which in range(heads):
            add_state((step - 1) * heads + which)
        group(step)
        return carry

    steps = head_count // heads
    lax.fori_loop(1, steps, body, 0)
    for which in range(heads):
        add_state((steps - 1) * heads + which)


def join_factors(docs_ref, doc_count, row_count, factor_ref):
    index = lax.axis_index("seq")
    for bit in range(factor_ref.shape[0] // 2):
        stride = 1 << bit
        upper_first = (((index >> (bit + 1)) << (bit + 1)) + stride) * row_count

        def step(i, found):
            gap = docs_ref[i] - upper_first
            return jnp.where((gap >= 0) & (gap < stride * row_count), 1, found)

        upper_has = lax.fori_loop(0, doc_count, step, jnp.int32(0), unroll=8)
        is_upper = (index >> bit) & 1
        keep_mine = jnp.where((upper_has == 1) & (is_upper == 0), 0.0, 1.0)
        keep_theirs = jnp.where((upper_has == 1) & (is_upper == 1), 0.0, 1.0)
        factor_ref[2 * bit : 2 * bit + 1, :] = jnp.full((1, LANES), keep_mine, jnp.float32)
        factor_ref[2 * bit + 1 : 2 * bit + 2, :] = jnp.full((1, LANES), keep_theirs, jnp.float32)


def near_kernel(
    docs_ref,
    query_ref,
    rim_ref,
    taps_ref,
    inside_ref,
    table_ref,
    start_ref,
    key_ref,
    value_ref,
    *rest,
    first_head,
    head_count,
    heads,
    skipped,
):
    query_out_ref, near_ref, window_ref, fine_ref, pair_ref = rest[skipped:]
    row_count = query_ref.shape[0]
    tiles = row_count // LANES
    span = 2 * LANES
    sub = lax.broadcasted_iota(jnp.int32, (8, row_count), 0)
    lane = lax.broadcasted_iota(jnp.int32, (8, row_count), 1)
    high = sub ^ (lane & 7)
    sub16 = lax.broadcasted_iota(jnp.int32, (16, row_count), 0)
    low_row = (lax.broadcasted_iota(jnp.int32, (16, row_count), 1) >> 3) & 15
    low = sub16 ^ low_row
    same_group = lax.broadcasted_iota(jnp.int32, (8, LANES), 0) == (
        lax.broadcasted_iota(jnp.int32, (8, LANES), 1) & 7
    )
    key_row = row_at(lax.broadcasted_iota(jnp.int32, (LANES, LANES), 0))

    def group(step, carry):
        for which in range(heads):
            head = first_head + step * heads + which
            fill_rim(window_ref.at[which], rim_ref[:, columns(head * LANES)])
            fill_rows(window_ref.at[which], query_ref[:, columns(head * LANES)], 0)

        for which in range(heads):
            head = first_head + step * heads + which
            taps = 0.5 * taps_ref[:, columns(head * LANES)]
            for tile in range(tiles):
                grown = silu_of_twice(convolved(window_ref.at[which], taps, inside_ref, tile))
                query_out_ref[head, tile * LANES : (tile + 1) * LANES, :] = grown.astype(
                    jnp.bfloat16
                )

        for which in range(heads):
            head = first_head + step * heads + which
            tok_bits = row_count.bit_length() - 1
            scaled = [table_ref[level, pl.ds(head, 1), :] for level in range(tok_bits + 1)]
            coarse = jnp.where(high < 2, scaled[5], jnp.where(high < 4, scaled[6], scaled[7]))
            coarse = jnp.where(sub > (lane & 7), 0.0, coarse)
            fine = jnp.where(
                low == 0,
                scaled[0],
                jnp.where(
                    low == 1,
                    scaled[1],
                    jnp.where(low < 4, scaled[2], jnp.where(low < 8, scaled[3], scaled[4])),
                ),
            )
            fine = jnp.where(sub16 > low_row, 0.0, fine)
            for tile in range(tiles):
                fine_ref[which, tile, 0:16, :] = fine[:, tile * LANES : (tile + 1) * LANES]
            for part in range(row_count // span):
                rows = (part + 1) * span
                scores = lax.dot_general(
                    key_ref[head, 0:rows, :],
                    query_out_ref[head, part * span : rows, :],
                    NT,
                    preferred_element_type=jnp.float32,
                )
                for side in range(2):
                    tile = 2 * part + side
                    cols = slice(tile * LANES, (tile + 1) * LANES)
                    starts = start_ref[0:1, cols]
                    for other in range(tile + 1):
                        if other == tile:
                            weight = jnp.concatenate(
                                [
                                    jnp.where(
                                        same_group,
                                        fine_ref[which, tile, pl.ds(a, 8, stride=0), :],
                                        coarse[:, cols],
                                    )
                                    for a in range(16)
                                ],
                                axis=0,
                            )
                        else:
                            weight = scaled[7 + (tile ^ other).bit_length()][:, cols]
                        piece = scores[
                            other * LANES : (other + 1) * LANES,
                            side * LANES : (side + 1) * LANES,
                        ]
                        valid = key_row >= starts - other * LANES
                        pair_ref[which, other * LANES : (other + 1) * LANES, cols] = jnp.where(
                            valid, piece * weight, 0.0
                        ).astype(jnp.bfloat16)
                    if side == 0:
                        pair_ref[which, (tile + 1) * LANES : rows, cols] = jnp.zeros(
                            (LANES, LANES), jnp.bfloat16
                        )
                near_ref[head, :, part * span : rows] = jnp.dot(
                    value_ref[head, :, 0:rows],
                    pair_ref[which, 0:rows, part * span : rows],
                    preferred_element_type=jnp.float32,
                )
        return carry

    lax.fori_loop(0, head_count // heads, group, 0)


def far_kernel(
    query_ref,
    near_ref,
    table_ref,
    gain_ref,
    first_state_ref,
    lower_ref,
    last_ref,
    *rest,
    group,
    previous,
    writes_own,
    dev_bits,
):
    head_count, row_count, _ = query_ref.shape
    quarter = head_count // 4
    wide = quarter * LANES
    span = 2 * LANES
    index = lax.axis_index("seq")
    core_bit = index & 1
    y_bit = (index >> 1) & 1
    tok_bits = row_count.bit_length() - 1

    def first_head_of(group):
        other_half, other_quarter = group
        return (core_bit ^ other_half) * 2 * quarter + (y_bit ^ other_quarter) * quarter

    def copy_out(result_ref, group, sem):
        cols = pl.ds(pl.multiple_of(first_head_of(group) * LANES, wide), wide)
        return pltpu.make_async_copy(result_ref, out_hbm_ref.at[:, cols], sem)

    rest = list(rest)
    previous_ref = rest.pop(0) if previous else None
    sems = rest.pop() if previous or writes_own else None
    result_ref = rest.pop()
    out_hbm_ref = rest.pop() if previous or writes_own else None
    copies = [copy_out(previous_ref, previous, sems.at[0])] if previous else []
    for copy in copies:
        copy.start()

    first_head = first_head_of(group)
    select = selection(span)
    finished = []
    for local_head in range(quarter):
        head = first_head + local_head
        first_place = logical_place(head, 1 - core_bit, y_bit)
        place = logical_place(head, core_bit, y_bit) & 7
        states = [first_state_ref[first_place]]
        for level in range(dev_bits - 2):
            states.append(lower_ref[level, place])
        states.append(last_ref[local_head])
        images = lax.dot_general(
            jnp.concatenate(states, axis=0),
            query_ref[head],
            NT,
            preferred_element_type=jnp.float32,
        )
        summed = near_ref[head]
        for bit in range(dev_bits):
            coef = table_ref[tok_bits + 1 + bit, pl.ds(head, 1), :]
            summed = summed + coef * images[bit * LANES : (bit + 1) * LANES, :]
        mean = jnp.mean(summed * summed, axis=0, keepdims=True)
        normed = summed * lax.rsqrt(mean + 1e-6)
        gain = jnp.concatenate([gain_ref[head]] * (row_count // LANES), axis=1)
        finished.append((normed * gain).astype(jnp.bfloat16))
        if local_head % 2 == 1:
            both = jnp.concatenate(finished[-2:], axis=0)
            cols = slice((local_head - 1) * LANES, (local_head + 1) * LANES)
            for first in range(0, row_count, span):
                turned = lax.dot_general(
                    select, both[:, first : first + span], NT, preferred_element_type=jnp.float32
                )
                result_ref[first : first + span, cols] = turned.astype(jnp.bfloat16)
    if writes_own:
        copies.append(copy_out(result_ref, group, sems.at[1]))
        copies[-1].start()
    for copy in copies:
        copy.wait()


def far_skip(*refs, **settings):
    far_kernel(*refs[:8], *refs[9:], **settings)


def local(query_in, key_in, value_in, conv_weight, level_weight, out_gain, doc_starts):
    row_count, width_all = query_in.shape
    head_count, level_count, _ = level_weight.shape
    head_size = width_all // head_count
    conv_width = conv_weight.shape[0]
    doc_count = doc_starts.shape[0]
    dev_index = lax.axis_index("seq")
    dev_count = lax.axis_size("seq")
    dev_bits = dev_count.bit_length() - 1
    rim_rows = conv_width - 1
    tiles = row_count // LANES
    smem = pl.BlockSpec(memory_space=pltpu.SMEM)
    vmem = pl.BlockSpec(memory_space=pltpu.VMEM)
    anywhere = pl.BlockSpec(memory_space=pl.ANY)

    tails = pl.pallas_call(
        rim_kernel,
        in_specs=[pl.BlockSpec(memory_space=pltpu.HBM)] * 3,
        out_specs=vmem,
        out_shape=pltpu.VMEM((rim_rows, 3 * width_all), query_in.dtype),
        scratch_shapes=[
            pltpu.VMEM((3, 16, width_all), query_in.dtype),
            pltpu.SemaphoreType.DMA((3,)),
        ],
        compiler_params=limited(1),
        name="rim",
    )(*(pltpu.with_memory_space_constraint(x, pltpu.HBM) for x in (query_in, key_in, value_in)))
    tails, docs = lax.optimization_barrier((tails, doc_starts))
    rims = exchange(tails, lambda i: (i + 1) % dev_count)
    heads = 4
    keys, values_t, later_state, inside = pl.pallas_call(
        functools.partial(later_rows_kernel, doc_count=doc_count, heads=2 * heads),
        in_specs=[smem] + [vmem] * 3,
        out_specs=[vmem] * 4,
        out_shape=[
            pltpu.VMEM((head_count, row_count, head_size), jnp.bfloat16),
            pltpu.VMEM((head_count, head_size, row_count), jnp.bfloat16),
            pltpu.VMEM((head_count, head_size, head_size), jnp.float32),
            pltpu.VMEM((tiles, LANES + 8 * (rim_rows - 1), LANES), jnp.float32),
        ],
        scratch_shapes=[pltpu.VMEM((4 * heads, window_rows(row_count), LANES), jnp.float32)],
        compiler_params=limited(14),
        cost_estimate=pl.CostEstimate(
            flops=500_000_000, bytes_accessed=4_000_000, transcendentals=1_500_000
        ),
        name="later_rows",
    )(docs, key_in, value_in, conv_weight)
    rims, keys, values_t, later_state = lax.optimization_barrier(
        (rims, keys, values_t, later_state)
    )
    keys, values_t, state = pl.pallas_call(
        functools.partial(
            first_rows_kernel, doc_count=doc_count, row_count=row_count, heads=2 * heads
        ),
        in_specs=[smem] + [vmem] * 8,
        out_specs=[vmem] * 3,
        out_shape=[
            pltpu.VMEM((head_count, row_count, head_size), jnp.bfloat16),
            pltpu.VMEM((head_count, head_size, row_count), jnp.bfloat16),
            pltpu.VMEM((head_count, head_size, head_size), jnp.bfloat16),
        ],
        scratch_shapes=[pltpu.VMEM((4 * heads, window_rows(LANES), LANES), jnp.float32)],
        input_output_aliases={7: 0, 8: 1},
        compiler_params=limited(6),
        name="first_rows",
    )(docs, key_in, value_in, conv_weight, rims, inside, later_state, keys, values_t)

    def joined(mine, theirs, bit):
        mine = mine.astype(jnp.float32) * factors[2 * bit]
        theirs = theirs.astype(jnp.float32) * factors[2 * bit + 1]
        return (mine + theirs).astype(jnp.bfloat16)

    def near_piece(first_head, piece_heads, buffers, docs):
        heads = piece_heads
        extra = [] if buffers is None else list(buffers)
        return pl.pallas_call(
            functools.partial(
                near_kernel,
                first_head=first_head,
                head_count=piece_heads,
                heads=heads,
                skipped=len(extra),
            ),
            in_specs=[smem] + [vmem] * (8 + len(extra)),
            out_specs=[vmem] * 2,
            out_shape=[
                pltpu.VMEM((head_count, row_count, head_size), jnp.bfloat16),
                pltpu.VMEM((head_count, head_size, row_count), jnp.float32),
            ],
            scratch_shapes=[
                pltpu.VMEM((heads, window_rows(row_count), LANES), jnp.float32),
                pltpu.VMEM((heads, tiles, 24, LANES), jnp.float32),
                pltpu.VMEM((heads, row_count, row_count), jnp.bfloat16),
            ],
            input_output_aliases={9: 0, 10: 1} if extra else {},
            compiler_params=limited(10),
            cost_estimate=pl.CostEstimate(
                flops=5_000_000_000, bytes_accessed=35_000_000, transcendentals=300_000
            ),
            name="near",
        )(docs, query_in, rims, conv_weight, inside, table, starts, keys, values_t, *extra)

    def far_piece(group, lower, last_state, previous=None, before=None, out=None, writes_own=False):
        writes = previous or writes_own
        extra = ([before] if previous else []) + ([] if out is None else [out])
        out_type = jax.ShapeDtypeStruct((row_count, width_all), jnp.bfloat16)
        result_type = pltpu.VMEM((row_count, width_all // 4), jnp.bfloat16)
        return pl.pallas_call(
            functools.partial(
                far_skip if out is not None else far_kernel,
                group=group,
                previous=previous,
                writes_own=writes_own,
                dev_bits=dev_bits,
            ),
            in_specs=[vmem] * (8 if previous else 7) + ([] if out is None else [anywhere]),
            out_specs=([anywhere] if writes else []) + ([] if writes_own else [vmem]),
            out_shape=([out_type] if writes else []) + ([] if writes_own else [result_type]),
            scratch_shapes=([result_type] if writes_own else [])
            + ([pltpu.SemaphoreType.DMA((2,))] if writes else []),
            input_output_aliases={} if out is None else {8: 0},
            compiler_params=limited(4),
            cost_estimate=pl.CostEstimate(
                flops=5_000_000_000, bytes_accessed=35_000_000, transcendentals=0
            ),
            name="far",
        )(queries, near, table, gains, first_state, lower, last_state, *extra)

    quarter = head_count // 4
    state, docs = lax.optimization_barrier((state, docs))
    first_state = swapped(state, 0)
    table, starts, gains, factors = pl.pallas_call(
        functools.partial(tables_kernel, doc_count=doc_count),
        in_specs=[smem, vmem, vmem],
        out_specs=[vmem] * 4,
        out_shape=[
            pltpu.VMEM((level_count, head_count, row_count), jnp.float32),
            pltpu.VMEM((8, row_count), jnp.int32),
            pltpu.VMEM((head_count, head_size, LANES), jnp.float32),
            pltpu.VMEM((2 * (dev_bits - 1), LANES), jnp.float32),
        ],
        compiler_params=limited(2),
        name="tables",
    )(docs, jnp.transpose(level_weight, (1, 0, 2)), out_gain.reshape(head_count, 1, head_size))
    first_state, table, starts, gains, factors = lax.optimization_barrier(
        (first_state, table, starts, gains, factors)
    )
    half = 2 * quarter
    pair_kept = joined(state[:quarter], first_state[half : half + quarter], 0)
    pair_sent = joined(state[quarter:half], first_state[half + quarter :], 0)

    pair_sent, tied = lax.optimization_barrier((pair_sent, docs))
    pair_in = swapped(pair_sent, 1)
    buffers = near_piece(0, quarter, None, tied)
    pair_in, buffers = lax.optimization_barrier((pair_in, buffers))
    carried = joined(pair_kept, pair_in, 1)

    received = []
    for bit in range(2, dev_bits - 1):
        if bit == 2:
            carried, tied = lax.optimization_barrier((carried, docs))
        arrived = swapped(carried, bit)
        if bit == 2:
            buffers = near_piece(quarter, quarter, buffers, tied)
            arrived, buffers = lax.optimization_barrier((arrived, buffers))
        received.append(arrived)
        carried = joined(carried, arrived, bit)

    mine = jnp.stack([pair_kept] + received)
    carried, mine, tied = lax.optimization_barrier((carried, mine, docs))
    last_own = swapped(carried, dev_bits - 1)
    theirs = swapped(mine, 1)
    buffers = near_piece(2 * quarter, 2 * quarter, buffers, tied)
    last_own, theirs, buffers = lax.optimization_barrier((last_own, theirs, buffers))
    queries, near = buffers
    own = jnp.concatenate([jnp.stack([pair_in] + received), theirs], axis=1)
    own, last_own = lax.optimization_barrier((own, last_own))

    last_next = swapped(last_own, 1)
    other = swapped(own, 0)
    last_other = swapped(last_own, 0)
    (done,) = far_piece((0, 0), own, last_own)
    other, last_other, done = lax.optimization_barrier((other, last_other, done))
    (out,) = far_piece((1, 0), other, last_other, (0, 0), done, writes_own=True)
    last_next, out = lax.optimization_barrier((last_next, out))
    last_far = swapped(last_next, 0)
    (done,) = far_piece((0, 1), own, last_next)
    last_far, out, done = lax.optimization_barrier((last_far, out, done))
    (out,) = far_piece((1, 1), other, last_far, (0, 1), done, out, writes_own=True)
    return out


def solution(mesh):
    in_specs = (
        P(("groups", "seq"), None),
        P(("groups", "seq"), None),
        P(("groups", "seq"), None),
        P(),
        P(None, None, ("groups", "seq")),
        P(),
        P("groups"),
    )
    out_specs = P(("groups", "seq"), None)
    return jax.shard_map(local, mesh=mesh, in_specs=in_specs, out_specs=out_specs, check_vma=False)
```
